32 devices in a mesh: row: 16 (over z, y, core), col: 2 (over x).
Axes of the slice: x: 2, y: 2, z: 4, core: 2. Of those that a mesh axis runs over, the one named last changes fastest.
Arguments:
- x_in: bfloat16 [2, 16384, 768], P(None, 'row', 'col'), may hold values from -6 to 6
- span_start: int32 [2, 16, 2], P(None, 'row'), may hold values from 0 to 768, as said below
- span_kind: int32 [2, 16, 2], P(None, 'row'), may hold values from 0 to 1
- ln1_gain: float32 [768], P('col'), may hold values from 0.5 to 1.5
- ln1_bias: float32 [768], P('col'), may hold values from -3 to 3
- w_qkv: bfloat16 [768, 3, 768], P('row', None, 'col'), may hold values from -0.3125 to 0.3125
- b_query: float32 [768], P('col'), may hold values from -3 to 3
- b_value: float32 [768], P('col'), may hold values from -3 to 3
- w_out: bfloat16 [768, 768], P('col', 'row'), may hold values from -0.875 to 0.875
- b_out: float32 [768], P('col'), may hold values from -3 to 3
- ln2_gain: float32 [768], P('col'), may hold values from 0.5 to 1.5
- ln2_bias: float32 [768], P('col'), may hold values from -3 to 3
- w_fc: bfloat16 [768, 3072], P('row', 'col'), may hold values from -0.21875 to 0.21875
- b_fc: float32 [3072], P('col'), may hold values from -3 to 3
- w_proj: bfloat16 [3072, 768], P('col', 'row'), may hold values from -0.15625 to 0.15625
- b_proj: float32 [768], P('col'), may hold values from -3 to 3
- cotangent: bfloat16 [2, 16384, 768], P(None, 'row', 'col'), may hold values from -6 to 6
Outputs:
- layer_out: bfloat16 [2, 16384, 768], P(None, 'row', 'col')
- grad_input: bfloat16 [2, 16384, 768], P(None, 'row', 'col')
- g_ln1_gain: float32 [768], P('col')
- g_ln1_bias: float32 [768], P('col')
- g_w_qkv: float32 [768, 3, 768], P('row', None, 'col')
- g_b_query: float32 [768], P('col')
- g_b_value: float32 [768], P('col')
- g_w_out: float32 [768, 768], P('col', 'row')
- g_b_out: float32 [768], P('col')
- g_ln2_gain: float32 [768], P('col')
- g_ln2_bias: float32 [768], P('col')
- g_w_fc: float32 [768, 3072], P('row', 'col')
- g_b_fc: float32 [3072], P('col')
- g_w_proj: float32 [3072, 768], P('col', 'row')
- g_b_proj: float32 [768], P('col')
The draws below stay inside these ranges and needn't reach their ends.
Inputs may be any that keep to these rules, and one draw needn't show every extreme that they name: `span_start`: span j of a sequence starts within the j-th of 2 equal parts of the sequence and ends within it, so spans never intersect.
All inputs are finite; a program needn't handle non-finite values.
Results may differ from the reference program's by a relative error of at most 0.017.
Values may be sent and summed in bfloat16 or wider, within the bound.
A program may use at most 192 MiB of HBM per device.

```python
from functools import partial
import jax
import jax.numpy as jnp
from jax import lax

D = 768
HEADS = 12
HEAD = 64
FF = 3072
SEQ_LEN = 1024
IMG = 256
SPANS = 2
MICRO = 2
SEQS = 16
TOKENS_MB = 16384


def draw_span_start(key, part):
    half_len = SEQ_LEN // SPANS
    offsets = jax.random.randint(key, (MICRO, SEQS, SPANS), 0, half_len - IMG + 1)
    return (offsets + jnp.arange(SPANS, dtype=jnp.int32) * half_len).astype(jnp.int32)


def set_ends(values, key, least, top_value):
    index_at = [jax.random.randint(jax.random.fold_in(key, axis), (), 0, length) for axis, length in enumerate(values.shape)]
    widest = values.shape.index(max(values.shape))
    neighbour = index_at[:widest] + [(index_at[widest] + 1) % values.shape[widest]] + index_at[widest + 1:]
    return values.at[tuple(index_at)].set(least).at[tuple(neighbour)].set(top_value)


def spiked(array, rng, source, target, blocks, factor):
    owner, partner = [(jnp.arange(array.shape[dim]) // (array.shape[dim] // blocks)).reshape([-1 if axis == dim else 1 for axis in range(array.ndim)]) for dim in (source, target)]
    chosen = jax.random.permutation(rng, blocks)[partner]
    strong = (owner == chosen) | (owner == (partner + blocks // 2) % blocks)
    return jnp.where(strong, factor * array, array)


def block_scale(own_key, dims, shards, smallest, high):
    def one(axis_at, shards_of):
        draws = jax.random.uniform(jax.random.fold_in(jax.random.fold_in(own_key, 6), axis_at), (shards_of,), jnp.float32, smallest / len(shards), high / len(shards))
        return jnp.repeat(jnp.exp(draws), dims[axis_at] // shards_of).reshape((-1,) + (1,) * (len(dims) - axis_at - 1))

    level = one(*shards[0])
    for cut in shards[1:]:
        level = level * one(*cut)
    return level


def scatter_about(own_key, extent, width, bound, pieces=(), kind=jnp.bfloat16):
    factor_of = block_scale(own_key, extent, pieces, -0.22, 0.18) if pieces else 1.0
    entries = jax.random.normal(own_key, extent, jnp.float32) * width * factor_of
    return jnp.minimum(jnp.maximum(entries, -bound), bound).astype(kind)


def bell_draw_with(key, dims, width, reach, split, heavy, kind=jnp.bfloat16):
    values = width * jax.random.normal(key, dims, jnp.float32)
    if split:
        values = values * block_scale(key, dims, split, -0.22, 0.18)
    return jnp.clip(spiked(values, jax.random.fold_in(key, 3), *heavy), -reach, reach).astype(kind)


def setup_inputs(seed: int = 0) -> dict:
    key_of = jax.random.split(jax.random.key(seed), 18)
    x_in = scatter_about(key_of[0], (MICRO, TOKENS_MB, D), 1.0, 6.0, ((1, 16), (2, 2)))
    span_start = draw_span_start(jax.random.fold_in(key_of[17], 71), 0)
    span_kind = set_ends(jax.random.randint(key_of[2], (MICRO, SEQS, SPANS), 0, 2), jax.random.fold_in(key_of[2], 1), 0, 1).astype(jnp.int32)
    ln1_gain = jnp.clip(0.5 + 1.0 * jax.random.uniform(key_of[3], (D,), jnp.float32) ** block_scale(key_of[3], (D,), ((0, 2),), -0.2, 0.2), 0.5, 1.5)
    ln1_bias = scatter_about(key_of[4], (D,), 0.5, 3.0, ((0, 2),), jnp.float32)
    w_qkv = scatter_about(key_of[5], (D, 3, D), (D // 2) ** -0.5, 0.3125, ((0, 16), (2, 2)))
    b_query = scatter_about(key_of[6], (D,), 0.5, 3.0, ((0, 2),), jnp.float32)
    b_value = scatter_about(key_of[7], (D,), 0.5, 3.0, ((0, 2),), jnp.float32)
    w_out = scatter_about(key_of[8], (D, D), (D // 16) ** -0.5, 0.875, ((0, 2), (1, 16)))
    b_out = scatter_about(key_of[9], (D,), 0.5, 3.0, ((0, 2),), jnp.float32)
    ln2_gain = jnp.clip(0.5 + 1.0 * jax.random.uniform(key_of[10], (D,), jnp.float32) ** block_scale(key_of[10], (D,), ((0, 2),), -0.2, 0.2), 0.5, 1.5)
    ln2_bias = scatter_about(key_of[11], (D,), 0.5, 3.0, ((0, 2),), jnp.float32)
    w_fc = scatter_about(key_of[12], (D, FF), D ** -0.5, 0.21875, ((0, 16), (1, 2)))
    b_fc = scatter_about(key_of[13], (FF,), 0.5, 3.0, ((0, 2),), jnp.float32)
    w_proj = scatter_about(key_of[14], (FF, D), (FF // 2) ** -0.5, 0.15625, ((0, 2), (1, 16)))
    b_proj = scatter_about(key_of[15], (D,), 0.5, 3.0, ((0, 2),), jnp.float32)
    cotangent = bell_draw_with(key_of[16], (MICRO, TOKENS_MB, D), 1.0, 6.0, ((1, 16), (2, 2)), (1, 2, 16, 2.0))
    return dict(x_in=x_in, span_start=span_start, span_kind=span_kind, ln1_gain=ln1_gain, ln1_bias=ln1_bias, w_qkv=w_qkv, b_query=b_query, b_value=b_value, w_out=w_out, b_out=b_out, ln2_gain=ln2_gain, ln2_bias=ln2_bias, w_fc=w_fc, b_fc=b_fc, w_proj=w_proj, b_proj=b_proj, cotangent=cotangent)


precise = lax.Precision.HIGHEST
epsilon = 1e-05

@jax.custom_vjp
def low(v):
    return lax.optimization_barrier(v.astype(jnp.bfloat16)).astype(jnp.float32)

@jax.custom_vjp
def low_back(v):
    return v

def low_keep(v):
    return (low(v), None)

def low_pass(kept, grad):
    return (grad,)

def back_keep(v):
    return (v, None)

def back_low(kept, grad):
    return (low(grad),)
low.defvjp(low_keep, low_pass)
low_back.defvjp(back_keep, back_low)

def span_allowed(starts, span_types, length):
    position = jnp.arange(length, dtype=jnp.int32)
    causal = position[None, :] <= position[:, None]
    inside = (position[:, None] >= starts[None, :]) & (position[:, None] < starts[None, :] + IMG)
    joined = inside[:, None, :] & inside[None, :, :] & (span_types[None, None, :] == 1)
    return causal | jnp.any(joined, axis=-1)

def attend(packed, starts, span_types):
    query = packed[:, 0]
    key_rows = packed[:, 1]
    values = packed[:, 2]
    scores = low_back(jnp.einsum('qhd,khd->hqk', query, key_rows, precision=precise)) * 0.125
    allowed = span_allowed(starts, span_types, query.shape[0])
    scores = jnp.where(allowed[None], scores, -1e+30)
    largest = lax.optimization_barrier(jnp.max(scores, axis=-1, keepdims=True))
    weights = jnp.exp(scores - largest)
    chance = weights / lax.optimization_barrier(jnp.sum(weights, axis=-1, keepdims=True))
    return jnp.einsum('hqk,khd->qhd', low(chance), values, precision=precise)

def attend_item(seq_item):
    return attend(seq_item[0], seq_item[1], seq_item[2])

def layer_norm(residual, gain, bias):
    average = lax.optimization_barrier(jnp.mean(residual, axis=-1, keepdims=True))
    variance = lax.optimization_barrier(jnp.mean(residual * residual, axis=-1, keepdims=True)) - average * average
    return (residual - average) * lax.rsqrt(variance + epsilon) * gain + bias

def forward(parameters, residual, starts, span_types):
    ln1_gain, ln1_bias, w_qkv, b_query, b_value, w_out, b_out, ln2_gain, ln2_bias, w_fc, b_fc, w_proj, b_proj = parameters
    row_count = residual.shape[0]
    normed = low(layer_norm(residual, ln1_gain, ln1_bias))
    packed = jnp.dot(normed, w_qkv.reshape(D, 3 * D), precision=precise).reshape(row_count, 3, D)
    bias_rows = jnp.stack([b_query, jnp.zeros_like(b_query), b_value])
    packed = low(low_back(packed + bias_rows[None]))
    packed = packed.reshape(row_count // SEQ_LEN, SEQ_LEN, 3, HEADS, HEAD)
    attended = lax.map(jax.checkpoint(attend_item), (packed, starts, span_types))
    attended = low(low_back(attended.reshape(row_count, D)))
    middle = residual + low_back(jnp.dot(attended, w_out, precision=precise)) + b_out
    normed_second = low(layer_norm(middle, ln2_gain, ln2_bias))
    hidden = low_back(jnp.dot(normed_second, w_fc, precision=precise) + b_fc)
    active = low(jax.nn.gelu(hidden, approximate=True))
    return middle + jnp.dot(active, w_proj, precision=precise) + b_proj

def reference(x_in, span_start, span_kind, ln1_gain, ln1_bias, w_qkv, b_query, b_value, w_out, b_out, ln2_gain, ln2_bias, w_fc, b_fc, w_proj, b_proj, cotangent):
    parameters = tuple((weight.astype(jnp.float32) for weight in (ln1_gain, ln1_bias, w_qkv, b_query, b_value, w_out, b_out, ln2_gain, ln2_bias, w_fc, b_fc, w_proj, b_proj)))
    totals = tuple((jnp.zeros_like(weight) for weight in parameters))
    outputs = []
    grads_in = []
    for micro_step in range(MICRO):
        residual = x_in[micro_step].astype(jnp.float32)
        runner = partial(forward, starts=span_start[micro_step], span_types=span_kind[micro_step])
        result, pullback = jax.vjp(runner, parameters, residual)
        grad_params, grad_residual = pullback(cotangent[micro_step].astype(jnp.float32))
        totals = tuple((earlier + added for earlier, added in zip(totals, grad_params)))
        outputs.append(result.astype(jnp.bfloat16))
        grads_in.append(grad_residual.astype(jnp.bfloat16))
    return (jnp.stack(outputs), jnp.stack(grads_in), totals[0], totals[1], totals[2], totals[3], totals[4], totals[5], totals[6], totals[7], totals[8], totals[9], totals[10], totals[11], totals[12])
```

```python
import jax
import jax.numpy as jnp
from jax import lax
from jax.experimental import pallas as pl
from jax.experimental.pallas import tpu as pltpu
from jax.sharding import PartitionSpec as P

HEAD = 64
IMG = 256
epsilon = 1e-05
bf16 = jnp.bfloat16
f32 = jnp.float32
GELU_A = 0.7978845608028654
GELU_B = 0.044715
PAIR = 2 * HEAD


def nn(a, b):
    return lax.dot_general(a, b, (((1,), (0,)), ((), ())), preferred_element_type=f32)


def nt(a, b):
    return lax.dot_general(a, b, (((1,), (1,)), ((), ())), preferred_element_type=f32)


def tn(a, b):
    return lax.dot_general(a, b, (((0,), (0,)), ((), ())), preferred_element_type=f32)


def half_bias(span_ref, part, half):
    start = span_ref[0, part]
    kind = span_ref[1, part]
    base = part * half
    rows = lax.broadcasted_iota(jnp.int32, (half, half), 0) + base
    cols = lax.broadcasted_iota(jnp.int32, (half, half), 1) + base
    first = jnp.where(kind == 1, start, 4 * half)
    joined = (rows >= first) & (rows < first + IMG) & (cols >= first) & (cols < first + IMG)
    return jnp.where((cols <= rows) | joined, 0.0, -1e30).astype(f32)


def lane_masks(rows):
    lane = lax.broadcasted_iota(jnp.int32, (rows, PAIR), 1)
    return lane < HEAD


def attend_forward_kernel(span_ref, q_ref, k_ref, v_ref, o_ref, p_ref, inv_ref, bias_ref):
    half = q_ref.shape[0] // 2

    @pl.when(pl.program_id(0) == 0)
    def _():
        for part in range(2):
            bias_ref[part] = half_bias(span_ref, part, half)

    low = lane_masks(half)
    for part in range(2):
        q = q_ref[part * half : (part + 1) * half, :] * jnp.asarray(0.125, bf16)
        zero = jnp.zeros_like(q)
        outs = []
        invs = []
        for head in range(2):
            mine = low if head == 0 else jnp.logical_not(low)
            qh = jnp.where(mine, q, zero)
            own = nt(qh, k_ref[part * half : (part + 1) * half, :]) + bias_ref[part]
            largest = jnp.max(own, axis=1, keepdims=True)
            if part == 1:
                before = nt(qh, k_ref[:half, :])
                largest = jnp.maximum(largest, jnp.max(before, axis=1, keepdims=True))
            own = jnp.exp(own - largest)
            total = jnp.sum(own, axis=1, keepdims=True)
            own = own.astype(bf16)
            p_ref[0, head, 2 * part] = own
            out = nn(own, v_ref[part * half : (part + 1) * half, :])
            if part == 1:
                before = jnp.exp(before - largest)
                total = total + jnp.sum(before, axis=1, keepdims=True)
                before = before.astype(bf16)
                p_ref[0, head, 1] = before
                out = out + nn(before, v_ref[:half, :])
            inv = 1.0 / total
            outs.append(out * inv)
            invs.append(inv)
        o_ref[part * half : (part + 1) * half, :] = jnp.where(low, outs[0], outs[1]).astype(bf16)
        inv_ref[part * half : (part + 1) * half, :] = jnp.where(low, invs[0], invs[1])


def qkv_specs(length, half_blocks):
    def spec(which):
        return pl.BlockSpec(
            (length, PAIR),
            lambda j: (0, (j // half_blocks) * 3 * half_blocks + which * half_blocks + j % half_blocks),
        )

    return [spec(0), spec(1), spec(2)]


def attend_forward(packed, spans):
    length = packed.shape[0]
    width = packed.shape[1] // 3
    pairs = width // PAIR
    half = length // 2
    return pl.pallas_call(
        attend_forward_kernel,
        grid=(pairs,),
        in_specs=[pl.BlockSpec(memory_space=pltpu.SMEM)] + qkv_specs(length, pairs // 2),
        out_specs=[
            pl.BlockSpec((length, PAIR), lambda j: (0, j)),
            pl.BlockSpec((1, 2, 3, half, half), lambda j: (j, 0, 0, 0, 0)),
            pl.BlockSpec((length, PAIR), lambda j: (0, j)),
        ],
        out_shape=[
            jax.ShapeDtypeStruct((length, width), bf16),
            jax.ShapeDtypeStruct((pairs, 2, 3, half, half), bf16),
            jax.ShapeDtypeStruct((length, width), f32),
        ],
        scratch_shapes=[pltpu.VMEM((2, half, half), f32)],
        compiler_params=pltpu.CompilerParams(vmem_limit_bytes=60 << 20),
        cost_estimate=pl.CostEstimate(
            flops=4 * 3 * half * half * width * 4, bytes_accessed=24 << 20, transcendentals=3 * half * half * 12
        ),
        name="attend_forward",
    )(spans, packed, packed, packed)


def attend_backward_kernel(q_ref, k_ref, v_ref, o_ref, p_ref, inv_ref, g_ref, dq_ref, dk_ref, dv_ref):
    half = q_ref.shape[0] // 2
    low = lane_masks(half)
    dks = [None, None]
    dvs = [None, None]

    def add(total, part, value):
        total[part] = value if total[part] is None else total[part] + value

    for part in range(2):
        rows = slice(part * half, (part + 1) * half)
        inv = inv_ref[rows, :]
        g = g_ref[rows, :].astype(f32) * inv
        scaled = g * o_ref[rows, :].astype(f32)
        q = q_ref[rows, :]
        gb = g.astype(bf16)
        zero = jnp.zeros_like(gb)
        dq = None
        for head in range(2):
            mine = low if head == 0 else jnp.logical_not(low)
            gh = jnp.where(mine, gb, zero)
            qh = jnp.where(mine, q, zero)
            rowdot = jnp.sum(jnp.where(mine, scaled, 0.0), axis=1, keepdims=True)
            for kpart in range(part + 1):
                krows = slice(kpart * half, (kpart + 1) * half)
                p = p_ref[0, head, part + kpart]
                kh = jnp.where(mine, k_ref[krows, :], zero)
                dp = nt(gh, v_ref[krows, :])
                ds = (p.astype(f32) * (dp - rowdot)).astype(bf16)
                term = nn(ds, kh)
                dq = term if dq is None else dq + term
                add(dks, kpart, tn(ds, qh))
                add(dvs, kpart, tn(p, gh))
        dq_ref[rows, :] = (dq * 0.125).astype(bf16)
    for part in range(2):
        rows = slice(part * half, (part + 1) * half)
        dk_ref[rows, :] = (dks[part] * 0.125).astype(bf16)
        dv_ref[rows, :] = dvs[part].astype(bf16)


def attend_backward(packed, attended, p, inv, grad_attended):
    length = packed.shape[0]
    width = packed.shape[1] // 3
    pairs = width // PAIR
    half = length // 2
    one = pl.BlockSpec((length, PAIR), lambda j: (0, j))
    return pl.pallas_call(
        attend_backward_kernel,
        grid=(pairs,),
        in_specs=qkv_specs(length, pairs // 2)
        + [one, pl.BlockSpec((1, 2, 3, half, half), lambda j: (j, 0, 0, 0, 0)), one, one],
        out_specs=[one, one, one],
        out_shape=[jax.ShapeDtypeStruct((length, width), bf16)] * 3,
        compiler_params=pltpu.CompilerParams(vmem_limit_bytes=60 << 20),
        cost_estimate=pl.CostEstimate(
            flops=8 * 3 * half * half * width * 4, bytes_accessed=32 << 20, transcendentals=0
        ),
        name="attend_backward",
    )(packed, packed, packed, attended, p, inv, grad_attended)


SWAP = [(0, 1), (1, 0)]


def swap(value):
    return lax.ppermute(value, "col", SWAP)


def ordered(mine, other, axis):
    first = lax.axis_index("col") == 0
    low = jnp.where(first, mine, other)
    high = jnp.where(first, other, mine)
    return jnp.concatenate([low, high], axis=axis)


def own_micro(halves):
    col = lax.axis_index("col")
    mine = lax.dynamic_index_in_dim(halves, col, 0, keepdims=False)
    other = swap(lax.dynamic_index_in_dim(halves, 1 - col, 0, keepdims=False))
    return ordered(mine, other, 1)


def back_micro(full):
    col = lax.axis_index("col")
    half = full.shape[1] // 2
    mine = lax.dynamic_slice_in_dim(full, col * half, half, 1)
    other = swap(lax.dynamic_slice_in_dim(full, (1 - col) * half, half, 1))
    first = col == 0
    return jnp.stack([jnp.where(first, mine, other), jnp.where(first, other, mine)])


def gather_weights(block):
    return lax.all_gather(block, ("col", "row"), axis=0, tiled=True)


def scatter_grad(total):
    return lax.psum_scatter(total, ("col", "row"), scatter_dimension=0, tiled=True)


def layer_norm(value):
    width = value.shape[-1]
    average = jnp.sum(value, axis=-1, keepdims=True) / width
    square = jnp.sum(value * value, axis=-1, keepdims=True) / width
    inverse = lax.rsqrt(square - average * average + epsilon)
    return (value - average) * inverse, inverse


def norm_backward(grad, centred, inverse, gain):
    scaled = grad * gain
    first = jnp.mean(scaled, axis=-1, keepdims=True)
    second = jnp.mean(scaled * centred, axis=-1, keepdims=True)
    back = inverse * (scaled - first - centred * second)
    return back, jnp.sum(grad * centred, axis=0), jnp.sum(grad, axis=0)


def body(
    x_in, span_start, span_kind, ln1_gain, ln1_bias, w_qkv, b_query, b_value, w_out, b_out,
    ln2_gain, ln2_bias, w_fc, b_fc, w_proj, b_proj, cotangent,
):
    half_width = x_in.shape[2]
    width = 2 * half_width
    ff_half = w_fc.shape[1]
    shard = w_qkv.shape[0]
    col = lax.axis_index("col")

    qkv_all = gather_weights(w_qkv.reshape(shard, 3 * half_width)).reshape(2, width, 3 * half_width)
    residual = own_micro(x_in).astype(f32)
    out_all = gather_weights(w_out.T).reshape(2, width, half_width)
    fc_all = gather_weights(w_fc).reshape(2, width, ff_half)
    proj_all = gather_weights(w_proj.T).reshape(2, width, ff_half)
    grad_out = own_micro(cotangent)

    vectors = [ln1_gain, ln1_bias, b_query, b_value, b_out, ln2_gain, ln2_bias, b_fc, b_proj]
    flat = jnp.concatenate(vectors)
    flat_other = swap(flat)
    full = []
    at = 0
    for vector in vectors:
        full.append(ordered(vector, flat_other[at : at + vector.shape[0]], 0))
        at += vector.shape[0]
    ln1_gain, ln1_bias, b_query, b_value, b_out, ln2_gain, ln2_bias, b_fc, b_proj = full

    starts = lax.dynamic_index_in_dim(span_start, col, 0, keepdims=False)[0]
    kinds = lax.dynamic_index_in_dim(span_kind, col, 0, keepdims=False)[0]
    spans = jnp.stack([starts, kinds])

    centred_first, inverse_first = layer_norm(residual)
    normed_first = (centred_first * ln1_gain + ln1_bias).astype(bf16)
    zero = jnp.zeros((half_width,), f32)
    pieces = []
    for h in range(2):
        part = slice(h * half_width, (h + 1) * half_width)
        bias = jnp.concatenate([b_query[part], zero, b_value[part]])
        pieces.append((nn(normed_first, qkv_all[h]) + bias).astype(bf16))
    packed = jnp.concatenate(pieces, axis=1)
    attended, p, inv = attend_forward(packed, spans)
    branch = nt(attended[:, :half_width], out_all[0]) + nt(attended[:, half_width:], out_all[1])
    middle = residual + branch + b_out
    centred_second, inverse_second = layer_norm(middle)
    normed_second = (centred_second * ln2_gain + ln2_bias).astype(bf16)
    branch = None
    slopes = []
    actives = []
    for h in range(2):
        hidden = nn(normed_second, fc_all[h]) + b_fc[h * ff_half : (h + 1) * ff_half]
        squared = hidden * hidden
        tanh = jnp.tanh(GELU_A * hidden * (1.0 + GELU_B * squared))
        active = (0.5 * hidden * (1.0 + tanh)).astype(bf16)
        slope = 0.5 * (1.0 + tanh) + 0.5 * hidden * (1.0 - tanh * tanh) * GELU_A * (
            1.0 + 3.0 * GELU_B * squared
        )
        slopes.append(slope.astype(bf16))
        actives.append(active)
        term = nt(active, proj_all[h])
        branch = term if branch is None else branch + term
    layer_out = back_micro((middle + branch + b_proj).astype(bf16))

    grad_out_wide = grad_out.astype(f32)
    g_proj = [tn(grad_out, active).astype(bf16) for active in actives]
    grad_hidden = [(nn(grad_out, proj_all[h]) * slopes[h].astype(f32)).astype(bf16) for h in range(2)]
    g_fc = [tn(normed_second, grad) for grad in grad_hidden]
    g_bfc = jnp.concatenate([jnp.sum(grad.astype(f32), axis=0) for grad in grad_hidden])
    out_proj = scatter_grad(jnp.concatenate([g.astype(bf16) for g in g_proj], axis=0))
    out_fc = scatter_grad(jnp.concatenate([g.astype(bf16) for g in g_fc], axis=0))
    grad_normed = nt(grad_hidden[0], fc_all[0]) + nt(grad_hidden[1], fc_all[1])
    back, g_ln2_gain, g_ln2_bias = norm_backward(grad_normed, centred_second, inverse_second, ln2_gain)
    grad_middle = grad_out_wide + back
    g_bproj = jnp.sum(grad_out_wide, axis=0)
    g_bout = jnp.sum(grad_middle, axis=0)
    grad_low = grad_middle.astype(bf16)
    g_out = [tn(grad_low, attended[:, h * half_width : (h + 1) * half_width]) for h in range(2)]
    out_out = scatter_grad(jnp.concatenate([g.astype(bf16) for g in g_out], axis=0))
    grad_attended = jnp.concatenate([nn(grad_low, out_all[h]).astype(bf16) for h in range(2)], axis=1)
    dq, dk, dv = attend_backward(packed, attended, p, inv, grad_attended)
    g_bquery = jnp.sum(dq.astype(f32), axis=0)
    g_bvalue = jnp.sum(dv.astype(f32), axis=0)
    grad_packed = []
    for h in range(2):
        part = slice(h * half_width, (h + 1) * half_width)
        grad_packed.append(jnp.concatenate([dq[:, part], dk[:, part], dv[:, part]], axis=1))
    g_qkv = [tn(normed_first, grad) for grad in grad_packed]
    out_qkv = scatter_grad(jnp.concatenate([g.astype(bf16) for g in g_qkv], axis=0))
    grad_normed = nt(grad_packed[0], qkv_all[0]) + nt(grad_packed[1], qkv_all[1])
    back, g_ln1_gain, g_ln1_bias = norm_backward(grad_normed, centred_first, inverse_first, ln1_gain)
    grad_input = back_micro((grad_middle + back).astype(bf16))

    small = [g_ln1_gain, g_ln1_bias, g_bquery, g_bvalue, g_bout, g_ln2_gain, g_ln2_bias, g_bfc, g_bproj]
    summed = lax.psum(jnp.concatenate(small), ("row", "col"))
    kept = []
    at = 0
    for vector in small:
        size = vector.shape[0] // 2
        kept.append(lax.dynamic_slice_in_dim(summed, at + col * size, size, 0))
        at += vector.shape[0]
    return (
        layer_out,
        grad_input,
        kept[0],
        kept[1],
        out_qkv.astype(f32).reshape(shard, 3, half_width),
        kept[2],
        kept[3],
        out_out.astype(f32).T,
        kept[4],
        kept[5],
        kept[6],
        out_fc.astype(f32),
        kept[7],
        out_proj.astype(f32).T,
        kept[8],
    )


def solution(mesh):
    placed = (
        P(None, "row", "col"), P(None, "row", None), P(None, "row", None), P("col"), P("col"),
        P("row", None, "col"), P("col"), P("col"), P("col", "row"), P("col"), P("col"), P("col"),
        P("row", "col"), P("col"), P("col", "row"), P("col"), P(None, "row", "col"),
    )
    return jax.shard_map(
        body,
        mesh=mesh,
        in_specs=placed,
        out_specs=(
            P(None, "row", "col"), P(None, "row", "col"), P("col"), P("col"), P("row", None, "col"),
            P("col"), P("col"), P("col", "row"), P("col"), P("col"), P("col"), P("row", "col"),
            P("col"), P("col", "row"), P("col"),
        ),
        check_vma=False,
    )
```

```python
from functools import partial

import jax
import jax.numpy as jnp
from jax import lax
from jax.experimental import pallas as pl
from jax.experimental.pallas import tpu as pltpu
from jax.sharding import PartitionSpec as P

HEAD = 64
IMG = 256
epsilon = 1e-05
bf16 = jnp.bfloat16
f32 = jnp.float32
GELU_A = 0.7978845608028654
GELU_B = 0.044715
PAIR = 2 * HEAD


def nn(a, b):
    return lax.dot_general(a, b, (((1,), (0,)), ((), ())), preferred_element_type=f32)


def nt(a, b):
    return lax.dot_general(a, b, (((1,), (1,)), ((), ())), preferred_element_type=f32)


def tn(a, b):
    return lax.dot_general(a, b, (((0,), (0,)), ((), ())), preferred_element_type=f32)


def half_bias(span_ref, part, half):
    start = span_ref[0, part]
    kind = span_ref[1, part]
    base = part * half
    rows = lax.broadcasted_iota(jnp.int32, (half, half), 0) + base
    cols = lax.broadcasted_iota(jnp.int32, (half, half), 1) + base
    first = jnp.where(kind == 1, start, 4 * half)
    joined = (rows >= first) & (rows < first + IMG) & (cols >= first) & (cols < first + IMG)
    return jnp.where((cols <= rows) | joined, 0.0, -1e30).astype(f32)


def lane_masks(rows):
    lane = lax.broadcasted_iota(jnp.int32, (rows, PAIR), 1)
    return lane < HEAD


def attend_forward_kernel(span_ref, qkv_ref, o_ref, p_ref, inv_ref, bias_ref):
    half = qkv_ref.shape[0] // 2
    q_ref, k_ref, v_ref = (qkv_ref.at[:, i * PAIR : (i + 1) * PAIR] for i in range(3))

    @pl.when(pl.program_id(0) == 0)
    def _():
        for part in range(2):
            bias_ref[part] = half_bias(span_ref, part, half)

    low = lane_masks(half)
    for part in range(2):
        q = q_ref[part * half : (part + 1) * half, :] * jnp.asarray(0.125, bf16)
        zero = jnp.zeros_like(q)
        outs = []
        invs = []
        for head in range(2):
            mine = low if head == 0 else jnp.logical_not(low)
            qh = jnp.where(mine, q, zero)
            own = nt(qh, k_ref[part * half : (part + 1) * half, :]) + bias_ref[part]
            largest = jnp.max(own, axis=1, keepdims=True)
            if part == 1:
                before = nt(qh, k_ref[:half, :])
                largest = jnp.maximum(largest, jnp.max(before, axis=1, keepdims=True))
            own = jnp.exp(own - largest)
            total = jnp.sum(own, axis=1, keepdims=True)
            own = own.astype(bf16)
            p_ref[0, head, 2 * part] = own
            out = nn(own, v_ref[part * half : (part + 1) * half, :])
            if part == 1:
                before = jnp.exp(before - largest)
                total = total + jnp.sum(before, axis=1, keepdims=True)
                before = before.astype(bf16)
                p_ref[0, head, 1] = before
                out = out + nn(before, v_ref[:half, :])
            inv = 1.0 / total
            outs.append(out * inv)
            invs.append(inv)
        o_ref[part * half : (part + 1) * half, :] = jnp.where(low, outs[0], outs[1]).astype(bf16)
        inv_ref[part * half : (part + 1) * half, :] = jnp.where(low, invs[0], invs[1])


def attend_forward(packed, spans):
    length = packed.shape[0]
    width = packed.shape[1] // 3
    pairs = width // PAIR
    half = length // 2
    return pl.pallas_call(
        attend_forward_kernel,
        grid=(pairs,),
        in_specs=[
            pl.BlockSpec(memory_space=pltpu.SMEM),
            pl.BlockSpec((length, 3 * PAIR), lambda j: (0, j)),
        ],
        out_specs=[
            pl.BlockSpec((length, PAIR), lambda j: (0, j)),
            pl.BlockSpec((1, 2, 3, half, half), lambda j: (j, 0, 0, 0, 0)),
            pl.BlockSpec((length, PAIR), lambda j: (0, j)),
        ],
        out_shape=[
            jax.ShapeDtypeStruct((length, width), bf16),
            jax.ShapeDtypeStruct((pairs, 2, 3, half, half), bf16),
            jax.ShapeDtypeStruct((length, width), f32),
        ],
        scratch_shapes=[pltpu.VMEM((2, half, half), f32)],
        compiler_params=pltpu.CompilerParams(vmem_limit_bytes=60 << 20),
        cost_estimate=pl.CostEstimate(
            flops=4 * 3 * half * half * width * 4, bytes_accessed=24 << 20, transcendentals=3 * half * half * 12
        ),
        name="attend_forward",
    )(spans, packed)


def attend_backward_kernel(qkv_ref, o_ref, p_ref, inv_ref, g_ref, d_ref, sum_ref):
    half = qkv_ref.shape[0] // 2
    low = lane_masks(half)
    q_ref, k_ref, v_ref = (qkv_ref.at[:, i * PAIR : (i + 1) * PAIR] for i in range(3))
    dks = [None, None]
    dvs = [None, None]
    sums = [None, None, None]

    def add(total, part, value):
        total[part] = value if total[part] is None else total[part] + value

    def put(which, rows, value):
        value = value.astype(bf16)
        d_ref[rows, which * PAIR : (which + 1) * PAIR] = value
        add(sums, which, jnp.sum(value.astype(f32), axis=0, keepdims=True))

    for part in range(2):
        rows = slice(part * half, (part + 1) * half)
        inv = inv_ref[rows, :]
        g = g_ref[rows, :].astype(f32) * inv
        scaled = g * o_ref[rows, :].astype(f32)
        q = q_ref[rows, :]
        gb = g.astype(bf16)
        zero = jnp.zeros_like(gb)
        dq = None
        for head in range(2):
            mine = low if head == 0 else jnp.logical_not(low)
            gh = jnp.where(mine, gb, zero)
            qh = jnp.where(mine, q, zero)
            rowdot = jnp.sum(jnp.where(mine, scaled, 0.0), axis=1, keepdims=True)
            for kpart in range(part + 1):
                krows = slice(kpart * half, (kpart + 1) * half)
                p = p_ref[0, head, part + kpart]
                kh = jnp.where(mine, k_ref[krows, :], zero)
                dp = nt(gh, v_ref[krows, :])
                ds = (p.astype(f32) * (dp - rowdot)).astype(bf16)
                term = nn(ds, kh)
                dq = term if dq is None else dq + term
                add(dks, kpart, tn(ds, qh))
                add(dvs, kpart, tn(p, gh))
        put(0, rows, dq * 0.125)
    for part in range(2):
        rows = slice(part * half, (part + 1) * half)
        put(1, rows, dks[part] * 0.125)
        put(2, rows, dvs[part])
    for which in range(3):
        sum_ref[0, :, which * PAIR : (which + 1) * PAIR] = sums[which]


def attend_backward(packed, attended, p, inv, grad_attended):
    length = packed.shape[0]
    width = packed.shape[1] // 3
    pairs = width // PAIR
    half = length // 2
    one = pl.BlockSpec((length, PAIR), lambda j: (0, j))
    three = pl.BlockSpec((length, 3 * PAIR), lambda j: (0, j))
    return pl.pallas_call(
        attend_backward_kernel,
        grid=(pairs,),
        in_specs=[three, one, pl.BlockSpec((1, 2, 3, half, half), lambda j: (j, 0, 0, 0, 0)), one, one],
        out_specs=[three, pl.BlockSpec((1, 1, 3 * PAIR), lambda j: (j, 0, 0))],
        out_shape=[
            jax.ShapeDtypeStruct(packed.shape, bf16),
            jax.ShapeDtypeStruct((pairs, 1, 3 * PAIR), f32),
        ],
        compiler_params=pltpu.CompilerParams(vmem_limit_bytes=56 << 20),
        cost_estimate=pl.CostEstimate(
            flops=8 * 3 * half * half * width * 4, bytes_accessed=32 << 20, transcendentals=0
        ),
        name="attend_backward",
    )(packed, attended, p, inv, grad_attended)


SWAP = [(0, 1), (1, 0)]


def swap(value):
    return lax.ppermute(value, "col", SWAP)


def ordered(mine, other, axis):
    first = lax.axis_index("col") == 0
    low = jnp.where(first, mine, other)
    high = jnp.where(first, other, mine)
    return jnp.concatenate([low, high], axis=axis)


def own_micro(halves):
    col = lax.axis_index("col")
    mine = lax.dynamic_index_in_dim(halves, col, 0, keepdims=False)
    other = swap(lax.dynamic_index_in_dim(halves, 1 - col, 0, keepdims=False))
    return ordered(mine, other, 1)


def back_micro(full):
    col = lax.axis_index("col")
    half = full.shape[1] // 2
    mine = lax.dynamic_slice_in_dim(full, col * half, half, 1)
    other = swap(lax.dynamic_slice_in_dim(full, (1 - col) * half, half, 1))
    first = col == 0
    return jnp.stack([jnp.where(first, mine, other), jnp.where(first, other, mine)])


GATHER_CUT = (0.3, 0.5)
REDUCE_CUT = (0.34, 0.33)


MESH = pl.DeviceIdType.MESH
DEPTH = 4
WAYS = ("up", "down", "y", "x", "core")
ORDERS = ("zyx", "zxy", "xyz")


def row_of(z, y, core):
    return z * 4 + y * 2 + core


def my_place():
    row = lax.axis_index("row")
    return row // 4, (row // 2) % 2, row % 2, lax.axis_index("col")


def maybe(cond, act):
    if cond is None:
        act()
    else:
        pl.when(cond)(act)


def remote(src, dst, send, recv, device):
    return pltpu.make_async_remote_copy(
        src_ref=src, dst_ref=dst, send_sem=send, recv_sem=recv, device_id=device, device_id_type=MESH
    )


def greet(always, z, up, down):
    barrier = pltpu.get_barrier_semaphore()

    def hello(device):
        pl.semaphore_signal(barrier, inc=1, device_id=device, device_id_type=MESH)

    for device in always:
        hello(device)
    pl.when(z < DEPTH - 1)(lambda: hello(up))
    pl.when(z > 0)(lambda: hello(down))
    pl.semaphore_wait(
        barrier, len(always) + (z < DEPTH - 1).astype(jnp.int32) + (z > 0).astype(jnp.int32)
    )


def tree_rounds(order):
    rounds = {}
    for dz in (0, -1, 1, -2, 2, -3, 3):
        for dy in (0, 1):
            for dx in (0, 1):
                step = {"z": dz, "y": dy, "x": dx}
                via = None
                for axis in order:
                    if step[axis]:
                        via = axis
                onward = []
                open_now = via is None
                for axis in order:
                    if axis == via:
                        open_now = True
                    if not open_now:
                        continue
                    if axis == "z":
                        onward += ["up"] if dz <= 0 else []
                        onward += ["down"] if dz >= 0 else []
                    elif axis != via:
                        onward.append(axis)
                onward.append("core")
                rounds.setdefault(abs(dz) + dy + dx, []).append((dz, dy, dx, onward))
    return rounds


def pieces_of(widths, cuts):
    found = []
    for part in range(3):
        base = 0
        for weight, width in enumerate(widths):
            lo = max(base, cuts[part])
            hi = min(base + width, cuts[part + 1])
            if hi > lo:
                found.append((part, weight, lo - cuts[part], lo - base, hi - lo))
            base += width
    return found


def gather_kernel(widths, cuts, *refs):
    count = len(widths)
    shards = refs[:count]
    outs = refs[count : 2 * count]
    bufs = refs[2 * count : 2 * count + 3]
    send, recv, local = refs[2 * count + 3 :]
    z, y, core, x = my_place()
    near = {
        "up": (row_of(z + 1, y, core), x),
        "down": (row_of(z - 1, y, core), x),
        "y": (row_of(z, 1 - y, core), x),
        "x": (row_of(z, y, core), 1 - x),
        "core": (row_of(z, y, 1 - core), x),
    }
    has = {"up": z < DEPTH - 1, "down": z > 0}
    pieces = pieces_of(widths, cuts)
    row = row_of(z, y, core)
    loads = []
    for i, (part, weight, at, src, width) in enumerate(pieces):
        loads.append(
            pltpu.make_async_copy(
                shards[weight].at[:, pl.ds(src, width)],
                bufs[part].at[x, row, :, pl.ds(at, width)],
                local.at[0, i],
            )
        )
    for load in loads:
        load.start()
    greet([near["y"], near["x"], near["core"]], z, near["up"], near["down"])
    for load in loads:
        load.wait()

    def copy(part, bz, by, bc, bx, way):
        block = bufs[part].at[bx, row_of(bz, by, bc)]
        slot = bx * 8 + bz * 2 + by
        return remote(
            block,
            block,
            send.at[part, slot, WAYS.index(way)],
            recv.at[part, bx * 16 + row_of(bz, by, bc)],
            near[way],
        )

    trees = [tree_rounds(order) for order in ORDERS]

    def each(step, act):
        for part in range(3):
            for dz, dy, dx, onward in trees[part].get(step, []):
                bz, by, bx = z + dz, (y + dy) % 2, (x + dx) % 2
                cond = None if dz == 0 else ((bz >= 0) & (bz <= DEPTH - 1))
                maybe(cond, lambda: act(part, bz, by, bx, onward))

    def forward(part, bz, by, bx, onward, step):
        if step:
            copy(part, bz, by, core, bx, "core").wait_recv()
        for way in onward:
            maybe(has.get(way), lambda way=way: copy(part, bz, by, core, bx, way).start())

    def finish(part, bz, by, bx, onward):
        copy(part, bz, by, 1 - core, bx, "core").wait_recv()
        for way in onward:
            maybe(has.get(way), lambda way=way: copy(part, bz, by, core, bx, way).wait_send())

    for step in range(6):
        each(step, lambda *a, step=step: forward(*a, step))
    for step in range(6):
        each(step, finish)
    stores = []
    for i, (part, weight, at, src, width) in enumerate(pieces):
        for side in range(2):
            stores.append(
                pltpu.make_async_copy(
                    bufs[part].at[side, :, :, pl.ds(at, width)],
                    outs[weight].at[:, :, pl.ds(side * widths[weight] + src, width)],
                    local.at[1 + side, i],
                )
            )
    for store in stores:
        store.start()
    for store in stores:
        store.wait()


def gather_near(shards, cuts):
    rows = shards[0].shape[0]
    widths = [shard.shape[1] for shard in shards]
    outs = pl.pallas_call(
        lambda *refs: gather_kernel(widths, cuts, *refs),
        in_specs=[pl.BlockSpec(memory_space=pl.ANY)] * len(shards),
        out_specs=[pl.BlockSpec(memory_space=pl.ANY)] * len(shards),
        out_shape=[jax.ShapeDtypeStruct((16, rows, 2 * width), bf16) for width in widths],
        scratch_shapes=[pltpu.VMEM((2, 16, rows, cuts[i + 1] - cuts[i]), bf16) for i in range(3)]
        + [
            pltpu.SemaphoreType.DMA((3, 16, 5)),
            pltpu.SemaphoreType.DMA((3, 32)),
            pltpu.SemaphoreType.DMA((3, 8)),
        ],
        compiler_params=pltpu.CompilerParams(
            collective_id=0, has_side_effects=True, vmem_limit_bytes=56 << 20
        ),
        cost_estimate=pl.CostEstimate(flops=0, bytes_accessed=200 << 20, transcendentals=0),
        name="gather_weights",
    )(*shards)
    return [out.reshape(16 * rows, 2 * width) for out, width in zip(outs, widths)]


def reduce_kernel(widths, cuts, *refs):
    count = len(widths)
    grads = refs[:count]
    small_ref = refs[count]
    outs = refs[count + 1 : 2 * count + 1]
    sum_ref = refs[2 * count + 1]
    scr = refs[2 * count + 2 :]
    acc, rcore = scr[0:3], scr[3:6]
    rx, ry, rz, cy, cx = scr[6:8], scr[8:10], scr[10:13], scr[13], scr[14]
    srecv, sacc, final = scr[15], scr[16], scr[17:20]
    s_core, r_core, s_x, r_x, s_y, r_y, s_z, r_z, s_c, r_c, s_s, r_s, s_load, s_out = scr[20:]
    z, y, core, x = my_place()
    up, down = (row_of(z + 1, y, core), x), (row_of(z - 1, y, core), x)
    to_y, to_x = (row_of(z, 1 - y, core), x), (row_of(z, y, core), 1 - x)
    to_core = (row_of(z, y, 1 - core), x)
    to_z1 = (row_of(z + 1 - 2 * (z % 2), y, core), x)
    to_z2 = (row_of((z + 2) % 4, y, core), x)
    pieces = pieces_of(widths, cuts)
    by_part = [[p for p in pieces if p[0] == part] for part in range(3)]

    def gcols(weight, side, src, width):
        return pl.ds(pl.multiple_of(side * widths[weight] + src, 128), width)

    loads = []
    for i, (part, weight, at, src, width) in enumerate(pieces):
        for side in range(2):
            loads.append(
                pltpu.make_async_copy(
                    grads[weight].at[:, :, core, :, gcols(weight, side, src, width)],
                    acc[part].at[side, :, :, :, pl.ds(at, width)],
                    s_load.at[side, i],
                )
            )
    for load in loads:
        load.start()
    greet([to_core, to_x, to_y, to_z2], z, up, down)

    def view(part, ref, far, zi):
        if part == 0:
            return ref.at[(1 - x) if far else x, zi]
        return ref.at[:, zi, (1 - y) if far else y]

    def core_copies(part, far, zi):
        copies = []
        for i, (_, weight, at, src, width) in enumerate(by_part[part]):
            cols = pl.ds(at, width)
            if part == 0:
                side = (1 - x) if far else x
                copies.append(
                    remote(
                        grads[weight].at[zi, :, 1 - core, :, gcols(weight, side, src, width)],
                        rcore[0].at[side, zi, :, :, cols],
                        s_core.at[0, int(far), zi, i, 0],
                        r_core.at[0, int(far), zi, i, 0],
                        to_core,
                    )
                )
            elif part == 1:
                by = (1 - y) if far else y
                for side in range(2):
                    copies.append(
                        remote(
                            grads[weight].at[zi, by, 1 - core, :, gcols(weight, side, src, width)],
                            rcore[1].at[side, zi, by, :, cols],
                            s_core.at[1, int(far), zi, i, side],
                            r_core.at[1, int(far), zi, i, side],
                            to_core,
                        )
                    )
            else:
                for side in range(2):
                    copies.append(
                        remote(
                            grads[weight].at[zi, :, 1 - core, :, gcols(weight, side, src, width)],
                            rcore[2].at[side, zi, :, :, cols],
                            s_core.at[2, 0, zi, i, side],
                            r_core.at[2, 0, zi, i, side],
                            to_core,
                        )
                    )
        return copies

    def loop(act):
        def step(zi, carry):
            act(zi)
            return carry

        lax.fori_loop(0, DEPTH, step, 0)

    def start_far(zi):
        for part in range(3):
            for copy in core_copies(part, True, zi):
                copy.start()

    def start_near(zi):
        for part in range(2):
            for copy in core_copies(part, False, zi):
                copy.start()

    loop(start_far)
    loop(start_near)
    partners = [to_core, to_x, to_y, to_z1, to_z2]
    sacc[0] = small_ref[...]

    def small_copy(step):
        return remote(sacc.at[step], srecv.at[step], s_s.at[step], r_s.at[step], partners[step])

    def small_next(step):
        small_copy(step).wait()
        sacc[step + 1] = sacc[step] + srecv[step]
        if step < 4:
            small_copy(step + 1).start()

    small_copy(0).start()
    for load in loads:
        load.wait()

    def add(total, term):
        total[...] = total[...] + term[...]

    first = [(rx[0], s_x, r_x, to_x), (ry[0], s_y, r_y, to_y)]
    second = [(ry[1], s_y, r_y, to_y), (rx[1], s_x, r_x, to_x)]

    def first_copy(part, zi):
        buf, send, recv, device = first[part]
        return remote(
            view(part, acc[part], True, zi), buf.at[zi], send.at[0, zi], recv.at[0, zi], device
        )

    def half_of(part, zi, far):
        if part == 0:
            return acc[0].at[x, zi, (1 - y) if far else y]
        return acc[1].at[(1 - x) if far else x, zi, y]

    def second_copy(part, zi):
        buf, send, recv, device = second[part]
        return remote(
            half_of(part, zi, True), buf.at[zi], send.at[1, zi], recv.at[1, zi], device
        )

    def far_step(zi):
        for part in range(2):
            for copy in core_copies(part, True, zi):
                copy.wait_recv()
            add(view(part, acc[part], True, zi), view(part, rcore[part], True, zi))
            first_copy(part, zi).start()
        for copy in core_copies(2, True, zi):
            copy.wait_recv()
        add(acc[2].at[:, zi], rcore[2].at[:, zi])

    def near_step(zi):
        for part in range(2):
            for copy in core_copies(part, False, zi):
                copy.wait_recv()
            add(view(part, acc[part], False, zi), view(part, rcore[part], False, zi))
            first_copy(part, zi).wait_recv()
            add(view(part, acc[part], False, zi), first[part][0].at[zi])
            second_copy(part, zi).start()

    def last_step(zi):
        for part in range(2):
            second_copy(part, zi).wait_recv()
            add(half_of(part, zi, False), second[part][0].at[zi])

    def block(part, zi):
        if part == 2:
            return acc[2].at[:, zi]
        return acc[part].at[x, zi, y]

    def line_copy(part, direction, zd):
        return remote(
            block(part, zd),
            rz[part].at[direction, zd],
            s_z.at[part, direction, zd],
            r_z.at[part, direction, zd],
            down if direction else up,
        )

    def line_sends(parts, step):
        for direction in range(2):
            at = DEPTH - 1 - step if direction else step
            for zd in (0, 1, 2) if direction else (3, 2, 1):
                if not ((at > zd) if direction else (at < zd)):
                    continue
                for part in parts:

                    def act(part=part, direction=direction, zd=zd):
                        if step > 0:
                            line_copy(part, direction, zd).wait_recv()
                            add(block(part, zd), rz[part].at[direction, zd])
                        line_copy(part, direction, zd).start()

                    pl.when(z == at)(act)

    def line_end(parts):
        for part in parts:
            for direction in range(2):

                def act(part=part, direction=direction):
                    line_copy(part, direction, z).wait_recv()
                    add(block(part, z), rz[part].at[direction, z])

                pl.when((z < DEPTH - 1) if direction else (z > 0))(act)

    loop(far_step)
    small_next(0)
    line_sends([2], 0)
    loop(near_step)
    small_next(1)
    line_sends([2], 1)
    loop(last_step)
    small_next(2)
    line_sends([0, 1], 0)
    line_sends([2], 2)
    line_end([2])
    y_copy = remote(acc[2].at[:, z, 1 - y], cy, s_c.at[0], r_c.at[0], to_y)
    y_copy.start()
    line_sends([0, 1], 1)
    small_next(3)
    y_copy.wait_recv()
    add(acc[2].at[:, z, y], cy)
    x_copy = remote(acc[2].at[1 - x, z, y], cx, s_c.at[1], r_c.at[1], to_x)
    x_copy.start()
    line_sends([0, 1], 2)
    x_copy.wait_recv()
    add(acc[2].at[x, z, y], cx)
    line_end([0, 1])
    small_next(4)
    sum_ref[...] = sacc[5]
    for part in range(3):
        final[part][...] = acc[part][x, z, y].astype(f32)
    stores = []
    for i, (part, weight, at, src, width) in enumerate(pieces):
        stores.append(
            pltpu.make_async_copy(
                final[part].at[:, pl.ds(at, width)], outs[weight].at[:, pl.ds(src, width)], s_out.at[i]
            )
        )
    for store in stores:
        store.start()

    def drain(zi):
        for part in range(3):
            for copy in core_copies(part, True, zi):
                copy.wait_send()
            if part < 2:
                for copy in core_copies(part, False, zi):
                    copy.wait_send()
                first_copy(part, zi).wait_send()
                second_copy(part, zi).wait_send()

    loop(drain)
    for part in range(3):
        for direction in range(2):
            for zd in range(DEPTH):
                pl.when((z > zd) if direction else (z < zd))(
                    lambda part=part, direction=direction, zd=zd: line_copy(part, direction, zd).wait_send()
                )
    y_copy.wait_send()
    x_copy.wait_send()
    for store in stores:
        store.wait()


def reduce_near(grads, small, cuts, rows):
    widths = [grad.shape[1] // 2 for grad in grads]
    w = [cuts[i + 1] - cuts[i] for i in range(3)]
    dma = pltpu.SemaphoreType.DMA

    def low(*shape):
        return pltpu.VMEM(shape, bf16)

    scratch = [low(2, 4, 2, rows, k) for k in w] * 2
    scratch += [low(4, 2, rows, w[0]), low(4, rows, w[1])]
    scratch += [low(4, 2, rows, w[1]), low(4, rows, w[0])]
    scratch += [low(2, 4, rows, w[0]), low(2, 4, rows, w[1]), low(2, 4, 2, 2, rows, w[2])]
    scratch += [low(2, rows, w[2]), low(rows, w[2])]
    scratch += [pltpu.VMEM((5,) + small.shape, f32), pltpu.VMEM((6,) + small.shape, f32)]
    scratch += [pltpu.VMEM((rows, k), f32) for k in w]
    scratch += [dma((3, 2, 4, 4, 2)), dma((3, 2, 4, 4, 2)), dma((2, 4)), dma((2, 4)), dma((2, 4)), dma((2, 4))]
    scratch += [dma((3, 2, 4)), dma((3, 2, 4)), dma((2,)), dma((2,)), dma((5,)), dma((5,)), dma((2, 8)), dma((8,))]
    shaped = [grad.reshape(4, 2, 2, rows, grad.shape[1]) for grad in grads]
    any_space = pl.BlockSpec(memory_space=pl.ANY)
    vmem = pl.BlockSpec(memory_space=pltpu.VMEM)
    outs = pl.pallas_call(
        lambda *refs: reduce_kernel(widths, cuts, *refs),
        in_specs=[any_space] * len(grads) + [vmem],
        out_specs=[any_space] * len(grads) + [vmem],
        out_shape=[jax.ShapeDtypeStruct((rows, width), f32) for width in widths]
        + [jax.ShapeDtypeStruct(small.shape, f32)],
        scratch_shapes=scratch,
        compiler_params=pltpu.CompilerParams(
            collective_id=1, has_side_effects=True, vmem_limit_bytes=56 << 20
        ),
        cost_estimate=pl.CostEstimate(flops=0, bytes_accessed=200 << 20, transcendentals=0),
        name="reduce_grads",
    )(*shaped, small)
    return outs[:-1], outs[-1]


def gather_far(shards):
    fulls = []
    for shard in shards:
        rows = lax.all_gather(shard, ("col", "row"), axis=0, tiled=True)
        fulls.append(jnp.concatenate(jnp.split(rows, 2, axis=0), axis=1))
    return fulls


def reduce_far(grads, small):
    outs = []
    for grad in grads:
        halves = jnp.concatenate(jnp.split(grad, 2, axis=1), axis=0)
        outs.append(lax.psum_scatter(halves, ("col", "row"), scatter_dimension=0, tiled=True).astype(f32))
    return outs, lax.psum(small, ("row", "col"))


def part_cuts(widths, first, second):
    total = sum(widths) // 128
    one = round(total * first)
    two = round(total * (first + second))
    return [0, one * 128, two * 128, total * 128]


def layer_norm(value):
    width = value.shape[-1]
    average = jnp.sum(value, axis=-1, keepdims=True) / width
    square = jnp.sum(value * value, axis=-1, keepdims=True) / width
    inverse = lax.rsqrt(square - average * average + epsilon)
    return (value - average) * inverse, inverse


def norm_backward(grad, centred, inverse, gain):
    scaled = grad * gain
    first = jnp.mean(scaled, axis=-1, keepdims=True)
    second = jnp.mean(scaled * centred, axis=-1, keepdims=True)
    back = inverse * (scaled - first - centred * second)
    return back, jnp.sum(grad * centred, axis=0), jnp.sum(grad, axis=0)


def by_pairs(block):
    rows, three, half = block.shape
    return block.reshape(rows, three, half // PAIR, PAIR).transpose(0, 2, 1, 3).reshape(rows, three * half)


def body(
    near, x_in, span_start, span_kind, ln1_gain, ln1_bias, w_qkv, b_query, b_value, w_out, b_out,
    ln2_gain, ln2_bias, w_fc, b_fc, w_proj, b_proj, cotangent,
):
    half_width = x_in.shape[2]
    shard = w_qkv.shape[0]
    col = lax.axis_index("col")

    residual = own_micro(x_in).astype(f32)
    grad_out = own_micro(cotangent)
    shards = [by_pairs(w_qkv), w_out.T, w_fc, w_proj.T]
    if near:
        qkv_all, out_all, fc_all, proj_all = gather_near(shards, part_cuts([s.shape[1] for s in shards], *GATHER_CUT))
    else:
        qkv_all, out_all, fc_all, proj_all = gather_far(shards)

    vectors = [ln1_gain, ln1_bias, b_query, b_value, b_out, ln2_gain, ln2_bias, b_fc, b_proj]
    flat = jnp.concatenate(vectors)
    flat_other = swap(flat)
    full = []
    at = 0
    for vector in vectors:
        full.append(ordered(vector, flat_other[at : at + vector.shape[0]], 0))
        at += vector.shape[0]
    ln1_gain, ln1_bias, b_query, b_value, b_out, ln2_gain, ln2_bias, b_fc, b_proj = full

    starts = lax.dynamic_index_in_dim(span_start, col, 0, keepdims=False)[0]
    kinds = lax.dynamic_index_in_dim(span_kind, col, 0, keepdims=False)[0]
    spans = jnp.stack([starts, kinds])

    centred_first, inverse_first = layer_norm(residual)
    normed_first = (centred_first * ln1_gain + ln1_bias).astype(bf16)
    bias = jnp.stack([b_query, jnp.zeros_like(b_query), b_value]).reshape(3, -1, PAIR)
    packed = (nn(normed_first, qkv_all) + bias.transpose(1, 0, 2).reshape(-1)).astype(bf16)
    attended, p, inv = attend_forward(packed, spans)
    middle = residual + nt(attended, out_all) + b_out
    centred_second, inverse_second = layer_norm(middle)
    normed_second = (centred_second * ln2_gain + ln2_bias).astype(bf16)
    hidden = nn(normed_second, fc_all) + b_fc
    squared = hidden * hidden
    tanh = jnp.tanh(GELU_A * hidden * (1.0 + GELU_B * squared))
    active = (0.5 * hidden * (1.0 + tanh)).astype(bf16)
    slope = (
        0.5 * (1.0 + tanh)
        + 0.5 * hidden * (1.0 - tanh * tanh) * GELU_A * (1.0 + 3.0 * GELU_B * squared)
    ).astype(bf16)
    layer_out = back_micro((middle + nt(active, proj_all) + b_proj).astype(bf16))

    grad_out_wide = grad_out.astype(f32)
    g_proj = tn(grad_out, active).astype(bf16)
    grad_hidden = (nn(grad_out, proj_all) * slope.astype(f32)).astype(bf16)
    g_fc = tn(normed_second, grad_hidden).astype(bf16)
    g_bfc = jnp.sum(grad_hidden.astype(f32), axis=0)
    grad_normed = nt(grad_hidden, fc_all)
    back, g_ln2_gain, g_ln2_bias = norm_backward(grad_normed, centred_second, inverse_second, ln2_gain)
    grad_middle = grad_out_wide + back
    g_bproj = jnp.sum(grad_out_wide, axis=0)
    g_bout = jnp.sum(grad_middle, axis=0)
    grad_low = grad_middle.astype(bf16)
    g_out = tn(grad_low, attended).astype(bf16)
    grad_attended = nn(grad_low, out_all).astype(bf16)
    grad_packed, g_bpacked = attend_backward(packed, attended, p, inv, grad_attended)
    g_bquery = g_bpacked[:, 0, :PAIR].reshape(-1)
    g_bvalue = g_bpacked[:, 0, 2 * PAIR :].reshape(-1)
    g_qkv = tn(normed_first, grad_packed).astype(bf16)
    grad_normed = nt(grad_packed, qkv_all)
    back, g_ln1_gain, g_ln1_bias = norm_backward(grad_normed, centred_first, inverse_first, ln1_gain)
    grad_input = back_micro((grad_middle + back).astype(bf16))

    small = [g_ln1_gain, g_ln1_bias, g_bquery, g_bvalue, g_bout, g_ln2_gain, g_ln2_bias, g_bfc, g_bproj]
    flat = jnp.concatenate(small).reshape(-1, 128)
    grads = [g_qkv, g_out, g_fc, g_proj]
    if near:
        outs, summed = reduce_near(grads, flat, part_cuts([g.shape[1] // 2 for g in grads], *REDUCE_CUT), shard)
    else:
        outs, summed = reduce_far(grads, flat)
    out_qkv, out_out, out_fc, out_proj = outs
    summed = summed.reshape(-1)
    kept = []
    at = 0
    for vector in small:
        size = vector.shape[0] // 2
        kept.append(lax.dynamic_slice_in_dim(summed, at + col * size, size, 0))
        at += vector.shape[0]
    return (
        layer_out,
        grad_input,
        kept[0],
        kept[1],
        out_qkv.reshape(shard, -1, 3, PAIR).transpose(0, 2, 1, 3).reshape(shard, 3, half_width),
        kept[2],
        kept[3],
        out_out.T,
        kept[4],
        kept[5],
        kept[6],
        out_fc,
        kept[7],
        out_proj.T,
        kept[8],
    )


def solution(mesh):
    placed = (
        P(None, "row", "col"), P(None, "row", None), P(None, "row", None), P("col"), P("col"),
        P("row", None, "col"), P("col"), P("col"), P("col", "row"), P("col"), P("col"), P("col"),
        P("row", "col"), P("col"), P("col", "row"), P("col"), P(None, "row", "col"),
    )
    near = mesh.shape["row"] == 16
    return jax.shard_map(
        partial(body, near),
        mesh=mesh,
        in_specs=placed,
        out_specs=(
            P(None, "row", "col"), P(None, "row", "col"), P("col"), P("col"), P("row", None, "col"),
            P("col"), P("col"), P("col", "row"), P("col"), P("col"), P("col"), P("row", "col"),
            P("col"), P("col", "row"), P("col"),
        ),
        check_vma=False,
    )
```

```python
from functools import partial

import jax
import jax.numpy as jnp
from jax import lax
from jax.experimental import pallas as pl
from jax.experimental.pallas import tpu as pltpu
from jax.sharding import PartitionSpec as P

HEAD = 64
IMG = 256
epsilon = 1e-05
bf16 = jnp.bfloat16
f32 = jnp.float32
GELU_A = 0.7978845608028654
GELU_B = 0.044715
PAIR = 2 * HEAD


def nn(a, b):
    return lax.dot_general(a, b, (((1,), (0,)), ((), ())), preferred_element_type=f32)


def nt(a, b):
    return lax.dot_general(a, b, (((1,), (1,)), ((), ())), preferred_element_type=f32)


def tn(a, b):
    return lax.dot_general(a, b, (((0,), (0,)), ((), ())), preferred_element_type=f32)


def half_bias(span_ref, part, half):
    start = span_ref[0, part]
    kind = span_ref[1, part]
    base = part * half
    rows = lax.broadcasted_iota(jnp.int32, (half, half), 0) + base
    cols = lax.broadcasted_iota(jnp.int32, (half, half), 1) + base
    first = jnp.where(kind == 1, start, 4 * half)
    joined = (rows >= first) & (rows < first + IMG) & (cols >= first) & (cols < first + IMG)
    return jnp.where((cols <= rows) | joined, 0.0, -1e30).astype(f32)


def lane_masks(rows):
    lane = lax.broadcasted_iota(jnp.int32, (rows, PAIR), 1)
    return lane < HEAD


def attend_forward_kernel(span_ref, qkv_ref, o_ref, p_ref, inv_ref, bias_ref):
    half = qkv_ref.shape[0] // 2
    q_ref, k_ref, v_ref = (qkv_ref.at[:, i * PAIR : (i + 1) * PAIR] for i in range(3))

    @pl.when(pl.program_id(0) == 0)
    def _():
        for part in range(2):
            bias_ref[part] = half_bias(span_ref, part, half)

    low = lane_masks(half)
    for part in range(2):
        q = q_ref[part * half : (part + 1) * half, :] * jnp.asarray(0.125, bf16)
        zero = jnp.zeros_like(q)
        outs = []
        invs = []
        for head in range(2):
            mine = low if head == 0 else jnp.logical_not(low)
            qh = jnp.where(mine, q, zero)
            own = nt(qh, k_ref[part * half : (part + 1) * half, :]) + bias_ref[part]
            largest = jnp.max(own, axis=1, keepdims=True)
            if part == 1:
                before = nt(qh, k_ref[:half, :])
                largest = jnp.maximum(largest, jnp.max(before, axis=1, keepdims=True))
            own = jnp.exp(own - largest)
            total = jnp.sum(own, axis=1, keepdims=True)
            own = own.astype(bf16)
            p_ref[0, head, 2 * part] = own
            out = nn(own, v_ref[part * half : (part + 1) * half, :])
            if part == 1:
                before = jnp.exp(before - largest)
                total = total + jnp.sum(before, axis=1, keepdims=True)
                before = before.astype(bf16)
                p_ref[0, head, 1] = before
                out = out + nn(before, v_ref[:half, :])
            inv = 1.0 / total
            outs.append(out * inv)
            invs.append(inv)
        o_ref[part * half : (part + 1) * half, :] = jnp.where(low, outs[0], outs[1]).astype(bf16)
        inv_ref[part * half : (part + 1) * half, :] = jnp.where(low, invs[0], invs[1])


def attend_forward(packed, spans):
    length = packed.shape[0]
    width = packed.shape[1] // 3
    pairs = width // PAIR
    half = length // 2
    return pl.pallas_call(
        attend_forward_kernel,
        grid=(pairs,),
        in_specs=[
            pl.BlockSpec(memory_space=pltpu.SMEM),
            pl.BlockSpec((length, 3 * PAIR), lambda j: (0, j)),
        ],
        out_specs=[
            pl.BlockSpec((length, PAIR), lambda j: (0, j)),
            pl.BlockSpec((1, 2, 3, half, half), lambda j: (j, 0, 0, 0, 0)),
            pl.BlockSpec((length, PAIR), lambda j: (0, j)),
        ],
        out_shape=[
            jax.ShapeDtypeStruct((length, width), bf16),
            jax.ShapeDtypeStruct((pairs, 2, 3, half, half), bf16),
            jax.ShapeDtypeStruct((length, width), f32),
        ],
        scratch_shapes=[pltpu.VMEM((2, half, half), f32)],
        compiler_params=pltpu.CompilerParams(vmem_limit_bytes=60 << 20),
        cost_estimate=pl.CostEstimate(
            flops=4 * 3 * half * half * width * 4, bytes_accessed=24 << 20, transcendentals=3 * half * half * 12
        ),
        name="attend_forward",
    )(spans, packed)


def attend_back_pair(qkv_ref, o_ref, p_ref, inv_ref, g_ref, sum_ref, at):
    length = qkv_ref.shape[0]
    half = length // 2
    low = lane_masks(half)
    q_ref, k_ref, v_ref = (qkv_ref.at[:, at + i * PAIR : at + (i + 1) * PAIR] for i in range(3))
    dks = [None, None]
    dvs = [None, None]
    dqs = []

    def add(total, part, value):
        total[part] = value if total[part] is None else total[part] + value

    for part in range(2):
        rows = slice(part * half, (part + 1) * half)
        inv = inv_ref[rows, :]
        g = g_ref[rows, :].astype(f32) * inv
        scaled = g * o_ref[rows, :].astype(f32)
        q = q_ref[rows, :]
        gb = g.astype(bf16)
        zero = jnp.zeros_like(gb)
        dq = None
        for head in range(2):
            mine = low if head == 0 else jnp.logical_not(low)
            gh = jnp.where(mine, gb, zero)
            qh = jnp.where(mine, q, zero)
            rowdot = jnp.sum(jnp.where(mine, scaled, 0.0), axis=1, keepdims=True)
            for kpart in range(part + 1):
                krows = slice(kpart * half, (kpart + 1) * half)
                p = p_ref[head, part + kpart]
                kh = jnp.where(mine, k_ref[krows, :], zero)
                dp = nt(gh, v_ref[krows, :])
                ds = (p.astype(f32) * (dp - rowdot)).astype(bf16)
                term = nn(ds, kh)
                dq = term if dq is None else dq + term
                add(dks, kpart, tn(ds, qh))
                add(dvs, kpart, tn(p, gh))
        dqs.append(dq)
    for which, (ref, values, scale) in enumerate(((q_ref, dqs, 0.125), (k_ref, dks, 0.125), (v_ref, dvs, 1.0))):
        total = None
        for part in range(2):
            value = (values[part] * scale).astype(bf16)
            ref[part * half : (part + 1) * half, :] = value
            term = jnp.sum(value.astype(f32), axis=0, keepdims=True)
            total = term if total is None else total + term
        if which != 1:
            sum_ref[which // 2] = total


def attend_backward_kernel(qkv_ref, o_ref, p_ref, inv_ref, g_ref, d_ref, sum_ref):
    d_ref[...] = qkv_ref[...]
    attend_back_pair(d_ref, o_ref, p_ref.at[0], inv_ref, g_ref, sum_ref.at[0], 0)


def attend_backward(packed, attended, p, inv, grad_attended):
    length = packed.shape[0]
    width = packed.shape[1] // 3
    pairs = width // PAIR
    half = length // 2
    one = pl.BlockSpec((length, PAIR), lambda j: (0, j))
    three = pl.BlockSpec((length, 3 * PAIR), lambda j: (0, j))
    return pl.pallas_call(
        attend_backward_kernel,
        grid=(pairs,),
        in_specs=[three, one, pl.BlockSpec((1, 2, 3, half, half), lambda j: (j, 0, 0, 0, 0)), one, one],
        out_specs=[three, pl.BlockSpec((1, 2, 1, PAIR), lambda j: (j, 0, 0, 0))],
        out_shape=[
            jax.ShapeDtypeStruct(packed.shape, bf16),
            jax.ShapeDtypeStruct((pairs, 2, 1, PAIR), f32),
        ],
        compiler_params=pltpu.CompilerParams(vmem_limit_bytes=56 << 20),
        name="attend_backward",
    )(packed, attended, p, inv, grad_attended)


SWAP = [(0, 1), (1, 0)]


def swap(value):
    return lax.ppermute(value, "col", SWAP)


def ordered(mine, other, axis):
    first = lax.axis_index("col") == 0
    low = jnp.where(first, mine, other)
    high = jnp.where(first, other, mine)
    return jnp.concatenate([low, high], axis=axis)


def own_micro(halves):
    col = lax.axis_index("col")
    mine = lax.dynamic_index_in_dim(halves, col, 0, keepdims=False)
    other = swap(lax.dynamic_index_in_dim(halves, 1 - col, 0, keepdims=False))
    return ordered(mine, other, 1)


def back_micro(full):
    col = lax.axis_index("col")
    half = full.shape[1] // 2
    mine = lax.dynamic_slice_in_dim(full, col * half, half, 1)
    other = swap(lax.dynamic_slice_in_dim(full, (1 - col) * half, half, 1))
    first = col == 0
    return jnp.stack([jnp.where(first, mine, other), jnp.where(first, other, mine)])


GATHER_CUT = (0.3, 0.5)
REDUCE_CUT = (0.34, 0.33)


MESH = pl.DeviceIdType.MESH
DEPTH = 4
WAYS = ("up", "down", "y", "x", "core")
ORDERS = ("zyx", "zxy", "xyz")


def row_of(z, y, core):
    return z * 4 + y * 2 + core


def my_place():
    row = lax.axis_index("row")
    return row // 4, (row // 2) % 2, row % 2, lax.axis_index("col")


def maybe(cond, act):
    if cond is None:
        act()
    else:
        pl.when(cond)(act)


def remote(src, dst, send, recv, device):
    return pltpu.make_async_remote_copy(
        src_ref=src, dst_ref=dst, send_sem=send, recv_sem=recv, device_id=device, device_id_type=MESH
    )


def greet(always, z, up, down):
    barrier = pltpu.get_barrier_semaphore()

    def hello(device):
        pl.semaphore_signal(barrier, inc=1, device_id=device, device_id_type=MESH)

    for device in always:
        hello(device)
    pl.when(z < DEPTH - 1)(lambda: hello(up))
    pl.when(z > 0)(lambda: hello(down))
    pl.semaphore_wait(
        barrier, len(always) + (z < DEPTH - 1).astype(jnp.int32) + (z > 0).astype(jnp.int32)
    )


def tree_rounds(order):
    rounds = {}
    for dz in (0, -1, 1, -2, 2, -3, 3):
        for dy in (0, 1):
            for dx in (0, 1):
                step = {"z": dz, "y": dy, "x": dx}
                via = None
                for axis in order:
                    if step[axis]:
                        via = axis
                onward = []
                open_now = via is None
                for axis in order:
                    if axis == via:
                        open_now = True
                    if not open_now:
                        continue
                    if axis == "z":
                        onward += ["up"] if dz <= 0 else []
                        onward += ["down"] if dz >= 0 else []
                    elif axis != via:
                        onward.append(axis)
                onward.append("core")
                rounds.setdefault(abs(dz) + dy + dx, []).append((dz, dy, dx, onward))
    return rounds


def pieces_of(widths, cuts):
    found = []
    for part in range(3):
        base = 0
        for weight, width in enumerate(widths):
            lo = max(base, cuts[part])
            hi = min(base + width, cuts[part + 1])
            if hi > lo:
                found.append((part, weight, lo - cuts[part], lo - base, hi - lo))
            base += width
    return found


def gather_kernel(widths, cuts, *refs):
    count = len(widths)
    shards = refs[:count]
    outs = refs[count : 2 * count]
    bufs = refs[2 * count : 2 * count + 3]
    send, recv, local = refs[2 * count + 3 :]
    z, y, core, x = my_place()
    near = {
        "up": (row_of(z + 1, y, core), x),
        "down": (row_of(z - 1, y, core), x),
        "y": (row_of(z, 1 - y, core), x),
        "x": (row_of(z, y, core), 1 - x),
        "core": (row_of(z, y, 1 - core), x),
    }
    has = {"up": z < DEPTH - 1, "down": z > 0}
    pieces = pieces_of(widths, cuts)
    row = row_of(z, y, core)
    loads = []
    for i, (part, weight, at, src, width) in enumerate(pieces):
        loads.append(
            pltpu.make_async_copy(
                shards[weight].at[:, pl.ds(src, width)],
                bufs[part].at[x, row, :, pl.ds(at, width)],
                local.at[0, i],
            )
        )
    for load in loads:
        load.start()
    greet([near["y"], near["x"], near["core"]], z, near["up"], near["down"])
    for load in loads:
        load.wait()

    def copy(part, bz, by, bc, bx, way):
        block = bufs[part].at[bx, row_of(bz, by, bc)]
        slot = bx * 8 + bz * 2 + by
        return remote(
            block,
            block,
            send.at[part, slot, WAYS.index(way)],
            recv.at[part, bx * 16 + row_of(bz, by, bc)],
            near[way],
        )

    trees = [tree_rounds(order) for order in ORDERS]

    def each(step, act):
        for part in range(3):
            for dz, dy, dx, onward in trees[part].get(step, []):
                bz, by, bx = z + dz, (y + dy) % 2, (x + dx) % 2
                cond = None if dz == 0 else ((bz >= 0) & (bz <= DEPTH - 1))
                maybe(cond, lambda: act(part, bz, by, bx, onward))

    def forward(part, bz, by, bx, onward, step):
        if step:
            copy(part, bz, by, core, bx, "core").wait_recv()
        for way in onward:
            maybe(has.get(way), lambda way=way: copy(part, bz, by, core, bx, way).start())

    def finish(part, bz, by, bx, onward):
        copy(part, bz, by, 1 - core, bx, "core").wait_recv()
        for way in onward:
            maybe(has.get(way), lambda way=way: copy(part, bz, by, core, bx, way).wait_send())

    for step in range(6):
        each(step, lambda *a, step=step: forward(*a, step))
    for step in range(6):
        each(step, finish)
    stores = []
    for i, (part, weight, at, src, width) in enumerate(pieces):
        for side in range(2):
            stores.append(
                pltpu.make_async_copy(
                    bufs[part].at[side, :, :, pl.ds(at, width)],
                    outs[weight].at[:, :, pl.ds(side * widths[weight] + src, width)],
                    local.at[1 + side, i],
                )
            )
    for store in stores:
        store.start()
    for store in stores:
        store.wait()


def gather_near(shards, cuts):
    rows = shards[0].shape[0]
    widths = [shard.shape[1] for shard in shards]
    outs = pl.pallas_call(
        lambda *refs: gather_kernel(widths, cuts, *refs),
        in_specs=[pl.BlockSpec(memory_space=pl.ANY)] * len(shards),
        out_specs=[pl.BlockSpec(memory_space=pl.ANY)] * len(shards),
        out_shape=[jax.ShapeDtypeStruct((16, rows, 2 * width), bf16) for width in widths],
        scratch_shapes=[pltpu.VMEM((2, 16, rows, cuts[i + 1] - cuts[i]), bf16) for i in range(3)]
        + [
            pltpu.SemaphoreType.DMA((3, 16, 5)),
            pltpu.SemaphoreType.DMA((3, 32)),
            pltpu.SemaphoreType.DMA((3, 8)),
        ],
        compiler_params=pltpu.CompilerParams(
            collective_id=0, has_side_effects=True, vmem_limit_bytes=56 << 20
        ),
        cost_estimate=pl.CostEstimate(flops=0, bytes_accessed=200 << 20, transcendentals=0),
        name="gather_weights",
    )(*shards)
    return [out.reshape(16 * rows, 2 * width) for out, width in zip(outs, widths)]


class Reducer:
    def __init__(self, place, grads, widths, cuts, scratch):
        self.z, self.y, self.core, self.x = place
        z, y, core, x = place
        self.grads = grads
        self.widths = widths
        self.acc, self.rcore = scratch[0:3], scratch[3:6]
        rx, ry, self.rz, self.cy, self.cx = scratch[6:8], scratch[8:10], scratch[10:13], scratch[13], scratch[14]
        self.final = scratch[15:18]
        (
            self.s_core, self.r_core, s_x, r_x, s_y, r_y, self.s_z, self.r_z, self.s_c, self.r_c, self.s_load,
            self.s_out,
        ) = scratch[18:]
        self.up, self.down = (row_of(z + 1, y, core), x), (row_of(z - 1, y, core), x)
        self.to_y, self.to_x = (row_of(z, 1 - y, core), x), (row_of(z, y, core), 1 - x)
        self.to_core = (row_of(z, y, 1 - core), x)
        self.by_part = [[p for p in pieces_of(widths, cuts) if p[0] == part] for part in range(3)]
        self.first = [(rx[0], s_x, r_x, self.to_x), (ry[0], s_y, r_y, self.to_y)]
        self.second = [(ry[1], s_y, r_y, self.to_y), (rx[1], s_x, r_x, self.to_x)]

    SCRATCH = 30

    @staticmethod
    def scratch_shapes(widths, cuts, rows):
        w = [cuts[i + 1] - cuts[i] for i in range(3)]
        dma = pltpu.SemaphoreType.DMA

        def low(*shape):
            return pltpu.VMEM(shape, bf16)

        scratch = [low(2, 4, 2, rows, k) for k in w] * 2
        scratch += [low(4, 2, rows, w[0]), low(4, rows, w[1])]
        scratch += [low(4, 2, rows, w[1]), low(4, rows, w[0])]
        scratch += [low(2, 4, rows, w[0]), low(2, 4, rows, w[1]), low(2, 4, 2, 2, rows, w[2])]
        scratch += [low(2, rows, w[2]), low(rows, w[2])]
        scratch += [pltpu.VMEM((rows, k), f32) for k in w]
        scratch += [dma((3, 2, 4, 2, 2)), dma((3, 2, 4, 2, 2)), dma((2, 4)), dma((2, 4)), dma((2, 4)), dma((2, 4))]
        scratch += [dma((3, 2, 4)), dma((3, 2, 4)), dma((2,)), dma((2,)), dma((3, 2, 2)), dma((3, 2))]
        return scratch

    def cols(self, weight, side, src, width):
        return pl.ds(pl.multiple_of(side * self.widths[weight] + src, 128), width)

    def loop(self, act):
        def step(zi, carry):
            act(zi)
            return carry

        lax.fori_loop(0, DEPTH, step, 0)

    def add(self, total, term):
        total[...] = total[...] + term[...]

    def loads(self, part):
        return [
            pltpu.make_async_copy(
                self.grads[weight].at[:, :, self.core, :, self.cols(weight, side, src, width)],
                self.acc[part].at[side, :, :, :, pl.ds(at, width)],
                self.s_load.at[part, side, i],
            )
            for i, (_, weight, at, src, width) in enumerate(self.by_part[part])
            for side in range(2)
        ]

    def view(self, part, ref, far, zi):
        if part == 0:
            return ref.at[(1 - self.x) if far else self.x, zi]
        return ref.at[:, zi, (1 - self.y) if far else self.y]

    def core_copies(self, part, far, zi):
        other = 1 - self.core
        copies = []
        for i, (_, weight, at, src, width) in enumerate(self.by_part[part]):
            cols = pl.ds(at, width)
            if part == 0:
                sides = [(1 - self.x) if far else self.x]
            else:
                sides = [0, 1]
            for k, side in enumerate(sides):
                gcols = self.cols(weight, side, src, width)
                if part == 1:
                    by = (1 - self.y) if far else self.y
                    src_ref = self.grads[weight].at[zi, by, other, :, gcols]
                    dst_ref = self.rcore[1].at[side, zi, by, :, cols]
                else:
                    src_ref = self.grads[weight].at[zi, :, other, :, gcols]
                    dst_ref = self.rcore[part].at[side, zi, :, :, cols]
                slot = (part, int(far), zi, i, k)
                copies.append(remote(src_ref, dst_ref, self.s_core.at[slot], self.r_core.at[slot], self.to_core))
        return copies

    def start(self, parts):
        for part in parts:
            for load in self.loads(part):
                load.start()

        def begin(far):
            def act(zi):
                for part in parts:
                    if far or part < 2:
                        for copy in self.core_copies(part, far, zi):
                            copy.start()

            self.loop(act)

        begin(True)
        begin(False)

    def first_copy(self, part, zi):
        buf, send, recv, device = self.first[part]
        return remote(self.view(part, self.acc[part], True, zi), buf.at[zi], send.at[0, zi], recv.at[0, zi], device)

    def half_of(self, part, zi, far):
        if part == 0:
            return self.acc[0].at[self.x, zi, (1 - self.y) if far else self.y]
        return self.acc[1].at[(1 - self.x) if far else self.x, zi, self.y]

    def second_copy(self, part, zi):
        buf, send, recv, device = self.second[part]
        return remote(self.half_of(part, zi, True), buf.at[zi], send.at[1, zi], recv.at[1, zi], device)

    def far(self, parts):
        for part in parts:
            for load in self.loads(part):
                load.wait()

        def act(zi):
            for part in parts:
                for copy in self.core_copies(part, True, zi):
                    copy.wait_recv()
                if part == 2:
                    self.add(self.acc[2].at[:, zi], self.rcore[2].at[:, zi])
                else:
                    self.add(self.view(part, self.acc[part], True, zi), self.view(part, self.rcore[part], True, zi))
                    self.first_copy(part, zi).start()

        self.loop(act)

    def near(self, parts):
        def act(zi):
            for part in parts:
                for copy in self.core_copies(part, False, zi):
                    copy.wait_recv()
                mine = self.view(part, self.acc[part], False, zi)
                self.add(mine, self.view(part, self.rcore[part], False, zi))
                self.first_copy(part, zi).wait_recv()
                self.add(mine, self.first[part][0].at[zi])
                self.second_copy(part, zi).start()

        self.loop(act)

    def last(self, parts):
        def act(zi):
            for part in parts:
                self.second_copy(part, zi).wait_recv()
                self.add(self.half_of(part, zi, False), self.second[part][0].at[zi])

        self.loop(act)

    def block(self, part, zi):
        if part == 2:
            return self.acc[2].at[:, zi]
        return self.acc[part].at[self.x, zi, self.y]

    def line_copy(self, part, direction, zd):
        return remote(
            self.block(part, zd),
            self.rz[part].at[direction, zd],
            self.s_z.at[part, direction, zd],
            self.r_z.at[part, direction, zd],
            self.down if direction else self.up,
        )

    def line(self, parts, step):
        for direction in range(2):
            at = DEPTH - 1 - step if direction else step
            for zd in (0, 1, 2) if direction else (3, 2, 1):
                if not ((at > zd) if direction else (at < zd)):
                    continue
                for part in parts:

                    def act(part=part, direction=direction, zd=zd):
                        if step > 0:
                            self.line_copy(part, direction, zd).wait_recv()
                            self.add(self.block(part, zd), self.rz[part].at[direction, zd])
                        self.line_copy(part, direction, zd).start()

                    pl.when(self.z == at)(act)

    def line_end(self, parts):
        for part in parts:
            for direction in range(2):

                def act(part=part, direction=direction):
                    self.line_copy(part, direction, self.z).wait_recv()
                    self.add(self.block(part, self.z), self.rz[part].at[direction, self.z])

                pl.when((self.z < DEPTH - 1) if direction else (self.z > 0))(act)

    def y_copy(self):
        return remote(self.acc[2].at[:, self.z, 1 - self.y], self.cy, self.s_c.at[0], self.r_c.at[0], self.to_y)

    def x_copy(self):
        return remote(self.acc[2].at[1 - self.x, self.z, self.y], self.cx, self.s_c.at[1], self.r_c.at[1], self.to_x)

    def turn(self):
        self.y_copy().wait_recv()
        self.add(self.acc[2].at[:, self.z, self.y], self.cy)
        self.x_copy().start()

    def turn_end(self):
        self.x_copy().wait_recv()
        self.add(self.acc[2].at[self.x, self.z, self.y], self.cx)

    def stores(self, outs):
        return [
            pltpu.make_async_copy(
                self.final[part].at[:, pl.ds(at, width)], outs[weight].at[:, pl.ds(src, width)], self.s_out.at[part, i]
            )
            for part in range(3)
            for i, (_, weight, at, src, width) in enumerate(self.by_part[part])
        ]

    def finish(self, outs):
        for part in range(3):
            self.final[part][...] = self.acc[part][self.x, self.z, self.y].astype(f32)
        for store in self.stores(outs):
            store.start()

    def drain(self, outs):
        def act(zi):
            for part in range(3):
                for copy in self.core_copies(part, True, zi):
                    copy.wait_send()
                if part < 2:
                    for copy in self.core_copies(part, False, zi):
                        copy.wait_send()
                    self.first_copy(part, zi).wait_send()
                    self.second_copy(part, zi).wait_send()

        self.loop(act)
        for part in range(3):
            for direction in range(2):
                for zd in range(DEPTH):
                    pl.when((self.z > zd) if direction else (self.z < zd))(
                        lambda part=part, direction=direction, zd=zd: self.line_copy(part, direction, zd).wait_send()
                    )
        self.y_copy().wait_send()
        self.x_copy().wait_send()
        for store in self.stores(outs):
            store.wait()


PAIR_ORDER = (2, 5, 0, 3, 1, 4)


def back_kernel(shape, *refs):
    (
        g_out, g_fc, g_proj, packed, attended, p_all, inv_all, gatt, normed_t, w_qkv, x_all, middle, gain_ref, small_in,
        o_qkv, o_out, o_fc, o_proj, o_sum, o_input,
    ) = refs[:20]
    scr = refs[20:]
    first = Reducer.SCRATCH
    place = my_place()
    z, y, core, x = place
    early = Reducer(place, [g_out, g_fc, g_proj], shape["early"], shape["early_cuts"], scr[:first])
    qkv, o_buf, p_buf, inv_buf, g_buf, nt_buf, w_buf, x_buf, m_buf, gqkv, gi, col_sum, srecv, sacc = scr[2 * first : 2 * first + 14]
    s_all, s_pair, s_mid, s_gi, r_gi, l_gi, s_s, r_s = scr[2 * first + 14 :]
    late = Reducer(place, [gqkv], shape["late"], shape["late_cuts"], scr[first : 2 * first])
    whole = [
        pltpu.make_async_copy(packed, qkv, s_all.at[0]),
        pltpu.make_async_copy(normed_t, nt_buf, s_all.at[1]),
        pltpu.make_async_copy(w_qkv, w_buf, s_all.at[2]),
        pltpu.make_async_copy(x_all, x_buf, s_all.at[3]),
    ]

    def pair_loads(step):
        j = PAIR_ORDER[step]
        slot = step % 2
        cols = pl.ds(j * PAIR, PAIR)
        return [
            pltpu.make_async_copy(p_all.at[j], p_buf.at[slot], s_pair.at[slot, 0]),
            pltpu.make_async_copy(attended.at[:, cols], o_buf.at[slot], s_pair.at[slot, 1]),
            pltpu.make_async_copy(inv_all.at[:, cols], inv_buf.at[slot], s_pair.at[slot, 2]),
            pltpu.make_async_copy(gatt.at[:, cols], g_buf.at[slot], s_pair.at[slot, 3]),
        ]

    def begin(copies):
        for copy in copies:
            copy.start()

    def end(copies):
        for copy in copies:
            copy.wait()

    begin(whole[:1])
    begin(pair_loads(0))
    begin(whole[1:])
    to_z1 = (row_of(z + 1 - 2 * (z % 2), y, core), x)
    to_z2 = (row_of((z + 2) % 4, y, core), x)
    greet([early.to_core, early.to_x, early.to_y, to_z2], z, early.up, early.down)
    early.start((0, 1, 2))
    end(whole[:1])

    def pair(step):
        j = PAIR_ORDER[step]
        slot = step % 2
        if step < 5:
            begin(pair_loads(step + 1))
        end(pair_loads(step))
        attend_back_pair(qkv, o_buf.at[slot], p_buf.at[slot], inv_buf.at[slot], g_buf.at[slot], col_sum.at[j], 3 * PAIR * j)
        if step == 0:
            end(whole[1:2])
        cols = slice(3 * PAIR * j, 3 * PAIR * (j + 1))
        grad = nn(nt_buf[...], qkv[:, cols]).astype(bf16)
        gqkv[:, :, :, :, cols] = grad.reshape(gqkv.shape[:4] + (3 * PAIR,))

    rows = m_buf.shape[1]
    blocks = x_buf.shape[0] // rows

    def mid_load(i):
        return pltpu.make_async_copy(middle.at[pl.ds(i * rows, rows)], m_buf.at[i % 2], s_mid.at[i % 2])

    def input_copies(i):
        span = pl.ds(i * rows, rows)
        return (
            pltpu.make_async_copy(gi.at[0, span], o_input.at[x, span], l_gi.at[i]),
            remote(gi.at[1, span], o_input.at[x, span], s_gi.at[i], r_gi.at[i], early.to_x),
        )

    sums = [None, None]

    def input_block(i):
        span = slice(i * rows, (i + 1) * rows)
        grad = nt(qkv[span, :], w_buf[...])
        if i + 1 < blocks:
            mid_load(i + 1).start()
        mid_load(i).wait()
        value = x_buf[span, :].astype(f32)
        width = value.shape[1]
        average = jnp.sum(value, axis=1, keepdims=True) / width
        square = jnp.sum(value * value, axis=1, keepdims=True) / width
        inverse = lax.rsqrt(square - average * average + epsilon)
        centred = (value - average) * inverse
        scaled = grad * gain_ref[...]
        one = jnp.sum(scaled, axis=1, keepdims=True) / width
        two = jnp.sum(scaled * centred, axis=1, keepdims=True) / width
        out = m_buf[i % 2] + inverse * (scaled - one - centred * two)
        for k, term in enumerate((grad * centred, grad)):
            term = jnp.sum(term, axis=0, keepdims=True)
            sums[k] = term if sums[k] is None else sums[k] + term
        half = width // 2
        is_low = x == 0
        gi[0, span, :] = jnp.where(is_low, out[:, :half], out[:, half:]).astype(bf16)
        gi[1, span, :] = jnp.where(is_low, out[:, half:], out[:, :half]).astype(bf16)
        for copy in input_copies(i):
            copy.start()

    partners = [early.to_core, early.to_x, early.to_y, to_z1, to_z2]

    def small_copy(step):
        return remote(sacc.at[step], srecv.at[step], s_s.at[step], r_s.at[step], partners[step])

    def small_start():
        sacc[0] = small_in[...]
        at = 0
        for k in range(2):
            for i in range(6):
                sacc[0, at : at + 1, :] = sums[k][:, i * PAIR : (i + 1) * PAIR]
                at += 1
        for k in range(2):
            for i in range(6):
                sacc[0, at : at + 1, :] = col_sum[i, k]
                at += 1
        small_copy(0).start()

    def small_next(step):
        small_copy(step).wait()
        sacc[step + 1] = sacc[step] + srecv[step]
        if step < 4:
            small_copy(step + 1).start()

    both = (0, 1)
    pair(0)
    early.far((0, 1, 2))
    early.line((2,), 0)
    pair(1)
    late.start((2,))
    early.line((2,), 1)
    pair(2)
    early.line((2,), 2)
    late.far((2,))
    late.line((2,), 0)
    pair(3)
    late.start((0,))
    early.near(both)
    early.line_end((2,))
    early.y_copy().start()
    late.line((2,), 1)
    pair(4)
    late.far((0,))
    early.turn()
    late.line((2,), 2)
    mid_load(0).start()
    pair(5)
    late.start((1,))
    early.last(both)
    early.line(both, 0)
    late.line_end((2,))
    late.y_copy().start()
    early.turn_end()
    end(whole[2:])
    input_block(0)
    late.far((1,))
    early.line(both, 1)
    late.turn()
    late.near((0,))
    input_block(1)
    early.line(both, 2)
    late.turn_end()
    late.near((1,))
    input_block(2)
    late.last((0,))
    late.line((0,), 0)
    input_block(3)
    small_start()
    early.line_end(both)
    early.finish([o_out, o_fc, o_proj])
    late.last((1,))
    late.line((1,), 0)
    small_next(0)
    late.line(both, 1)
    small_next(1)
    late.line(both, 2)
    small_next(2)
    late.line_end(both)
    late.finish([o_qkv])
    small_next(3)
    small_next(4)
    o_sum[...] = sacc[5]
    for i in range(blocks):
        local, other = input_copies(i)
        local.wait()
        other.wait()
    early.drain([o_out, o_fc, o_proj])
    late.drain([o_qkv])


def back_near(grads, packed, attended, p, inv, gatt, normed_t, w_qkv, x, middle, gain, small, rows):
    length, width = x.shape
    wide = packed.shape[1]
    early = [grad.shape[1] // 2 for grad in grads]
    shape = {"early": early, "early_cuts": part_cuts(early, *REDUCE_CUT), "late": [wide // 2]}
    shape["late_cuts"] = [0, wide // 6, wide // 3, wide // 2]
    dma = pltpu.SemaphoreType.DMA
    half = length // 2
    blocks = 4
    scratch = Reducer.scratch_shapes(early, shape["early_cuts"], rows)
    scratch += Reducer.scratch_shapes(shape["late"], shape["late_cuts"], rows)
    scratch += [
        pltpu.VMEM((length, wide), bf16),
        pltpu.VMEM((2, length, PAIR), bf16),
        pltpu.VMEM((2, 2, 3, half, half), bf16),
        pltpu.VMEM((2, length, PAIR), f32),
        pltpu.VMEM((2, length, PAIR), bf16),
        pltpu.VMEM((width, length), bf16),
        pltpu.VMEM((width, wide), bf16),
        pltpu.VMEM((length, width), bf16),
        pltpu.VMEM((2, length // blocks, width), f32),
        pltpu.VMEM((4, 2, 2, rows, wide), bf16),
        pltpu.VMEM((2, length, width // 2), bf16),
        pltpu.VMEM((width // PAIR, 2, 1, PAIR), f32),
        pltpu.VMEM((5,) + small.shape, f32),
        pltpu.VMEM((6,) + small.shape, f32),
    ]
    scratch += [dma((4,)), dma((2, 4)), dma((2,)), dma((4,)), dma((4,)), dma((4,)), dma((5,)), dma((5,))]
    shaped = [grad.reshape(4, 2, 2, rows, grad.shape[1]) for grad in grads]
    any_space = pl.BlockSpec(memory_space=pl.ANY)
    vmem = pl.BlockSpec(memory_space=pltpu.VMEM)
    outs = pl.pallas_call(
        lambda *refs: back_kernel(shape, *refs),
        in_specs=[any_space] * 12 + [vmem, vmem],
        out_specs=[any_space] * 4 + [vmem, any_space],
        out_shape=[jax.ShapeDtypeStruct((rows, w), f32) for w in [wide // 2] + early]
        + [jax.ShapeDtypeStruct(small.shape, f32), jax.ShapeDtypeStruct((2, length, width // 2), bf16)],
        scratch_shapes=scratch,
        compiler_params=pltpu.CompilerParams(
            collective_id=1, has_side_effects=True, vmem_limit_bytes=67043328
        ),
        cost_estimate=pl.CostEstimate(flops=30 << 30, bytes_accessed=200 << 20, transcendentals=0),
        name="reduce_grads",
    )(*shaped, packed, attended, p, inv, gatt, normed_t, w_qkv, x, middle, gain.reshape(1, -1), small)
    return outs


def gather_far(shards):
    fulls = []
    for shard in shards:
        rows = lax.all_gather(shard, ("col", "row"), axis=0, tiled=True)
        fulls.append(jnp.concatenate(jnp.split(rows, 2, axis=0), axis=1))
    return fulls


def reduce_far(grads, small):
    outs = []
    for grad in grads:
        halves = jnp.concatenate(jnp.split(grad, 2, axis=1), axis=0)
        outs.append(lax.psum_scatter(halves, ("col", "row"), scatter_dimension=0, tiled=True).astype(f32))
    return outs, lax.psum(small, ("row", "col"))


def part_cuts(widths, first, second):
    total = sum(widths) // 128
    one = round(total * first)
    two = round(total * (first + second))
    return [0, one * 128, two * 128, total * 128]


def layer_norm(value):
    width = value.shape[-1]
    average = jnp.sum(value, axis=-1, keepdims=True) / width
    square = jnp.sum(value * value, axis=-1, keepdims=True) / width
    inverse = lax.rsqrt(square - average * average + epsilon)
    return (value - average) * inverse, inverse


def norm_backward(grad, centred, inverse, gain):
    scaled = grad * gain
    first = jnp.mean(scaled, axis=-1, keepdims=True)
    second = jnp.mean(scaled * centred, axis=-1, keepdims=True)
    back = inverse * (scaled - first - centred * second)
    return back, jnp.sum(grad * centred, axis=0), jnp.sum(grad, axis=0)


def by_pairs(block):
    rows, three, half = block.shape
    return block.reshape(rows, three, half // PAIR, PAIR).transpose(0, 2, 1, 3).reshape(rows, three * half)


def body(
    near, x_in, span_start, span_kind, ln1_gain, ln1_bias, w_qkv, b_query, b_value, w_out, b_out,
    ln2_gain, ln2_bias, w_fc, b_fc, w_proj, b_proj, cotangent,
):
    half_width = x_in.shape[2]
    shard = w_qkv.shape[0]
    col = lax.axis_index("col")

    x_own = own_micro(x_in)
    width = x_own.shape[1]
    residual = x_own.astype(f32)
    grad_out = own_micro(cotangent)
    shards = [by_pairs(w_qkv), w_out.T, w_fc, w_proj.T]
    if near:
        qkv_all, out_all, fc_all, proj_all = gather_near(shards, part_cuts([s.shape[1] for s in shards], *GATHER_CUT))
    else:
        qkv_all, out_all, fc_all, proj_all = gather_far(shards)

    vectors = [ln1_gain, ln1_bias, b_query, b_value, b_out, ln2_gain, ln2_bias, b_fc, b_proj]
    flat = jnp.concatenate(vectors)
    flat_other = swap(flat)
    full = []
    at = 0
    for vector in vectors:
        full.append(ordered(vector, flat_other[at : at + vector.shape[0]], 0))
        at += vector.shape[0]
    ln1_gain, ln1_bias, b_query, b_value, b_out, ln2_gain, ln2_bias, b_fc, b_proj = full

    starts = lax.dynamic_index_in_dim(span_start, col, 0, keepdims=False)[0]
    kinds = lax.dynamic_index_in_dim(span_kind, col, 0, keepdims=False)[0]
    spans = jnp.stack([starts, kinds])

    centred_first, inverse_first = layer_norm(residual)
    normed_first = (centred_first * ln1_gain + ln1_bias).astype(bf16)
    bias = jnp.stack([b_query, jnp.zeros_like(b_query), b_value]).reshape(3, -1, PAIR)
    packed = (nn(normed_first, qkv_all) + bias.transpose(1, 0, 2).reshape(-1)).astype(bf16)
    attended, p, inv = attend_forward(packed, spans)
    middle = residual + nt(attended, out_all) + b_out
    centred_second, inverse_second = layer_norm(middle)
    normed_second = (centred_second * ln2_gain + ln2_bias).astype(bf16)
    hidden = nn(normed_second, fc_all) + b_fc
    squared = hidden * hidden
    tanh = jnp.tanh(GELU_A * hidden * (1.0 + GELU_B * squared))
    active = (0.5 * hidden * (1.0 + tanh)).astype(bf16)
    slope = (
        0.5 * (1.0 + tanh)
        + 0.5 * hidden * (1.0 - tanh * tanh) * GELU_A * (1.0 + 3.0 * GELU_B * squared)
    ).astype(bf16)
    layer_out = back_micro((middle + nt(active, proj_all) + b_proj).astype(bf16))

    grad_out_wide = grad_out.astype(f32)
    g_proj = tn(grad_out, active).astype(bf16)
    grad_hidden = (nn(grad_out, proj_all) * slope.astype(f32)).astype(bf16)
    g_fc = tn(normed_second, grad_hidden).astype(bf16)
    g_bfc = jnp.sum(grad_hidden.astype(f32), axis=0)
    grad_normed = nt(grad_hidden, fc_all)
    back, g_ln2_gain, g_ln2_bias = norm_backward(grad_normed, centred_second, inverse_second, ln2_gain)
    grad_middle = grad_out_wide + back
    g_bproj = jnp.sum(grad_out_wide, axis=0)
    g_bout = jnp.sum(grad_middle, axis=0)
    grad_low = grad_middle.astype(bf16)
    g_out = tn(grad_low, attended).astype(bf16)
    grad_attended = nn(grad_low, out_all).astype(bf16)
    zeros = jnp.zeros((width,), f32)
    small = [zeros, zeros, zeros, zeros, g_bout, g_ln2_gain, g_ln2_bias, g_bfc, g_bproj]
    if near:
        flat = jnp.concatenate(small).reshape(-1, 128)
        *outs, summed, grad_input = back_near(
            [g_out, g_fc, g_proj], packed, attended, p, inv, grad_attended, normed_first.T, qkv_all,
            x_own, grad_middle, ln1_gain, flat, shard,
        )
    else:
        grad_packed, sums = attend_backward(packed, attended, p, inv, grad_attended)
        g_qkv = tn(normed_first, grad_packed).astype(bf16)
        grad_normed = nt(grad_packed, qkv_all)
        back, g_ln1_gain, g_ln1_bias = norm_backward(grad_normed, centred_first, inverse_first, ln1_gain)
        grad_input = back_micro((grad_middle + back).astype(bf16))
        small[:4] = [g_ln1_gain, g_ln1_bias, sums[:, 0, 0].reshape(-1), sums[:, 1, 0].reshape(-1)]
        outs, summed = reduce_far([g_qkv, g_out, g_fc, g_proj], jnp.concatenate(small))
    out_qkv, out_out, out_fc, out_proj = outs
    summed = summed.reshape(-1)
    kept = []
    at = 0
    for vector in small:
        size = vector.shape[0] // 2
        kept.append(lax.dynamic_slice_in_dim(summed, at + col * size, size, 0))
        at += vector.shape[0]
    return (
        layer_out,
        grad_input,
        kept[0],
        kept[1],
        out_qkv.reshape(shard, -1, 3, PAIR).transpose(0, 2, 1, 3).reshape(shard, 3, half_width),
        kept[2],
        kept[3],
        out_out.T,
        kept[4],
        kept[5],
        kept[6],
        out_fc,
        kept[7],
        out_proj.T,
        kept[8],
    )


def solution(mesh):
    placed = (
        P(None, "row", "col"), P(None, "row", None), P(None, "row", None), P("col"), P("col"),
        P("row", None, "col"), P("col"), P("col"), P("col", "row"), P("col"), P("col"), P("col"),
        P("row", "col"), P("col"), P("col", "row"), P("col"), P(None, "row", "col"),
    )
    near = mesh.shape["row"] == 16
    return jax.shard_map(
        partial(body, near),
        mesh=mesh,
        in_specs=placed,
        out_specs=(
            P(None, "row", "col"), P(None, "row", "col"), P("col"), P("col"), P("row", None, "col"),
            P("col"), P("col"), P("col", "row"), P("col"), P("col"), P("col"), P("row", "col"),
            P("col"), P("col", "row"), P("col"),
        ),
        check_vma=False,
    )
```

```python
from functools import partial

import jax
import jax.numpy as jnp
from jax import lax
from jax.experimental import pallas as pl
from jax.experimental.pallas import tpu as pltpu
from jax.sharding import PartitionSpec as P

HEAD = 64
IMG = 256
epsilon = 1e-05
bf16 = jnp.bfloat16
f32 = jnp.float32
GELU_A = 0.7978845608028654
GELU_B = 0.044715
PAIR = 2 * HEAD


def nn(a, b):
    return lax.dot_general(a, b, (((1,), (0,)), ((), ())), preferred_element_type=f32)


def nt(a, b):
    return lax.dot_general(a, b, (((1,), (1,)), ((), ())), preferred_element_type=f32)


def tn(a, b):
    return lax.dot_general(a, b, (((0,), (0,)), ((), ())), preferred_element_type=f32)


def half_bias(start, kind, part, half):
    base = part * half
    rows = lax.broadcasted_iota(jnp.int32, (half, half), 0) + base
    cols = lax.broadcasted_iota(jnp.int32, (half, half), 1) + base
    first = jnp.where(kind == 1, start, 4 * half)
    joined = (rows >= first) & (rows < first + IMG) & (cols >= first) & (cols < first + IMG)
    return jnp.where((cols <= rows) | joined, 0.0, -1e30).astype(f32)


def lane_masks(rows):
    lane = lax.broadcasted_iota(jnp.int32, (rows, PAIR), 1)
    return lane < HEAD


def attend_pair(qkv_ref, o_ref, p_ref, inv_ref, bias_ref):
    half = qkv_ref.shape[0] // 2
    q_ref, k_ref, v_ref = (qkv_ref.at[:, i * PAIR : (i + 1) * PAIR] for i in range(3))
    low = lane_masks(half)
    for part in range(2):
        rows = slice(part * half, (part + 1) * half)
        q = q_ref[rows, :] * jnp.asarray(0.125, bf16)
        zero = jnp.zeros_like(q)
        outs = []
        invs = []
        for head in range(2):
            mine = low if head == 0 else jnp.logical_not(low)
            qh = jnp.where(mine, q, zero)
            own = nt(qh, k_ref[rows, :]) + bias_ref[part]
            largest = jnp.max(own, axis=1, keepdims=True)
            if part == 1:
                before = nt(qh, k_ref[:half, :])
                largest = jnp.maximum(largest, jnp.max(before, axis=1, keepdims=True))
            own = jnp.exp(own - largest)
            total = jnp.sum(own, axis=1, keepdims=True)
            own = own.astype(bf16)
            p_ref[head, 2 * part] = own
            out = nn(own, v_ref[rows, :])
            if part == 1:
                before = jnp.exp(before - largest)
                total = total + jnp.sum(before, axis=1, keepdims=True)
                before = before.astype(bf16)
                p_ref[head, 1] = before
                out = out + nn(before, v_ref[:half, :])
            inv = 1.0 / total
            outs.append(out * inv)
            invs.append(inv)
        o_ref[rows, :] = jnp.where(low, outs[0], outs[1]).astype(bf16)
        inv_ref[rows, :] = jnp.where(low, invs[0], invs[1])


def attend_forward_kernel(span_ref, qkv_ref, o_ref, p_ref, inv_ref, bias_ref):
    half = qkv_ref.shape[0] // 2

    @pl.when(pl.program_id(0) == 0)
    def _():
        for part in range(2):
            bias_ref[part] = half_bias(span_ref[0, part], span_ref[1, part], part, half)

    attend_pair(qkv_ref, o_ref, p_ref.at[0], inv_ref, bias_ref)


def attend_forward(packed, spans):
    length = packed.shape[0]
    width = packed.shape[1] // 3
    pairs = width // PAIR
    half = length // 2
    return pl.pallas_call(
        attend_forward_kernel,
        grid=(pairs,),
        in_specs=[
            pl.BlockSpec(memory_space=pltpu.SMEM),
            pl.BlockSpec((length, 3 * PAIR), lambda j: (0, j)),
        ],
        out_specs=[
            pl.BlockSpec((length, PAIR), lambda j: (0, j)),
            pl.BlockSpec((1, 2, 3, half, half), lambda j: (j, 0, 0, 0, 0)),
            pl.BlockSpec((length, PAIR), lambda j: (0, j)),
        ],
        out_shape=[
            jax.ShapeDtypeStruct((length, width), bf16),
            jax.ShapeDtypeStruct((pairs, 2, 3, half, half), bf16),
            jax.ShapeDtypeStruct((length, width), f32),
        ],
        scratch_shapes=[pltpu.VMEM((2, half, half), f32)],
        compiler_params=pltpu.CompilerParams(vmem_limit_bytes=60 << 20),
        cost_estimate=pl.CostEstimate(
            flops=4 * 3 * half * half * width * 4, bytes_accessed=24 << 20, transcendentals=3 * half * half * 12
        ),
        name="attend_forward",
    )(spans, packed)


def attend_back_pair(qkv_ref, o_ref, p_ref, inv_ref, g_ref, sum_ref, at):
    length = qkv_ref.shape[0]
    half = length // 2
    low = lane_masks(half)
    q_ref, k_ref, v_ref = (qkv_ref.at[:, at + i * PAIR : at + (i + 1) * PAIR] for i in range(3))
    dks = [None, None]
    dvs = [None, None]
    dqs = []

    def add(total, part, value):
        total[part] = value if total[part] is None else total[part] + value

    for part in range(2):
        rows = slice(part * half, (part + 1) * half)
        inv = inv_ref[rows, :]
        g = g_ref[rows, :].astype(f32) * inv
        scaled = g * o_ref[rows, :].astype(f32)
        q = q_ref[rows, :]
        gb = g.astype(bf16)
        zero = jnp.zeros_like(gb)
        dq = None
        for head in range(2):
            mine = low if head == 0 else jnp.logical_not(low)
            gh = jnp.where(mine, gb, zero)
            qh = jnp.where(mine, q, zero)
            rowdot = jnp.sum(jnp.where(mine, scaled, 0.0), axis=1, keepdims=True)
            for kpart in range(part + 1):
                krows = slice(kpart * half, (kpart + 1) * half)
                p = p_ref[head, part + kpart]
                kh = jnp.where(mine, k_ref[krows, :], zero)
                dp = nt(gh, v_ref[krows, :])
                ds = (p.astype(f32) * (dp - rowdot)).astype(bf16)
                term = nn(ds, kh)
                dq = term if dq is None else dq + term
                add(dks, kpart, tn(ds, qh))
                add(dvs, kpart, tn(p, gh))
        dqs.append(dq)
    for which, (ref, values, scale) in enumerate(((q_ref, dqs, 0.125), (k_ref, dks, 0.125), (v_ref, dvs, 1.0))):
        total = None
        for part in range(2):
            value = (values[part] * scale).astype(bf16)
            ref[part * half : (part + 1) * half, :] = value
            term = jnp.sum(value.astype(f32), axis=0, keepdims=True)
            total = term if total is None else total + term
        if which != 1:
            sum_ref[which // 2] = total


def attend_backward_kernel(qkv_ref, o_ref, p_ref, inv_ref, g_ref, d_ref, sum_ref):
    d_ref[...] = qkv_ref[...]
    attend_back_pair(d_ref, o_ref, p_ref.at[0], inv_ref, g_ref, sum_ref.at[0], 0)


def attend_backward(packed, attended, p, inv, grad_attended):
    length = packed.shape[0]
    width = packed.shape[1] // 3
    pairs = width // PAIR
    half = length // 2
    one = pl.BlockSpec((length, PAIR), lambda j: (0, j))
    three = pl.BlockSpec((length, 3 * PAIR), lambda j: (0, j))
    return pl.pallas_call(
        attend_backward_kernel,
        grid=(pairs,),
        in_specs=[three, one, pl.BlockSpec((1, 2, 3, half, half), lambda j: (j, 0, 0, 0, 0)), one, one],
        out_specs=[three, pl.BlockSpec((1, 2, 1, PAIR), lambda j: (j, 0, 0, 0))],
        out_shape=[
            jax.ShapeDtypeStruct(packed.shape, bf16),
            jax.ShapeDtypeStruct((pairs, 2, 1, PAIR), f32),
        ],
        compiler_params=pltpu.CompilerParams(vmem_limit_bytes=56 << 20),
        name="attend_backward",
    )(packed, attended, p, inv, grad_attended)


SWAP = [(0, 1), (1, 0)]


def swap(value):
    return lax.ppermute(value, "col", SWAP)


def ordered(mine, other, axis):
    first = lax.axis_index("col") == 0
    low = jnp.where(first, mine, other)
    high = jnp.where(first, other, mine)
    return jnp.concatenate([low, high], axis=axis)


def own_micro(halves):
    col = lax.axis_index("col")
    mine = lax.dynamic_index_in_dim(halves, col, 0, keepdims=False)
    other = swap(lax.dynamic_index_in_dim(halves, 1 - col, 0, keepdims=False))
    return ordered(mine, other, 1)


def back_micro(full):
    col = lax.axis_index("col")
    half = full.shape[1] // 2
    mine = lax.dynamic_slice_in_dim(full, col * half, half, 1)
    other = swap(lax.dynamic_slice_in_dim(full, (1 - col) * half, half, 1))
    first = col == 0
    return jnp.stack([jnp.where(first, mine, other), jnp.where(first, other, mine)])


MIDDLE_CUT = (0.467, 0.4)
GATHER_CUT = (0.33, 0.5)
REDUCE_CUT = (0.34, 0.33)


MESH = pl.DeviceIdType.MESH
DEPTH = 4
WAYS = ("up", "down", "y", "x", "core")
ORDERS = ("zyx", "zxy", "xyz")


def row_of(z, y, core):
    return z * 4 + y * 2 + core


def my_place():
    row = lax.axis_index("row")
    return row // 4, (row // 2) % 2, row % 2, lax.axis_index("col")


def maybe(cond, act):
    if cond is None:
        act()
    else:
        pl.when(cond)(act)


def remote(src, dst, send, recv, device):
    return pltpu.make_async_remote_copy(
        src_ref=src, dst_ref=dst, send_sem=send, recv_sem=recv, device_id=device, device_id_type=MESH
    )


def greet(always, z, up, down):
    barrier = pltpu.get_barrier_semaphore()

    def hello(device):
        pl.semaphore_signal(barrier, inc=1, device_id=device, device_id_type=MESH)

    for device in always:
        hello(device)
    pl.when(z < DEPTH - 1)(lambda: hello(up))
    pl.when(z > 0)(lambda: hello(down))
    pl.semaphore_wait(
        barrier, len(always) + (z < DEPTH - 1).astype(jnp.int32) + (z > 0).astype(jnp.int32)
    )


def tree_rounds(order):
    rounds = {}
    for dz in (0, -1, 1, -2, 2, -3, 3):
        for dy in (0, 1):
            for dx in (0, 1):
                step = {"z": dz, "y": dy, "x": dx}
                via = None
                for axis in order:
                    if step[axis]:
                        via = axis
                onward = []
                open_now = via is None
                for axis in order:
                    if axis == via:
                        open_now = True
                    if not open_now:
                        continue
                    if axis == "z":
                        onward += ["up"] if dz <= 0 else []
                        onward += ["down"] if dz >= 0 else []
                    elif axis != via:
                        onward.append(axis)
                onward.append("core")
                rounds.setdefault(abs(dz) + dy + dx, []).append((dz, dy, dx, onward))
    return rounds


def pieces_of(widths, cuts):
    found = []
    for part in range(3):
        base = 0
        for weight, width in enumerate(widths):
            lo = max(base, cuts[part])
            hi = min(base + width, cuts[part + 1])
            if hi > lo:
                found.append((part, weight, lo - cuts[part], lo - base, hi - lo))
            base += width
    return found


class Gatherer:
    def __init__(self, place, shards, widths, cuts, scratch):
        self.z, self.y, self.core, self.x = place
        z, y, core, x = place
        self.shards, self.widths = shards, widths
        self.bufs = scratch[:3]
        self.send, self.recv, self.local = scratch[3:]
        self.near = {
            "up": (row_of(z + 1, y, core), x),
            "down": (row_of(z - 1, y, core), x),
            "y": (row_of(z, 1 - y, core), x),
            "x": (row_of(z, y, core), 1 - x),
            "core": (row_of(z, y, 1 - core), x),
        }
        self.has = {"up": z < DEPTH - 1, "down": z > 0}
        self.pieces = pieces_of(widths, cuts)
        self.trees = [tree_rounds(order) for order in ORDERS]

    SCRATCH = 6

    @staticmethod
    def scratch_shapes(cuts, rows):
        dma = pltpu.SemaphoreType.DMA
        return [pltpu.VMEM((2, 16, rows, cuts[i + 1] - cuts[i]), bf16) for i in range(3)] + [
            dma((3, 16, 5)),
            dma((3, 32)),
            dma((3, 6)),
        ]

    def loads(self):
        row = row_of(self.z, self.y, self.core)
        return [
            pltpu.make_async_copy(
                self.shards[weight].at[:, pl.ds(src, width)],
                self.bufs[part].at[self.x, row, :, pl.ds(at, width)],
                self.local.at[0, i],
            )
            for i, (part, weight, at, src, width) in enumerate(self.pieces)
        ]

    def copy(self, part, bz, by, bc, bx, way):
        block = self.bufs[part].at[bx, row_of(bz, by, bc)]
        return remote(
            block,
            block,
            self.send.at[part, bx * 8 + bz * 2 + by, WAYS.index(way)],
            self.recv.at[part, bx * 16 + row_of(bz, by, bc)],
            self.near[way],
        )

    def each(self, step, act):
        for part in range(3):
            for dz, dy, dx, onward in self.trees[part].get(step, []):
                bz, by, bx = self.z + dz, (self.y + dy) % 2, (self.x + dx) % 2
                cond = None if dz == 0 else ((bz >= 0) & (bz <= DEPTH - 1))
                maybe(cond, lambda: act(part, bz, by, bx, onward))

    def forward(self, step):
        def act(part, bz, by, bx, onward):
            if step:
                self.copy(part, bz, by, self.core, bx, "core").wait_recv()
            for way in onward:
                maybe(self.has.get(way), lambda way=way: self.copy(part, bz, by, self.core, bx, way).start())

        self.each(step, act)

    def arrive(self):
        def act(part, bz, by, bx, onward):
            self.copy(part, bz, by, 1 - self.core, bx, "core").wait_recv()

        for step in range(6):
            self.each(step, act)

    def drain(self):
        def act(part, bz, by, bx, onward):
            for way in onward:
                maybe(self.has.get(way), lambda way=way: self.copy(part, bz, by, self.core, bx, way).wait_send())

        for step in range(6):
            self.each(step, act)

    def stores(self, outs):
        return [
            pltpu.make_async_copy(
                self.bufs[part].at[side, :, :, pl.ds(at, width)],
                outs[weight].at[:, :, pl.ds(side * self.widths[weight] + src, width)],
                self.local.at[1 + side, i],
            )
            for i, (part, weight, at, src, width) in enumerate(self.pieces)
            for side in range(2)
        ]

    def weight(self, part, side, at, width):
        block = self.bufs[part][side, :, :, at : at + width]
        return block.reshape(-1, width)


def begin(copies):
    for copy in copies:
        copy.start()


def end(copies):
    for copy in copies:
        copy.wait()


FORWARD_ORDER = (0, 3, 1, 4, 2, 5)
ROWS = 256


def front_kernel(shape, *refs):
    (w_qkv, w_out, w_fc, w_proj, x_in, cot, vectors, starts, kinds) = refs[:9]
    (
        o_qkv, o_out, o_fc, o_proj, o_x, o_cot, o_vec, o_packed, o_p, o_inv, o_att, o_normed, o_middle, o_second,
        o_active, o_slope,
    ) = refs[9:25]
    scr = refs[25:]
    n = Gatherer.SCRATCH
    place = my_place()
    z, y, core, x = place
    one, two, three = (
        Gatherer(place, shards, *shape["groups"][i], scr[n * i : n * (i + 1)])
        for i, shards in enumerate(([w_qkv], [w_out, w_fc], [w_proj]))
    )
    (
        xm, xo, cm, xf, n1, pk, pb, ib, att, bias, mid, n2, act_buf, slope_buf, vec_o, s_x, r_x, s_c, r_c, s_v, r_v,
        s_in, s_pair, s_end,
    ) = scr[3 * n :]
    length, half_width = xm.shape
    width = 2 * half_width
    half = length // 2
    blocks = length // ROWS
    to_x = one.near["x"]

    def x_copy(i):
        span = pl.ds(i * ROWS, ROWS)
        return remote(x_in.at[1 - x, span], xo.at[span], s_x.at[i], r_x.at[i], to_x)

    cot_copy = remote(cot.at[1 - x], o_cot.at[:, pl.ds(pl.multiple_of(x * half_width, PAIR), half_width)], s_c, r_c, to_x)
    vec_copy = remote(vectors, vec_o, s_v, r_v, to_x)
    own_x = pltpu.make_async_copy(x_in.at[x], xm, s_in.at[0])
    own_cot = pltpu.make_async_copy(cot.at[x], cm, s_in.at[1])
    put_cot = pltpu.make_async_copy(
        cm, o_cot.at[:, pl.ds(pl.multiple_of(x * half_width, PAIR), half_width)], s_in.at[2]
    )
    begin(one.loads())
    own_x.start()
    begin(two.loads())
    begin(three.loads())
    own_cot.start()
    greet([to_x, one.near["y"], one.near["core"]], z, one.near["up"], one.near["down"])
    vec_copy.start()
    end(one.loads())
    one.forward(0)
    begin([x_copy(i) for i in range(blocks)])
    for part in range(2):
        bias[part] = half_bias(starts[x, 0, part], kinds[x, 0, part], part, half)
    one.forward(1)
    end(two.loads())
    end(three.loads())
    one.forward(2)
    two.forward(0)
    vec_copy.wait()
    is_low = x == 0
    at = 0
    full = []
    for size in shape["vectors"]:
        mine, other = vectors[:, at : at + size], vec_o[:, at : at + size]
        low, high = jnp.where(is_low, mine, other), jnp.where(is_low, other, mine)
        o_vec[:, 2 * at : 2 * at + size] = low
        o_vec[:, 2 * at + size : 2 * at + 2 * size] = high
        full.append(slice(2 * at, 2 * at + 2 * size))
        at += size
    own_x.wait()

    def norm(value, gain, shift):
        average = jnp.sum(value, axis=1, keepdims=True) / width
        square = jnp.sum(value * value, axis=1, keepdims=True) / width
        inverse = lax.rsqrt(square - average * average + epsilon)
        return ((value - average) * inverse * o_vec[:, full[gain]] + o_vec[:, full[shift]]).astype(bf16)

    one.forward(3)
    for i in range(blocks):
        span = slice(i * ROWS, (i + 1) * ROWS)
        x_copy(i).wait_recv()
        mine, other = xm[span, :], xo[span, :]
        xf[span, :half_width] = jnp.where(is_low, mine, other)
        xf[span, half_width:] = jnp.where(is_low, other, mine)
        n1[span, :] = norm(xf[span, :].astype(f32), 0, 1)
    to_x_out = pltpu.make_async_copy(xf, o_x, s_end.at[0])
    to_normed = pltpu.make_async_copy(n1, o_normed, s_end.at[1])
    begin([to_x_out, to_normed])
    one.forward(4)
    one.forward(5)
    one.arrive()

    def pair_puts(step):
        j = FORWARD_ORDER[step]
        slot = step % 2
        return [
            pltpu.make_async_copy(pk.at[slot], o_packed.at[:, pl.ds(3 * PAIR * j, 3 * PAIR)], s_pair.at[slot, 0]),
            pltpu.make_async_copy(pb.at[slot], o_p.at[j], s_pair.at[slot, 1]),
            pltpu.make_async_copy(ib.at[slot], o_inv.at[:, pl.ds(PAIR * j, PAIR)], s_pair.at[slot, 2]),
        ]

    def pair(step):
        j = FORWARD_ORDER[step]
        slot = step % 2
        if step >= 2:
            end(pair_puts(step - 2))
        value = nn(n1[...], one.weight(j % 3, j // 3, 0, 3 * PAIR))
        cols = slice(PAIR * j, PAIR * (j + 1))
        shift = jnp.concatenate(
            [
                o_vec[:, full[2]][:, cols],
                jnp.zeros((1, PAIR), f32),
                o_vec[:, full[3]][:, cols],
            ],
            axis=1,
        )
        pk[slot] = (value + shift).astype(bf16)
        attend_pair(pk.at[slot], att.at[:, cols], pb.at[slot], ib.at[slot], bias)
        begin(pair_puts(step))

    qkv_stores = one.stores([o_qkv])
    begin(qkv_stores)
    pair(0)
    two.forward(1)
    pair(1)
    two.forward(2)
    three.forward(0)
    pair(2)
    two.forward(3)
    pair(3)
    two.forward(4)
    three.forward(1)
    own_cot.wait()
    put_cot.start()
    pair(4)
    two.forward(5)
    three.forward(2)
    cot_copy.start()
    pair(5)
    three.forward(3)
    two.arrive()
    two_stores = two.stores([o_out, o_fc])
    begin(two_stores)
    end(pair_puts(4))
    end(pair_puts(5))
    to_att = pltpu.make_async_copy(att, o_att, s_end.at[2])
    to_att.start()
    out_pieces = [p for p in two.pieces if p[1] == 0]
    fc_pieces = [p for p in two.pieces if p[1] == 1]
    for i in range(blocks):
        span = slice(i * ROWS, (i + 1) * ROWS)
        total = xf[span, :].astype(f32) + o_vec[:, full[4]]
        for part, _, at, src, w in out_pieces:
            for side in range(2):
                cols = slice(side * half_width + src, side * half_width + src + w)
                total = total + nt(att[span, cols], two.weight(part, side, at, w))
        mid[span, :] = total
        n2[span, :] = norm(total, 5, 6)
    to_mid = pltpu.make_async_copy(mid, o_middle, s_end.at[3])
    to_second = pltpu.make_async_copy(n2, o_second, s_end.at[4])
    begin([to_mid, to_second])
    three.forward(4)
    ff_half = two.widths[1]
    puts = []
    for k, ((part, _, at, src, w), side) in enumerate([(p, side) for p in fc_pieces for side in range(2)]):
        cols = slice(side * ff_half + src, side * ff_half + src + w)
        b_cols = slice(full[7].start + cols.start, full[7].start + cols.stop)

        def block(i, carry):
            span = pl.ds(pl.multiple_of(i * ROWS, ROWS), ROWS)
            hidden = nn(n2[span, :], two.weight(part, side, at, w)) + o_vec[:, b_cols]
            squared = hidden * hidden
            tanh = jnp.tanh(hidden * (GELU_A + (GELU_A * GELU_B) * squared))
            gate = 0.5 + 0.5 * tanh
            act_buf[span, cols] = (hidden * gate).astype(bf16)
            inner = hidden * (GELU_A + (3.0 * GELU_A * GELU_B) * squared)
            slope_buf[span, cols] = (gate + inner * (0.5 - 0.5 * tanh * tanh)).astype(bf16)
            return carry

        lax.fori_loop(0, blocks, block, 0)
        now = [
            pltpu.make_async_copy(act_buf.at[:, cols], o_active.at[:, cols], s_end.at[5 + 2 * k]),
            pltpu.make_async_copy(slope_buf.at[:, cols], o_slope.at[:, cols], s_end.at[6 + 2 * k]),
        ]
        begin(now)
        puts += now
        if k == 1:
            three.forward(5)
    three.arrive()
    three_stores = three.stores([o_proj])
    begin(three_stores)
    one.drain()
    two.drain()
    three.drain()
    for i in range(blocks):
        x_copy(i).wait_send()
    cot_copy.wait()
    end([put_cot, to_x_out, to_normed, to_att, to_mid, to_second] + puts)
    end(qkv_stores)
    end(two_stores)
    end(three_stores)


def front_near(shards, x_in, cot, vectors, starts, kinds):
    rows = shards[0].shape[0]
    widths = [shard.shape[1] for shard in shards]
    _, length, half_width = x_in.shape
    width = 2 * half_width
    half = length // 2
    pairs = width // PAIR
    groups = [
        (widths[:1], [0, 3 * PAIR, 6 * PAIR, 9 * PAIR]),
        (widths[1:3], part_cuts(widths[1:3], *MIDDLE_CUT)),
        (widths[3:], part_cuts(widths[3:], *GATHER_CUT)),
    ]
    ff = 2 * widths[2]
    sizes = [v.shape[0] for v in vectors]
    shape = {"groups": groups, "vectors": sizes}
    dma = pltpu.SemaphoreType.DMA
    scratch = []
    for _, cuts in groups:
        scratch += Gatherer.scratch_shapes(cuts, rows)
    scratch += [
        pltpu.VMEM((length, half_width), bf16),
        pltpu.VMEM((length, half_width), bf16),
        pltpu.VMEM((length, half_width), bf16),
        pltpu.VMEM((length, width), bf16),
        pltpu.VMEM((length, width), bf16),
        pltpu.VMEM((2, length, 3 * PAIR), bf16),
        pltpu.VMEM((2, 2, 3, half, half), bf16),
        pltpu.VMEM((2, length, PAIR), f32),
        pltpu.VMEM((length, width), bf16),
        pltpu.VMEM((2, half, half), f32),
        pltpu.VMEM((length, width), f32),
        pltpu.VMEM((length, width), bf16),
        pltpu.VMEM((length, ff), bf16),
        pltpu.VMEM((length, ff), bf16),
        pltpu.VMEM((1, sum(sizes)), f32),
    ]
    scratch += [dma((4,)), dma((4,)), dma(()), dma(()), dma(()), dma(()), dma((3,)), dma((2, 3)), dma((20,))]
    any_space = pl.BlockSpec(memory_space=pl.ANY)
    vmem = pl.BlockSpec(memory_space=pltpu.VMEM)
    smem = pl.BlockSpec(memory_space=pltpu.SMEM)

    def out(dims, kind=bf16):
        return jax.ShapeDtypeStruct(dims, kind)

    outs = pl.pallas_call(
        lambda *refs: front_kernel(shape, *refs),
        in_specs=[any_space] * 6 + [vmem, smem, smem],
        out_specs=[any_space] * 6 + [vmem] + [any_space] * 9,
        out_shape=[out((16, rows, 2 * w)) for w in widths]
        + [
            out((length, width)),
            out((length, width)),
            out((1, 2 * sum(sizes)), f32),
            out((length, 3 * width)),
            out((pairs, 2, 3, half, half)),
            out((length, width), f32),
            out((length, width)),
            out((length, width)),
            out((length, width), f32),
            out((length, width)),
            out((length, ff)),
            out((length, ff)),
        ],
        scratch_shapes=scratch,
        compiler_params=pltpu.CompilerParams(
            collective_id=0, has_side_effects=True, vmem_limit_bytes=67043328
        ),
        cost_estimate=pl.CostEstimate(flops=20 << 30, bytes_accessed=200 << 20, transcendentals=0),
        name="gather_weights",
    )(*shards, x_in, cot, jnp.concatenate(vectors).reshape(1, -1), starts, kinds)
    full = [w.reshape(16 * rows, -1) for w in outs[:4]]
    vec = outs[6].reshape(-1)
    at = 0
    fulls = []
    for size in sizes:
        fulls.append(vec[at : at + 2 * size])
        at += 2 * size
    return full, list(outs[4:6]), fulls, list(outs[7:])


class Reducer:
    def __init__(self, place, grads, widths, cuts, scratch):
        self.z, self.y, self.core, self.x = place
        z, y, core, x = place
        self.grads = grads
        self.widths = widths
        self.acc, self.rcore = scratch[0:3], scratch[3:6]
        rx, ry, self.rz, self.cy, self.cx = scratch[6:8], scratch[8:10], scratch[10:13], scratch[13], scratch[14]
        self.final = scratch[15:18]
        (
            self.s_core, self.r_core, s_x, r_x, s_y, r_y, self.s_z, self.r_z, self.s_c, self.r_c, self.s_load,
            self.s_out,
        ) = scratch[18:]
        self.up, self.down = (row_of(z + 1, y, core), x), (row_of(z - 1, y, core), x)
        self.to_y, self.to_x = (row_of(z, 1 - y, core), x), (row_of(z, y, core), 1 - x)
        self.to_core = (row_of(z, y, 1 - core), x)
        self.by_part = [[p for p in pieces_of(widths, cuts) if p[0] == part] for part in range(3)]
        self.first = [(rx[0], s_x, r_x, self.to_x), (ry[0], s_y, r_y, self.to_y)]
        self.second = [(ry[1], s_y, r_y, self.to_y), (rx[1], s_x, r_x, self.to_x)]

    SCRATCH = 30

    @staticmethod
    def scratch_shapes(widths, cuts, rows):
        w = [cuts[i + 1] - cuts[i] for i in range(3)]
        dma = pltpu.SemaphoreType.DMA

        def low(*shape):
            return pltpu.VMEM(shape, bf16)

        scratch = [low(2, 4, 2, rows, k) for k in w] * 2
        scratch += [low(4, 2, rows, w[0]), low(4, rows, w[1])]
        scratch += [low(4, 2, rows, w[1]), low(4, rows, w[0])]
        scratch += [low(2, 4, rows, w[0]), low(2, 4, rows, w[1]), low(2, 4, 2, 2, rows, w[2])]
        scratch += [low(2, rows, w[2]), low(rows, w[2])]
        scratch += [pltpu.VMEM((rows, k), f32) for k in w]
        scratch += [dma((3, 2, 4, 2, 2)), dma((3, 2, 4, 2, 2)), dma((2, 4)), dma((2, 4)), dma((2, 4)), dma((2, 4))]
        scratch += [dma((3, 2, 4)), dma((3, 2, 4)), dma((2,)), dma((2,)), dma((3, 2, 2)), dma((3, 2))]
        return scratch

    def cols(self, weight, side, src, width):
        return pl.ds(pl.multiple_of(side * self.widths[weight] + src, 128), width)

    def loop(self, act):
        def step(zi, carry):
            act(zi)
            return carry

        lax.fori_loop(0, DEPTH, step, 0)

    def add(self, total, term):
        total[...] = total[...] + term[...]

    def loads(self, part):
        return [
            pltpu.make_async_copy(
                self.grads[weight].at[:, :, self.core, :, self.cols(weight, side, src, width)],
                self.acc[part].at[side, :, :, :, pl.ds(at, width)],
                self.s_load.at[part, side, i],
            )
            for i, (_, weight, at, src, width) in enumerate(self.by_part[part])
            for side in range(2)
        ]

    def view(self, part, ref, far, zi):
        if part == 0:
            return ref.at[(1 - self.x) if far else self.x, zi]
        return ref.at[:, zi, (1 - self.y) if far else self.y]

    def core_copies(self, part, far, zi):
        other = 1 - self.core
        copies = []
        for i, (_, weight, at, src, width) in enumerate(self.by_part[part]):
            cols = pl.ds(at, width)
            if part == 0:
                sides = [(1 - self.x) if far else self.x]
            else:
                sides = [0, 1]
            for k, side in enumerate(sides):
                gcols = self.cols(weight, side, src, width)
                if part == 1:
                    by = (1 - self.y) if far else self.y
                    src_ref = self.grads[weight].at[zi, by, other, :, gcols]
                    dst_ref = self.rcore[1].at[side, zi, by, :, cols]
                else:
                    src_ref = self.grads[weight].at[zi, :, other, :, gcols]
                    dst_ref = self.rcore[part].at[side, zi, :, :, cols]
                slot = (part, int(far), zi, i, k)
                copies.append(remote(src_ref, dst_ref, self.s_core.at[slot], self.r_core.at[slot], self.to_core))
        return copies

    def start(self, parts):
        for part in parts:
            for load in self.loads(part):
                load.start()

        def begin(far):
            def act(zi):
                for part in parts:
                    if far or part < 2:
                        for copy in self.core_copies(part, far, zi):
                            copy.start()

            self.loop(act)

        begin(True)
        begin(False)

    def first_copy(self, part, zi):
        buf, send, recv, device = self.first[part]
        return remote(self.view(part, self.acc[part], True, zi), buf.at[zi], send.at[0, zi], recv.at[0, zi], device)

    def half_of(self, part, zi, far):
        if part == 0:
            return self.acc[0].at[self.x, zi, (1 - self.y) if far else self.y]
        return self.acc[1].at[(1 - self.x) if far else self.x, zi, self.y]

    def second_copy(self, part, zi):
        buf, send, recv, device = self.second[part]
        return remote(self.half_of(part, zi, True), buf.at[zi], send.at[1, zi], recv.at[1, zi], device)

    def far(self, parts):
        for part in parts:
            for load in self.loads(part):
                load.wait()

        def act(zi):
            for part in parts:
                for copy in self.core_copies(part, True, zi):
                    copy.wait_recv()
                if part == 2:
                    self.add(self.acc[2].at[:, zi], self.rcore[2].at[:, zi])
                else:
                    self.add(self.view(part, self.acc[part], True, zi), self.view(part, self.rcore[part], True, zi))
                    self.first_copy(part, zi).start()

        self.loop(act)

    def near(self, parts):
        def act(zi):
            for part in parts:
                for copy in self.core_copies(part, False, zi):
                    copy.wait_recv()
                mine = self.view(part, self.acc[part], False, zi)
                self.add(mine, self.view(part, self.rcore[part], False, zi))
                self.first_copy(part, zi).wait_recv()
                self.add(mine, self.first[part][0].at[zi])
                self.second_copy(part, zi).start()

        self.loop(act)

    def last(self, parts):
        def act(zi):
            for part in parts:
                self.second_copy(part, zi).wait_recv()
                self.add(self.half_of(part, zi, False), self.second[part][0].at[zi])

        self.loop(act)

    def block(self, part, zi):
        if part == 2:
            return self.acc[2].at[:, zi]
        return self.acc[part].at[self.x, zi, self.y]

    def line_copy(self, part, direction, zd):
        return remote(
            self.block(part, zd),
            self.rz[part].at[direction, zd],
            self.s_z.at[part, direction, zd],
            self.r_z.at[part, direction, zd],
            self.down if direction else self.up,
        )

    def line(self, parts, step):
        for direction in range(2):
            at = DEPTH - 1 - step if direction else step
            for zd in (0, 1, 2) if direction else (3, 2, 1):
                if not ((at > zd) if direction else (at < zd)):
                    continue
                for part in parts:

                    def act(part=part, direction=direction, zd=zd):
                        if step > 0:
                            self.line_copy(part, direction, zd).wait_recv()
                            self.add(self.block(part, zd), self.rz[part].at[direction, zd])
                        self.line_copy(part, direction, zd).start()

                    pl.when(self.z == at)(act)

    def line_end(self, parts):
        for part in parts:
            for direction in range(2):

                def act(part=part, direction=direction):
                    self.line_copy(part, direction, self.z).wait_recv()
                    self.add(self.block(part, self.z), self.rz[part].at[direction, self.z])

                pl.when((self.z < DEPTH - 1) if direction else (self.z > 0))(act)

    def y_copy(self):
        return remote(self.acc[2].at[:, self.z, 1 - self.y], self.cy, self.s_c.at[0], self.r_c.at[0], self.to_y)

    def x_copy(self):
        return remote(self.acc[2].at[1 - self.x, self.z, self.y], self.cx, self.s_c.at[1], self.r_c.at[1], self.to_x)

    def turn(self):
        self.y_copy().wait_recv()
        self.add(self.acc[2].at[:, self.z, self.y], self.cy)
        self.x_copy().start()

    def turn_end(self):
        self.x_copy().wait_recv()
        self.add(self.acc[2].at[self.x, self.z, self.y], self.cx)

    def stores(self, outs):
        return [
            pltpu.make_async_copy(
                self.final[part].at[:, pl.ds(at, width)], outs[weight].at[:, pl.ds(src, width)], self.s_out.at[part, i]
            )
            for part in range(3)
            for i, (_, weight, at, src, width) in enumerate(self.by_part[part])
        ]

    def finish(self, outs):
        for part in range(3):
            self.final[part][...] = self.acc[part][self.x, self.z, self.y].astype(f32)
        for store in self.stores(outs):
            store.start()

    def drain(self, outs):
        def act(zi):
            for part in range(3):
                for copy in self.core_copies(part, True, zi):
                    copy.wait_send()
                if part < 2:
                    for copy in self.core_copies(part, False, zi):
                        copy.wait_send()
                    self.first_copy(part, zi).wait_send()
                    self.second_copy(part, zi).wait_send()

        self.loop(act)
        for part in range(3):
            for direction in range(2):
                for zd in range(DEPTH):
                    pl.when((self.z > zd) if direction else (self.z < zd))(
                        lambda part=part, direction=direction, zd=zd: self.line_copy(part, direction, zd).wait_send()
                    )
        self.y_copy().wait_send()
        self.x_copy().wait_send()
        for store in self.stores(outs):
            store.wait()


PAIR_ORDER = (2, 5, 0, 3, 1, 4)


def back_kernel(shape, *refs):
    (
        g_out, g_fc, g_proj, packed, attended, p_all, inv_all, gatt, normed_t, w_qkv, x_all, middle, gain_ref, small_in,
        o_qkv, o_out, o_fc, o_proj, o_sum, o_input,
    ) = refs[:20]
    scr = refs[20:]
    first = Reducer.SCRATCH
    place = my_place()
    z, y, core, x = place
    early = Reducer(place, [g_out, g_fc, g_proj], shape["early"], shape["early_cuts"], scr[:first])
    qkv, o_buf, p_buf, inv_buf, g_buf, nt_buf, w_buf, x_buf, m_buf, gqkv, gi, col_sum, srecv, sacc = scr[2 * first : 2 * first + 14]
    s_all, s_pair, s_mid, s_gi, r_gi, l_gi, s_s, r_s = scr[2 * first + 14 :]
    late = Reducer(place, [gqkv], shape["late"], shape["late_cuts"], scr[first : 2 * first])
    whole = [
        pltpu.make_async_copy(packed, qkv, s_all.at[0]),
        pltpu.make_async_copy(normed_t, nt_buf, s_all.at[1]),
        pltpu.make_async_copy(w_qkv, w_buf, s_all.at[2]),
        pltpu.make_async_copy(x_all, x_buf, s_all.at[3]),
    ]

    def pair_loads(step):
        j = PAIR_ORDER[step]
        slot = step % 2
        cols = pl.ds(j * PAIR, PAIR)
        return [
            pltpu.make_async_copy(p_all.at[j], p_buf.at[slot], s_pair.at[slot, 0]),
            pltpu.make_async_copy(attended.at[:, cols], o_buf.at[slot], s_pair.at[slot, 1]),
            pltpu.make_async_copy(inv_all.at[:, cols], inv_buf.at[slot], s_pair.at[slot, 2]),
            pltpu.make_async_copy(gatt.at[:, cols], g_buf.at[slot], s_pair.at[slot, 3]),
        ]

    def begin(copies):
        for copy in copies:
            copy.start()

    def end(copies):
        for copy in copies:
            copy.wait()

    begin(whole[:1])
    begin(pair_loads(0))
    begin(whole[1:])
    to_z1 = (row_of(z + 1 - 2 * (z % 2), y, core), x)
    to_z2 = (row_of((z + 2) % 4, y, core), x)
    greet([early.to_core, early.to_x, early.to_y, to_z2], z, early.up, early.down)
    early.start((0, 1, 2))
    end(whole[:1])

    def pair(step):
        j = PAIR_ORDER[step]
        slot = step % 2
        if step < 5:
            begin(pair_loads(step + 1))
        end(pair_loads(step))
        attend_back_pair(qkv, o_buf.at[slot], p_buf.at[slot], inv_buf.at[slot], g_buf.at[slot], col_sum.at[j], 3 * PAIR * j)
        if step == 0:
            end(whole[1:2])
        cols = slice(3 * PAIR * j, 3 * PAIR * (j + 1))
        grad = nn(nt_buf[...], qkv[:, cols]).astype(bf16)
        gqkv[:, :, :, :, cols] = grad.reshape(gqkv.shape[:4] + (3 * PAIR,))

    rows = m_buf.shape[1]
    blocks = x_buf.shape[0] // rows

    def mid_load(i):
        return pltpu.make_async_copy(middle.at[pl.ds(i * rows, rows)], m_buf.at[i % 2], s_mid.at[i % 2])

    def input_copies(i):
        span = pl.ds(i * rows, rows)
        return (
            pltpu.make_async_copy(gi.at[0, span], o_input.at[x, span], l_gi.at[i]),
            remote(gi.at[1, span], o_input.at[x, span], s_gi.at[i], r_gi.at[i], early.to_x),
        )

    sums = [None, None]

    def input_block(i):
        span = slice(i * rows, (i + 1) * rows)
        grad = nt(qkv[span, :], w_buf[...])
        if i + 1 < blocks:
            mid_load(i + 1).start()
        mid_load(i).wait()
        value = x_buf[span, :].astype(f32)
        width = value.shape[1]
        average = jnp.sum(value, axis=1, keepdims=True) / width
        square = jnp.sum(value * value, axis=1, keepdims=True) / width
        inverse = lax.rsqrt(square - average * average + epsilon)
        centred = (value - average) * inverse
        scaled = grad * gain_ref[...]
        one = jnp.sum(scaled, axis=1, keepdims=True) / width
        two = jnp.sum(scaled * centred, axis=1, keepdims=True) / width
        out = m_buf[i % 2] + inverse * (scaled - one - centred * two)
        for k, term in enumerate((grad * centred, grad)):
            term = jnp.sum(term, axis=0, keepdims=True)
            sums[k] = term if sums[k] is None else sums[k] + term
        half = width // 2
        is_low = x == 0
        gi[0, span, :] = jnp.where(is_low, out[:, :half], out[:, half:]).astype(bf16)
        gi[1, span, :] = jnp.where(is_low, out[:, half:], out[:, :half]).astype(bf16)
        for copy in input_copies(i):
            copy.start()

    partners = [early.to_core, early.to_x, early.to_y, to_z1, to_z2]

    def small_copy(step):
        return remote(sacc.at[step], srecv.at[step], s_s.at[step], r_s.at[step], partners[step])

    def small_start():
        sacc[0] = small_in[...]
        at = 0
        for k in range(2):
            for i in range(6):
                sacc[0, at : at + 1, :] = sums[k][:, i * PAIR : (i + 1) * PAIR]
                at += 1
        for k in range(2):
            for i in range(6):
                sacc[0, at : at + 1, :] = col_sum[i, k]
                at += 1
        small_copy(0).start()

    def small_next(step):
        small_copy(step).wait()
        sacc[step + 1] = sacc[step] + srecv[step]
        if step < 4:
            small_copy(step + 1).start()

    both = (0, 1)
    pair(0)
    early.far((0, 1, 2))
    early.line((2,), 0)
    pair(1)
    late.start((2,))
    early.line((2,), 1)
    pair(2)
    early.line((2,), 2)
    late.far((2,))
    late.line((2,), 0)
    pair(3)
    late.start((0,))
    early.near(both)
    early.line_end((2,))
    early.y_copy().start()
    late.line((2,), 1)
    pair(4)
    late.far((0,))
    early.turn()
    late.line((2,), 2)
    mid_load(0).start()
    pair(5)
    late.start((1,))
    early.last(both)
    early.line(both, 0)
    late.line_end((2,))
    late.y_copy().start()
    early.turn_end()
    end(whole[2:])
    input_block(0)
    late.far((1,))
    early.line(both, 1)
    late.turn()
    late.near((0,))
    input_block(1)
    early.line(both, 2)
    late.turn_end()
    late.near((1,))
    input_block(2)
    late.last((0,))
    late.line((0,), 0)
    input_block(3)
    small_start()
    early.line_end(both)
    early.finish([o_out, o_fc, o_proj])
    late.last((1,))
    late.line((1,), 0)
    small_next(0)
    late.line(both, 1)
    small_next(1)
    late.line(both, 2)
    small_next(2)
    late.line_end(both)
    late.finish([o_qkv])
    small_next(3)
    small_next(4)
    o_sum[...] = sacc[5]
    for i in range(blocks):
        local, other = input_copies(i)
        local.wait()
        other.wait()
    early.drain([o_out, o_fc, o_proj])
    late.drain([o_qkv])


def back_near(grads, packed, attended, p, inv, gatt, normed_t, w_qkv, x, middle, gain, small, rows):
    length, width = x.shape
    wide = packed.shape[1]
    early = [grad.shape[1] // 2 for grad in grads]
    shape = {"early": early, "early_cuts": part_cuts(early, *REDUCE_CUT), "late": [wide // 2]}
    shape["late_cuts"] = [0, wide // 6, wide // 3, wide // 2]
    dma = pltpu.SemaphoreType.DMA
    half = length // 2
    blocks = 4
    scratch = Reducer.scratch_shapes(early, shape["early_cuts"], rows)
    scratch += Reducer.scratch_shapes(shape["late"], shape["late_cuts"], rows)
    scratch += [
        pltpu.VMEM((length, wide), bf16),
        pltpu.VMEM((2, length, PAIR), bf16),
        pltpu.VMEM((2, 2, 3, half, half), bf16),
        pltpu.VMEM((2, length, PAIR), f32),
        pltpu.VMEM((2, length, PAIR), bf16),
        pltpu.VMEM((width, length), bf16),
        pltpu.VMEM((width, wide), bf16),
        pltpu.VMEM((length, width), bf16),
        pltpu.VMEM((2, length // blocks, width), f32),
        pltpu.VMEM((4, 2, 2, rows, wide), bf16),
        pltpu.VMEM((2, length, width // 2), bf16),
        pltpu.VMEM((width // PAIR, 2, 1, PAIR), f32),
        pltpu.VMEM((5,) + small.shape, f32),
        pltpu.VMEM((6,) + small.shape, f32),
    ]
    scratch += [dma((4,)), dma((2, 4)), dma((2,)), dma((4,)), dma((4,)), dma((4,)), dma((5,)), dma((5,))]
    shaped = [grad.reshape(4, 2, 2, rows, grad.shape[1]) for grad in grads]
    any_space = pl.BlockSpec(memory_space=pl.ANY)
    vmem = pl.BlockSpec(memory_space=pltpu.VMEM)
    outs = pl.pallas_call(
        lambda *refs: back_kernel(shape, *refs),
        in_specs=[any_space] * 12 + [vmem, vmem],
        out_specs=[any_space] * 4 + [vmem, any_space],
        out_shape=[jax.ShapeDtypeStruct((rows, w), f32) for w in [wide // 2] + early]
        + [jax.ShapeDtypeStruct(small.shape, f32), jax.ShapeDtypeStruct((2, length, width // 2), bf16)],
        scratch_shapes=scratch,
        compiler_params=pltpu.CompilerParams(
            collective_id=1, has_side_effects=True, vmem_limit_bytes=67043328
        ),
        cost_estimate=pl.CostEstimate(flops=30 << 30, bytes_accessed=200 << 20, transcendentals=0),
        name="reduce_grads",
    )(*shaped, packed, attended, p, inv, gatt, normed_t, w_qkv, x, middle, gain.reshape(1, -1), small)
    return outs


def gather_far(shards):
    fulls = []
    for shard in shards:
        rows = lax.all_gather(shard, ("col", "row"), axis=0, tiled=True)
        fulls.append(jnp.concatenate(jnp.split(rows, 2, axis=0), axis=1))
    return fulls


def reduce_far(grads, small):
    outs = []
    for grad in grads:
        halves = jnp.concatenate(jnp.split(grad, 2, axis=1), axis=0)
        outs.append(lax.psum_scatter(halves, ("col", "row"), scatter_dimension=0, tiled=True).astype(f32))
    return outs, lax.psum(small, ("row", "col"))


def part_cuts(widths, first, second):
    total = sum(widths) // 128
    one = round(total * first)
    two = round(total * (first + second))
    return [0, one * 128, two * 128, total * 128]


def layer_norm(value):
    width = value.shape[-1]
    average = jnp.sum(value, axis=-1, keepdims=True) / width
    square = jnp.sum(value * value, axis=-1, keepdims=True) / width
    inverse = lax.rsqrt(square - average * average + epsilon)
    return (value - average) * inverse, inverse


def norm_backward(grad, centred, inverse, gain):
    scaled = grad * gain
    first = jnp.mean(scaled, axis=-1, keepdims=True)
    second = jnp.mean(scaled * centred, axis=-1, keepdims=True)
    back = inverse * (scaled - first - centred * second)
    return back, jnp.sum(grad * centred, axis=0), jnp.sum(grad, axis=0)


def by_pairs(block):
    rows, three, half = block.shape
    return block.reshape(rows, three, half // PAIR, PAIR).transpose(0, 2, 1, 3).reshape(rows, three * half)


def body(
    near, x_in, span_start, span_kind, ln1_gain, ln1_bias, w_qkv, b_query, b_value, w_out, b_out,
    ln2_gain, ln2_bias, w_fc, b_fc, w_proj, b_proj, cotangent,
):
    half_width = x_in.shape[2]
    shard = w_qkv.shape[0]
    col = lax.axis_index("col")

    vectors = [ln1_gain, ln1_bias, b_query, b_value, b_out, ln2_gain, ln2_bias, b_fc, b_proj]
    shards = [by_pairs(w_qkv), w_out.T, w_fc, w_proj.T]
    width = 2 * half_width
    if near:
        weights, (x_own, grad_out), vectors, saved = front_near(shards, x_in, cotangent, vectors, span_start, span_kind)
        qkv_all, out_all, fc_all, proj_all = weights
        ln1_gain, _, _, _, _, ln2_gain, _, _, b_proj = vectors
        packed, p, inv, attended, normed_first, middle, normed_second, active, slope = saved
        centred_second, inverse_second = layer_norm(middle)
    else:
        x_own = own_micro(x_in)
        residual = x_own.astype(f32)
        grad_out = own_micro(cotangent)
        qkv_all, out_all, fc_all, proj_all = gather_far(shards)
        flat = jnp.concatenate(vectors)
        flat_other = swap(flat)
        full = []
        at = 0
        for vector in vectors:
            full.append(ordered(vector, flat_other[at : at + vector.shape[0]], 0))
            at += vector.shape[0]
        ln1_gain, ln1_bias, b_query, b_value, b_out, ln2_gain, ln2_bias, b_fc, b_proj = full
        starts = lax.dynamic_index_in_dim(span_start, col, 0, keepdims=False)[0]
        kinds = lax.dynamic_index_in_dim(span_kind, col, 0, keepdims=False)[0]
        spans = jnp.stack([starts, kinds])
        centred_first, inverse_first = layer_norm(residual)
        normed_first = (centred_first * ln1_gain + ln1_bias).astype(bf16)
        bias = jnp.stack([b_query, jnp.zeros_like(b_query), b_value]).reshape(3, -1, PAIR)
        packed = (nn(normed_first, qkv_all) + bias.transpose(1, 0, 2).reshape(-1)).astype(bf16)
        attended, p, inv = attend_forward(packed, spans)
        middle = residual + nt(attended, out_all) + b_out
        centred_second, inverse_second = layer_norm(middle)
        normed_second = (centred_second * ln2_gain + ln2_bias).astype(bf16)
        hidden = nn(normed_second, fc_all) + b_fc
        squared = hidden * hidden
        tanh = jnp.tanh(GELU_A * hidden * (1.0 + GELU_B * squared))
        active = (0.5 * hidden * (1.0 + tanh)).astype(bf16)
        slope = (
            0.5 * (1.0 + tanh)
            + 0.5 * hidden * (1.0 - tanh * tanh) * GELU_A * (1.0 + 3.0 * GELU_B * squared)
        ).astype(bf16)
    layer_out = back_micro((middle + nt(active, proj_all) + b_proj).astype(bf16))

    grad_out_wide = grad_out.astype(f32)
    g_proj = tn(grad_out, active).astype(bf16)
    grad_hidden = (nn(grad_out, proj_all) * slope.astype(f32)).astype(bf16)
    g_fc = tn(normed_second, grad_hidden).astype(bf16)
    g_bfc = jnp.sum(grad_hidden.astype(f32), axis=0)
    grad_normed = nt(grad_hidden, fc_all)
    back, g_ln2_gain, g_ln2_bias = norm_backward(grad_normed, centred_second, inverse_second, ln2_gain)
    grad_middle = grad_out_wide + back
    g_bproj = jnp.sum(grad_out_wide, axis=0)
    g_bout = jnp.sum(grad_middle, axis=0)
    grad_low = grad_middle.astype(bf16)
    g_out = tn(grad_low, attended).astype(bf16)
    grad_attended = nn(grad_low, out_all).astype(bf16)
    zeros = jnp.zeros((width,), f32)
    small = [zeros, zeros, zeros, zeros, g_bout, g_ln2_gain, g_ln2_bias, g_bfc, g_bproj]
    if near:
        flat = jnp.concatenate(small).reshape(-1, 128)
        *outs, summed, grad_input = back_near(
            [g_out, g_fc, g_proj], packed, attended, p, inv, grad_attended, normed_first.T, qkv_all,
            x_own, grad_middle, ln1_gain, flat, shard,
        )
    else:
        grad_packed, sums = attend_backward(packed, attended, p, inv, grad_attended)
        g_qkv = tn(normed_first, grad_packed).astype(bf16)
        grad_normed = nt(grad_packed, qkv_all)
        back, g_ln1_gain, g_ln1_bias = norm_backward(grad_normed, centred_first, inverse_first, ln1_gain)
        grad_input = back_micro((grad_middle + back).astype(bf16))
        small[:4] = [g_ln1_gain, g_ln1_bias, sums[:, 0, 0].reshape(-1), sums[:, 1, 0].reshape(-1)]
        outs, summed = reduce_far([g_qkv, g_out, g_fc, g_proj], jnp.concatenate(small))
    out_qkv, out_out, out_fc, out_proj = outs
    summed = summed.reshape(-1)
    kept = []
    at = 0
    for vector in small:
        size = vector.shape[0] // 2
        kept.append(lax.dynamic_slice_in_dim(summed, at + col * size, size, 0))
        at += vector.shape[0]
    return (
        layer_out,
        grad_input,
        kept[0],
        kept[1],
        out_qkv.reshape(shard, -1, 3, PAIR).transpose(0, 2, 1, 3).reshape(shard, 3, half_width),
        kept[2],
        kept[3],
        out_out.T,
        kept[4],
        kept[5],
        kept[6],
        out_fc,
        kept[7],
        out_proj.T,
        kept[8],
    )


def solution(mesh):
    placed = (
        P(None, "row", "col"), P(None, "row", None), P(None, "row", None), P("col"), P("col"),
        P("row", None, "col"), P("col"), P("col"), P("col", "row"), P("col"), P("col"), P("col"),
        P("row", "col"), P("col"), P("col", "row"), P("col"), P(None, "row", "col"),
    )
    near = mesh.shape["row"] == 16
    return jax.shard_map(
        partial(body, near),
        mesh=mesh,
        in_specs=placed,
        out_specs=(
            P(None, "row", "col"), P(None, "row", "col"), P("col"), P("col"), P("row", None, "col"),
            P("col"), P("col"), P("col", "row"), P("col"), P("col"), P("col"), P("row", "col"),
            P("col"), P("col", "row"), P("col"),
        ),
        check_vma=False,
    )
```

```python
from functools import partial

import jax
import jax.numpy as jnp
from jax import lax
from jax.experimental import pallas as pl
from jax.experimental.pallas import tpu as pltpu
from jax.sharding import PartitionSpec as P

HEAD = 64
IMG = 256
epsilon = 1e-05
bf16 = jnp.bfloat16
f32 = jnp.float32
GELU_A = 0.7978845608028654
GELU_B = 0.044715
PAIR = 2 * HEAD


def nn(a, b):
    return lax.dot_general(a, b, (((1,), (0,)), ((), ())), preferred_element_type=f32)


def nt(a, b):
    return lax.dot_general(a, b, (((1,), (1,)), ((), ())), preferred_element_type=f32)


def tn(a, b):
    return lax.dot_general(a, b, (((0,), (0,)), ((), ())), preferred_element_type=f32)


def half_bias(start, kind, part, half):
    base = part * half
    rows = lax.broadcasted_iota(jnp.int32, (half, half), 0) + base
    cols = lax.broadcasted_iota(jnp.int32, (half, half), 1) + base
    first = jnp.where(kind == 1, start, 4 * half)
    joined = (rows >= first) & (rows < first + IMG) & (cols >= first) & (cols < first + IMG)
    return jnp.where((cols <= rows) | joined, 0.0, -1e30).astype(f32)


def lane_masks(rows):
    lane = lax.broadcasted_iota(jnp.int32, (rows, PAIR), 1)
    return lane < HEAD


def attend_pair(qkv_ref, o_ref, p_ref, inv_ref, bias_ref):
    half = qkv_ref.shape[0] // 2
    q_ref, k_ref, v_ref = (qkv_ref.at[:, i * PAIR : (i + 1) * PAIR] for i in range(3))
    low = lane_masks(half)
    for part in range(2):
        rows = slice(part * half, (part + 1) * half)
        q = q_ref[rows, :] * jnp.asarray(0.125, bf16)
        zero = jnp.zeros_like(q)
        outs = []
        invs = []
        for head in range(2):
            mine = low if head == 0 else jnp.logical_not(low)
            qh = jnp.where(mine, q, zero)
            own = nt(qh, k_ref[rows, :]) + bias_ref[part]
            largest = jnp.max(own, axis=1, keepdims=True)
            if part == 1:
                before = nt(qh, k_ref[:half, :])
                largest = jnp.maximum(largest, jnp.max(before, axis=1, keepdims=True))
            own = jnp.exp(own - largest)
            total = jnp.sum(own, axis=1, keepdims=True)
            own = own.astype(bf16)
            p_ref[head, 2 * part] = own
            out = nn(own, v_ref[rows, :])
            if part == 1:
                before = jnp.exp(before - largest)
                total = total + jnp.sum(before, axis=1, keepdims=True)
                before = before.astype(bf16)
                p_ref[head, 1] = before
                out = out + nn(before, v_ref[:half, :])
            inv = 1.0 / total
            outs.append(out * inv)
            invs.append(inv)
        o_ref[rows, :] = jnp.where(low, outs[0], outs[1]).astype(bf16)
        inv_ref[rows, :] = jnp.where(low, invs[0], invs[1])


def attend_forward_kernel(span_ref, qkv_ref, o_ref, p_ref, inv_ref, bias_ref):
    half = qkv_ref.shape[0] // 2

    @pl.when(pl.program_id(0) == 0)
    def _():
        for part in range(2):
            bias_ref[part] = half_bias(span_ref[0, part], span_ref[1, part], part, half)

    attend_pair(qkv_ref, o_ref, p_ref.at[0], inv_ref, bias_ref)


def attend_forward(packed, spans):
    length = packed.shape[0]
    width = packed.shape[1] // 3
    pairs = width // PAIR
    half = length // 2
    return pl.pallas_call(
        attend_forward_kernel,
        grid=(pairs,),
        in_specs=[
            pl.BlockSpec(memory_space=pltpu.SMEM),
            pl.BlockSpec((length, 3 * PAIR), lambda j: (0, j)),
        ],
        out_specs=[
            pl.BlockSpec((length, PAIR), lambda j: (0, j)),
            pl.BlockSpec((1, 2, 3, half, half), lambda j: (j, 0, 0, 0, 0)),
            pl.BlockSpec((length, PAIR), lambda j: (0, j)),
        ],
        out_shape=[
            jax.ShapeDtypeStruct((length, width), bf16),
            jax.ShapeDtypeStruct((pairs, 2, 3, half, half), bf16),
            jax.ShapeDtypeStruct((length, width), f32),
        ],
        scratch_shapes=[pltpu.VMEM((2, half, half), f32)],
        compiler_params=pltpu.CompilerParams(vmem_limit_bytes=60 << 20),
        cost_estimate=pl.CostEstimate(
            flops=4 * 3 * half * half * width * 4, bytes_accessed=24 << 20, transcendentals=3 * half * half * 12
        ),
        name="attend_forward",
    )(spans, packed)


def attend_back_pair(qkv_ref, o_ref, p_ref, inv_ref, g_ref, sum_ref, at):
    length = qkv_ref.shape[0]
    half = length // 2
    low = lane_masks(half)
    q_ref, k_ref, v_ref = (qkv_ref.at[:, at + i * PAIR : at + (i + 1) * PAIR] for i in range(3))
    dks = [None, None]
    dvs = [None, None]
    dqs = []

    def add(total, part, value):
        total[part] = value if total[part] is None else total[part] + value

    for part in range(2):
        rows = slice(part * half, (part + 1) * half)
        inv = inv_ref[rows, :]
        g = g_ref[rows, :].astype(f32) * inv
        scaled = g * o_ref[rows, :].astype(f32)
        q = q_ref[rows, :]
        gb = g.astype(bf16)
        zero = jnp.zeros_like(gb)
        dq = None
        for head in range(2):
            mine = low if head == 0 else jnp.logical_not(low)
            gh = jnp.where(mine, gb, zero)
            qh = jnp.where(mine, q, zero)
            rowdot = jnp.sum(jnp.where(mine, scaled, 0.0), axis=1, keepdims=True)
            for kpart in range(part + 1):
                krows = slice(kpart * half, (kpart + 1) * half)
                p = p_ref[head, part + kpart]
                kh = jnp.where(mine, k_ref[krows, :], zero)
                dp = nt(gh, v_ref[krows, :])
                ds = (p.astype(f32) * (dp - rowdot)).astype(bf16)
                term = nn(ds, kh)
                dq = term if dq is None else dq + term
                add(dks, kpart, tn(ds, qh))
                add(dvs, kpart, tn(p, gh))
        dqs.append(dq)
    for which, (ref, values, scale) in enumerate(((q_ref, dqs, 0.125), (k_ref, dks, 0.125), (v_ref, dvs, 1.0))):
        total = None
        for part in range(2):
            value = (values[part] * scale).astype(bf16)
            ref[part * half : (part + 1) * half, :] = value
            term = jnp.sum(value.astype(f32), axis=0, keepdims=True)
            total = term if total is None else total + term
        if which != 1:
            sum_ref[which // 2] = total


def attend_backward_kernel(qkv_ref, o_ref, p_ref, inv_ref, g_ref, d_ref, sum_ref):
    d_ref[...] = qkv_ref[...]
    attend_back_pair(d_ref, o_ref, p_ref.at[0], inv_ref, g_ref, sum_ref.at[0], 0)


def attend_backward(packed, attended, p, inv, grad_attended):
    length = packed.shape[0]
    width = packed.shape[1] // 3
    pairs = width // PAIR
    half = length // 2
    one = pl.BlockSpec((length, PAIR), lambda j: (0, j))
    three = pl.BlockSpec((length, 3 * PAIR), lambda j: (0, j))
    return pl.pallas_call(
        attend_backward_kernel,
        grid=(pairs,),
        in_specs=[three, one, pl.BlockSpec((1, 2, 3, half, half), lambda j: (j, 0, 0, 0, 0)), one, one],
        out_specs=[three, pl.BlockSpec((1, 2, 1, PAIR), lambda j: (j, 0, 0, 0))],
        out_shape=[
            jax.ShapeDtypeStruct(packed.shape, bf16),
            jax.ShapeDtypeStruct((pairs, 2, 1, PAIR), f32),
        ],
        compiler_params=pltpu.CompilerParams(vmem_limit_bytes=56 << 20),
        name="attend_backward",
    )(packed, attended, p, inv, grad_attended)


SWAP = [(0, 1), (1, 0)]


def swap(value):
    return lax.ppermute(value, "col", SWAP)


def ordered(mine, other, axis):
    first = lax.axis_index("col") == 0
    low = jnp.where(first, mine, other)
    high = jnp.where(first, other, mine)
    return jnp.concatenate([low, high], axis=axis)


def own_micro(halves):
    col = lax.axis_index("col")
    mine = lax.dynamic_index_in_dim(halves, col, 0, keepdims=False)
    other = swap(lax.dynamic_index_in_dim(halves, 1 - col, 0, keepdims=False))
    return ordered(mine, other, 1)


def back_micro(full):
    col = lax.axis_index("col")
    half = full.shape[1] // 2
    mine = lax.dynamic_slice_in_dim(full, col * half, half, 1)
    other = swap(lax.dynamic_slice_in_dim(full, (1 - col) * half, half, 1))
    first = col == 0
    return jnp.stack([jnp.where(first, mine, other), jnp.where(first, other, mine)])


G0_ORDERS = ("xzy", "xzy", "xyz")
REST_ORDERS = ("zxy", "zxy", "xyz")
MIDDLE_CUT = (5 / 15, 6 / 15)
GATHER_CUT = (4 / 12, 4 / 12)
REDUCE_CUT = (10 / 27, 11 / 27)


MESH = pl.DeviceIdType.MESH
DEPTH = 4
WAYS = ("up", "down", "y", "x", "core")
SIZES = {"z": DEPTH, "y": 2, "x": 2}


def row_of(z, y, core):
    return z * 4 + y * 2 + core


def my_place():
    row = lax.axis_index("row")
    return row // 4, (row // 2) % 2, row % 2, lax.axis_index("col")


def maybe(cond, act):
    if cond is None:
        act()
    else:
        pl.when(cond)(act)


def remote(src, dst, send, recv, device):
    return pltpu.make_async_remote_copy(
        src_ref=src, dst_ref=dst, send_sem=send, recv_sem=recv, device_id=device, device_id_type=MESH
    )


def greet(always, z, up, down):
    barrier = pltpu.get_barrier_semaphore()

    def hello(device):
        pl.semaphore_signal(barrier, inc=1, device_id=device, device_id_type=MESH)

    for device in always:
        hello(device)
    pl.when(z < DEPTH - 1)(lambda: hello(up))
    pl.when(z > 0)(lambda: hello(down))
    pl.semaphore_wait(
        barrier, len(always) + (z < DEPTH - 1).astype(jnp.int32) + (z > 0).astype(jnp.int32)
    )


def tree_rounds(order):
    rounds = {}
    for dz in (0, -1, 1, -2, 2, -3, 3):
        for dy in (0, 1):
            for dx in (0, 1):
                step = {"z": dz, "y": dy, "x": dx}
                via = None
                for axis in order:
                    if step[axis]:
                        via = axis
                onward = []
                open_now = via is None
                for axis in order:
                    if axis == via:
                        open_now = True
                    if not open_now:
                        continue
                    if axis == "z":
                        onward += ["up"] if dz <= 0 else []
                        onward += ["down"] if dz >= 0 else []
                    elif axis != via:
                        onward.append(axis)
                onward.append("core")
                rounds.setdefault(abs(dz) + dy + dx, []).append((dz, dy, dx, onward))
    return rounds


def pieces_of(widths, cuts):
    found = []
    for part in range(3):
        base = 0
        for weight, width in enumerate(widths):
            lo = max(base, cuts[part])
            hi = min(base + width, cuts[part + 1])
            if hi > lo:
                found.append((part, weight, lo - cuts[part], lo - base, hi - lo))
            base += width
    return found


class Gatherer:
    def __init__(self, place, shards, widths, cuts, orders, scratch):
        self.z, self.y, self.core, self.x = place
        z, y, core, x = place
        self.shards, self.widths = shards, widths
        self.bufs = scratch[:3]
        self.send, self.recv, self.local = scratch[3:]
        self.near = {
            "up": (row_of(z + 1, y, core), x),
            "down": (row_of(z - 1, y, core), x),
            "y": (row_of(z, 1 - y, core), x),
            "x": (row_of(z, y, core), 1 - x),
            "core": (row_of(z, y, 1 - core), x),
        }
        self.has = {"up": z < DEPTH - 1, "down": z > 0}
        self.orders = orders
        self.pieces = pieces_of(widths, cuts)
        self.trees = [tree_rounds(order) for order in orders]

    SCRATCH = 6

    @staticmethod
    def scratch_shapes(cuts, rows):
        dma = pltpu.SemaphoreType.DMA
        return [pltpu.VMEM((2, 16, rows, cuts[i + 1] - cuts[i]), bf16) for i in range(3)] + [
            dma((3, 5)),
            dma((3, 17)),
            dma((3, 6)),
        ]

    def loads(self):
        row = row_of(self.z, self.y, self.core)
        return [
            pltpu.make_async_copy(
                self.shards[weight].at[:, pl.ds(src, width)],
                self.bufs[part].at[self.x, row, :, pl.ds(at, width)],
                self.local.at[0, i],
            )
            for i, (part, weight, at, src, width) in enumerate(self.pieces)
        ]

    def copy(self, part, bz, by, bx, way):
        block = self.bufs[part].at[bx, row_of(bz, by, self.core)]
        slot = 16 if way == "core" else bx * 8 + bz * 2 + by
        return remote(
            block, block, self.send.at[part, WAYS.index(way)], self.recv.at[part, slot], self.near[way]
        )

    def all_of(self, part, count, way):
        blocks = self.bufs[part].at[0, pl.ds(0, count)]
        return remote(
            blocks, blocks, self.send.at[part, WAYS.index(way)], self.recv.at[part, 16], self.near[way]
        )

    def each(self, step, act, parts=(0, 1, 2)):
        for part in parts:
            for dz, dy, dx, onward in self.trees[part].get(step, []):
                bz, by, bx = self.z + dz, (self.y + dy) % 2, (self.x + dx) % 2
                cond = None if dz == 0 else ((bz >= 0) & (bz <= DEPTH - 1))
                maybe(cond, lambda: act(part, bz, by, bx, onward))

    def forward(self, step, parts=(0, 1, 2)):
        def act(part, bz, by, bx, onward):
            if step:
                self.copy(part, bz, by, bx, "y").wait_recv()
            for way in onward:
                maybe(self.has.get(way), lambda way=way: self.copy(part, bz, by, bx, way).start())

        self.each(step, act, parts)

    def arrive(self, parts=(0, 1, 2)):
        for part in parts:
            self.all_of(part, 16, "core").wait_recv()

    def drain(self):
        for part in range(3):
            count = 1
            for axis in self.orders[part]:
                if axis == "z":
                    for at in range(DEPTH):

                        def act(part=part, at=at, count=count):
                            if at < DEPTH - 1:
                                self.all_of(part, count * (at + 1), "up").wait_send()
                            if at > 0:
                                self.all_of(part, count * (DEPTH - at), "down").wait_send()

                        pl.when(self.z == at)(act)
                else:
                    self.all_of(part, count, axis).wait_send()
                count *= SIZES[axis]
            self.all_of(part, count, "core").wait_send()

    def stores(self, outs):
        return [
            pltpu.make_async_copy(
                self.bufs[part].at[side, :, :, pl.ds(at, width)],
                outs[weight].at[:, :, pl.ds(side * self.widths[weight] + src, width)],
                self.local.at[1 + side, i],
            )
            for i, (part, weight, at, src, width) in enumerate(self.pieces)
            for side in range(2)
        ]

    def weight(self, part, side, at, width):
        block = self.bufs[part][side, :, :, at : at + width]
        return block.reshape(-1, width)


def begin(copies):
    for copy in copies:
        copy.start()


def end(copies):
    for copy in copies:
        copy.wait()


FORWARD_ORDER = (0, 3, 1, 4, 2, 5)
ROWS = 256


def front_kernel(shape, *refs):
    (w_qkv, w_out, w_fc, w_proj, x_in, cot, vectors, starts, kinds) = refs[:9]
    (
        o_qkv, o_out, o_fc, o_proj, o_x, o_cot, o_vec, o_packed, o_p, o_inv, o_att, o_normed, o_middle, o_second,
        o_active, o_slope,
    ) = refs[9:25]
    scr = refs[25:]
    n = Gatherer.SCRATCH
    place = my_place()
    z, y, core, x = place
    one, two, three = (
        Gatherer(place, shards, *shape["groups"][i], scr[n * i : n * (i + 1)])
        for i, shards in enumerate(([w_qkv], [w_out, w_fc], [w_proj]))
    )
    (
        xm, xo, cm, xf, n1, pk, pb, ib, att, bias, mid, n2, act_buf, slope_buf, vec_o, s_x, r_x, s_c, r_c, s_v, r_v,
        s_in, s_pair, s_end,
    ) = scr[3 * n :]
    length, half_width = xm.shape
    width = 2 * half_width
    half = length // 2
    blocks = length // ROWS
    to_x = one.near["x"]

    def x_copy(i):
        span = pl.ds(i * ROWS, ROWS)
        return remote(x_in.at[1 - x, span], xo.at[span], s_x.at[i], r_x.at[i], to_x)

    own_cols = pl.ds(pl.multiple_of(x * half_width, PAIR), half_width)

    def cot_copy(i):
        span = pl.ds(i * ROWS, ROWS)
        return remote(cot.at[1 - x, span], o_cot.at[span, own_cols], s_c.at[i], r_c.at[i], to_x)

    vec_copy = remote(vectors, vec_o, s_v, r_v, to_x)
    own_x = pltpu.make_async_copy(x_in.at[x], xm, s_in.at[0])
    own_cot = pltpu.make_async_copy(cot.at[x], cm, s_in.at[1])
    put_cot = pltpu.make_async_copy(cm, o_cot.at[:, own_cols], s_in.at[2])
    begin(one.loads())
    own_x.start()
    begin(two.loads())
    begin(three.loads())
    own_cot.start()
    greet([to_x, one.near["y"], one.near["core"]], z, one.near["up"], one.near["down"])
    vec_copy.start()
    end(one.loads())
    one.forward(0)
    begin([x_copy(i) for i in range(blocks)])
    for part in range(2):
        bias[part] = half_bias(starts[x, 0, part], kinds[x, 0, part], part, half)
    one.forward(1)
    end(two.loads())
    end(three.loads())
    one.forward(2)
    two.forward(0)
    vec_copy.wait()
    is_low = x == 0
    at = 0
    full = []
    for size in shape["vectors"]:
        mine, other = vectors[:, at : at + size], vec_o[:, at : at + size]
        low, high = jnp.where(is_low, mine, other), jnp.where(is_low, other, mine)
        o_vec[:, 2 * at : 2 * at + size] = low
        o_vec[:, 2 * at + size : 2 * at + 2 * size] = high
        full.append(slice(2 * at, 2 * at + 2 * size))
        at += size
    own_x.wait()

    def norm(value, gain, shift):
        average = jnp.sum(value, axis=1, keepdims=True) / width
        square = jnp.sum(value * value, axis=1, keepdims=True) / width
        inverse = lax.rsqrt(square - average * average + epsilon)
        return ((value - average) * inverse * o_vec[:, full[gain]] + o_vec[:, full[shift]]).astype(bf16)

    def first_norm(i):
        span = slice(i * ROWS, (i + 1) * ROWS)
        x_copy(i).wait_recv()
        mine, other = xm[span, :], xo[span, :]
        xf[span, :half_width] = jnp.where(is_low, mine, other)
        xf[span, half_width:] = jnp.where(is_low, other, mine)
        n1[span, :] = norm(xf[span, :].astype(f32), 0, 1)

    one.forward(3)
    first_norm(0)
    first_norm(1)
    one.forward(4)
    first_norm(2)
    one.forward(5)
    first_norm(3)
    two.forward(1)
    to_x_out = pltpu.make_async_copy(xf, o_x, s_end.at[0])
    to_normed = pltpu.make_async_copy(n1, o_normed, s_end.at[1])
    begin([to_x_out, to_normed])

    def pair_puts(step):
        j = FORWARD_ORDER[step]
        slot = step % 2
        return [
            pltpu.make_async_copy(pk.at[slot], o_packed.at[:, pl.ds(3 * PAIR * j, 3 * PAIR)], s_pair.at[slot, 0]),
            pltpu.make_async_copy(pb.at[slot], o_p.at[j], s_pair.at[slot, 1]),
            pltpu.make_async_copy(ib.at[slot], o_inv.at[:, pl.ds(PAIR * j, PAIR)], s_pair.at[slot, 2]),
        ]

    def pair(step):
        j = FORWARD_ORDER[step]
        slot = step % 2
        if step >= 2:
            end(pair_puts(step - 2))
        value = nn(n1[...], one.weight(j % 3, j // 3, 0, 3 * PAIR))
        cols = slice(PAIR * j, PAIR * (j + 1))
        shift = jnp.concatenate(
            [
                o_vec[:, full[2]][:, cols],
                jnp.zeros((1, PAIR), f32),
                o_vec[:, full[3]][:, cols],
            ],
            axis=1,
        )
        pk[slot] = (value + shift).astype(bf16)
        attend_pair(pk.at[slot], att.at[:, cols], pb.at[slot], ib.at[slot], bias)
        begin(pair_puts(step))

    one.arrive((0,))
    pair(0)
    two.forward(2)
    one.arrive((1,))
    pair(1)
    two.forward(3)
    three.forward(0)
    pair(2)
    two.forward(4)
    cot_copy(0).start()
    one.arrive((2,))
    qkv_stores = one.stores([o_qkv])
    begin(qkv_stores)
    pair(3)
    two.forward(5)
    three.forward(1)
    cot_copy(1).start()
    own_cot.wait()
    put_cot.start()
    pair(4)
    three.forward(2)
    cot_copy(2).start()
    pair(5)
    three.forward(3)
    cot_copy(3).start()
    two.arrive()
    two_stores = two.stores([o_out, o_fc])
    begin(two_stores)
    end(pair_puts(4))
    end(pair_puts(5))
    to_att = pltpu.make_async_copy(att, o_att, s_end.at[2])
    to_att.start()
    out_pieces = [p for p in two.pieces if p[1] == 0]
    fc_pieces = [p for p in two.pieces if p[1] == 1]
    for i in range(blocks):
        span = slice(i * ROWS, (i + 1) * ROWS)
        total = xf[span, :].astype(f32) + o_vec[:, full[4]]
        for part, _, at, src, w in out_pieces:
            for side in range(2):
                cols = slice(side * half_width + src, side * half_width + src + w)
                total = total + nt(att[span, cols], two.weight(part, side, at, w))
        mid[span, :] = total
        n2[span, :] = norm(total, 5, 6)
    to_mid = pltpu.make_async_copy(mid, o_middle, s_end.at[3])
    to_second = pltpu.make_async_copy(n2, o_second, s_end.at[4])
    begin([to_mid, to_second])
    three.forward(4)
    ff_half = two.widths[1]
    puts = []
    for k, ((part, _, at, src, w), side) in enumerate([(p, side) for p in fc_pieces for side in range(2)]):
        cols = slice(side * ff_half + src, side * ff_half + src + w)
        b_cols = slice(full[7].start + cols.start, full[7].start + cols.stop)

        def block(i, carry):
            span = pl.ds(pl.multiple_of(i * ROWS, ROWS), ROWS)
            hidden = nn(n2[span, :], two.weight(part, side, at, w)) + o_vec[:, b_cols]
            squared = hidden * hidden
            tanh = jnp.tanh(hidden * (GELU_A + (GELU_A * GELU_B) * squared))
            gate = 0.5 + 0.5 * tanh
            act_buf[span, cols] = (hidden * gate).astype(bf16)
            inner = hidden * (GELU_A + (3.0 * GELU_A * GELU_B) * squared)
            slope_buf[span, cols] = (gate + inner * (0.5 - 0.5 * tanh * tanh)).astype(bf16)
            return carry

        lax.fori_loop(0, blocks, block, 0)
        now = [
            pltpu.make_async_copy(act_buf.at[:, cols], o_active.at[:, cols], s_end.at[5 + 2 * k]),
            pltpu.make_async_copy(slope_buf.at[:, cols], o_slope.at[:, cols], s_end.at[6 + 2 * k]),
        ]
        begin(now)
        puts += now
        if k == 1:
            three.forward(5)
    three.arrive()
    three_stores = three.stores([o_proj])
    begin(three_stores)
    one.drain()
    two.drain()
    three.drain()
    for i in range(blocks):
        x_copy(i).wait_send()
    for i in range(blocks):
        cot_copy(i).wait()
    end([put_cot, to_x_out, to_normed, to_att, to_mid, to_second] + puts)
    end(qkv_stores)
    end(two_stores)
    end(three_stores)


def front_near(shards, x_in, cot, vectors, starts, kinds):
    rows = shards[0].shape[0]
    widths = [shard.shape[1] for shard in shards]
    _, length, half_width = x_in.shape
    width = 2 * half_width
    half = length // 2
    pairs = width // PAIR
    groups = [
        (widths[:1], [0, 3 * PAIR, 6 * PAIR, 9 * PAIR], G0_ORDERS),
        (widths[1:3], part_cuts(widths[1:3], *MIDDLE_CUT), REST_ORDERS),
        (widths[3:], part_cuts(widths[3:], *GATHER_CUT), REST_ORDERS),
    ]
    ff = 2 * widths[2]
    sizes = [v.shape[0] for v in vectors]
    shape = {"groups": groups, "vectors": sizes}
    dma = pltpu.SemaphoreType.DMA
    scratch = []
    for _, cuts, _ in groups:
        scratch += Gatherer.scratch_shapes(cuts, rows)
    scratch += [
        pltpu.VMEM((length, half_width), bf16),
        pltpu.VMEM((length, half_width), bf16),
        pltpu.VMEM((length, half_width), bf16),
        pltpu.VMEM((length, width), bf16),
        pltpu.VMEM((length, width), bf16),
        pltpu.VMEM((2, length, 3 * PAIR), bf16),
        pltpu.VMEM((2, 2, 3, half, half), bf16),
        pltpu.VMEM((2, length, PAIR), f32),
        pltpu.VMEM((length, width), bf16),
        pltpu.VMEM((2, half, half), f32),
        pltpu.VMEM((length, width), f32),
        pltpu.VMEM((length, width), bf16),
        pltpu.VMEM((length, ff), bf16),
        pltpu.VMEM((length, ff), bf16),
        pltpu.VMEM((1, sum(sizes)), f32),
    ]
    scratch += [dma((4,)), dma((4,)), dma((4,)), dma((4,)), dma(()), dma(()), dma((3,)), dma((2, 3)), dma((20,))]
    any_space = pl.BlockSpec(memory_space=pl.ANY)
    vmem = pl.BlockSpec(memory_space=pltpu.VMEM)
    smem = pl.BlockSpec(memory_space=pltpu.SMEM)

    def out(dims, kind=bf16):
        return jax.ShapeDtypeStruct(dims, kind)

    outs = pl.pallas_call(
        lambda *refs: front_kernel(shape, *refs),
        in_specs=[any_space] * 6 + [vmem, smem, smem],
        out_specs=[any_space] * 6 + [vmem] + [any_space] * 9,
        out_shape=[out((16, rows, 2 * w)) for w in widths]
        + [
            out((length, width)),
            out((length, width)),
            out((1, 2 * sum(sizes)), f32),
            out((length, 3 * width)),
            out((pairs, 2, 3, half, half)),
            out((length, width), f32),
            out((length, width)),
            out((length, width)),
            out((length, width), f32),
            out((length, width)),
            out((length, ff)),
            out((length, ff)),
        ],
        scratch_shapes=scratch,
        compiler_params=pltpu.CompilerParams(
            collective_id=0, has_side_effects=True, vmem_limit_bytes=67043328
        ),
        cost_estimate=pl.CostEstimate(flops=20 << 30, bytes_accessed=200 << 20, transcendentals=0),
        name="gather_weights",
    )(*shards, x_in, cot, jnp.concatenate(vectors).reshape(1, -1), starts, kinds)
    full = [w.reshape(16 * rows, -1) for w in outs[:4]]
    vec = outs[6].reshape(-1)
    at = 0
    fulls = []
    for size in sizes:
        fulls.append(vec[at : at + 2 * size])
        at += 2 * size
    return full, list(outs[4:6]), fulls, list(outs[7:])


class Reducer:
    def __init__(self, place, grads, widths, cuts, scratch):
        self.z, self.y, self.core, self.x = place
        z, y, core, x = place
        self.grads = grads
        self.widths = widths
        self.acc, self.rcore = scratch[0:3], scratch[3:6]
        rx, ry, self.rz, self.cy, self.cx = scratch[6:8], scratch[8:10], scratch[10:13], scratch[13], scratch[14]
        self.final = scratch[15:18]
        (
            self.s_core, self.r_core, self.s_one, self.r_one, self.s_two, self.r_two, self.s_z, self.r_z, self.s_c,
            self.r_c, self.s_load, self.s_out,
        ) = scratch[18:]
        self.up, self.down = (row_of(z + 1, y, core), x), (row_of(z - 1, y, core), x)
        self.to_y, self.to_x = (row_of(z, 1 - y, core), x), (row_of(z, y, core), 1 - x)
        self.to_core = (row_of(z, y, 1 - core), x)
        self.by_part = [[p for p in pieces_of(widths, cuts) if p[0] == part] for part in range(3)]
        self.first = [(rx[0], self.to_x), (ry[0], self.to_y)]
        self.second = [(ry[1], self.to_y), (rx[1], self.to_x)]

    SCRATCH = 30

    @staticmethod
    def scratch_shapes(widths, cuts, rows):
        w = [cuts[i + 1] - cuts[i] for i in range(3)]
        dma = pltpu.SemaphoreType.DMA

        def low(*shape):
            return pltpu.VMEM(shape, bf16)

        scratch = [low(2, 4, 2, rows, k) for k in w] * 2
        scratch += [low(4, 2, rows, w[0]), low(4, rows, w[1])]
        scratch += [low(4, 2, rows, w[1]), low(4, rows, w[0])]
        scratch += [low(2, 4, rows, w[0]), low(2, 4, rows, w[1]), low(2, 4, 2, 2, rows, w[2])]
        scratch += [low(2, rows, w[2]), low(rows, w[2])]
        scratch += [pltpu.VMEM((rows, k), f32) for k in w]
        scratch += [dma((3,)), dma((3, 2, 4)), dma((2,)), dma((2, 4)), dma((2,)), dma((2, 4))]
        scratch += [dma((3, 2, 4)), dma((3, 2, 4)), dma((2,)), dma((2,)), dma((3,)), dma((3, 2))]
        return scratch

    def cols(self, weight, side, src, width):
        return pl.ds(pl.multiple_of(side * self.widths[weight] + src, 128), width)

    def loop(self, act):
        def step(zi, carry):
            act(zi)
            return carry

        lax.fori_loop(0, DEPTH, step, 0)

    def add(self, total, term):
        total[...] = total[...] + term[...]

    def loads(self, part):
        return [
            pltpu.make_async_copy(
                self.grads[weight].at[:, :, self.core, :, self.cols(weight, side, src, width)],
                self.acc[part].at[side, :, :, :, pl.ds(at, width)],
                self.s_load.at[part],
            )
            for i, (_, weight, at, src, width) in enumerate(self.by_part[part])
            for side in range(2)
        ]

    def view(self, part, ref, far, zi):
        if part == 0:
            return ref.at[(1 - self.x) if far else self.x, zi]
        return ref.at[:, zi, (1 - self.y) if far else self.y]

    def core_copies(self, part, far, zi):
        other = 1 - self.core
        copies = []
        for i, (_, weight, at, src, width) in enumerate(self.by_part[part]):
            cols = pl.ds(at, width)
            if part == 0:
                sides = [(1 - self.x) if far else self.x]
            else:
                sides = [0, 1]
            for k, side in enumerate(sides):
                gcols = self.cols(weight, side, src, width)
                if part == 1:
                    by = (1 - self.y) if far else self.y
                    src_ref = self.grads[weight].at[zi, by, other, :, gcols]
                    dst_ref = self.rcore[1].at[side, zi, by, :, cols]
                else:
                    src_ref = self.grads[weight].at[zi, :, other, :, gcols]
                    dst_ref = self.rcore[part].at[side, zi, :, :, cols]
                copies.append(
                    remote(
                        src_ref, dst_ref, self.s_core.at[part], self.r_core.at[part, int(far), zi], self.to_core
                    )
                )
        return copies

    def core_wait(self, part, far, zi):
        if part == 2:
            blocks = self.rcore[2].at[:, zi]
        else:
            blocks = self.view(part, self.rcore[part], far, zi)
        remote(
            blocks, blocks, self.s_core.at[part], self.r_core.at[part, int(far), zi], self.to_core
        ).wait_recv()

    def start(self, parts):
        for part in parts:
            for load in self.loads(part):
                load.start()

        def begin(far):
            def act(zi):
                for part in parts:
                    if far or part < 2:
                        for copy in self.core_copies(part, far, zi):
                            copy.start()

            self.loop(act)

        begin(True)
        begin(False)

    def first_copy(self, part, zi):
        buf, device = self.first[part]
        return remote(
            self.view(part, self.acc[part], True, zi), buf.at[zi], self.s_one.at[part], self.r_one.at[part, zi], device
        )

    def half_of(self, part, zi, far):
        if part == 0:
            return self.acc[0].at[self.x, zi, (1 - self.y) if far else self.y]
        return self.acc[1].at[(1 - self.x) if far else self.x, zi, self.y]

    def second_copy(self, part, zi):
        buf, device = self.second[part]
        return remote(self.half_of(part, zi, True), buf.at[zi], self.s_two.at[part], self.r_two.at[part, zi], device)

    def far(self, parts):
        for part in parts:
            pltpu.make_async_copy(self.rcore[part], self.acc[part], self.s_load.at[part]).wait()

        def act(zi):
            for part in parts:
                self.core_wait(part, True, zi)
                if part == 2:
                    self.add(self.acc[2].at[:, zi], self.rcore[2].at[:, zi])
                else:
                    self.add(self.view(part, self.acc[part], True, zi), self.view(part, self.rcore[part], True, zi))
                    self.first_copy(part, zi).start()

        self.loop(act)

    def near(self, parts):
        def act(zi):
            for part in parts:
                self.core_wait(part, False, zi)
                mine = self.view(part, self.acc[part], False, zi)
                self.add(mine, self.view(part, self.rcore[part], False, zi))
                self.first_copy(part, zi).wait_recv()
                self.add(mine, self.first[part][0].at[zi])
                self.second_copy(part, zi).start()

        self.loop(act)

    def last(self, parts):
        def act(zi):
            for part in parts:
                self.second_copy(part, zi).wait_recv()
                self.add(self.half_of(part, zi, False), self.second[part][0].at[zi])

        self.loop(act)

    def block(self, part, zi):
        if part == 2:
            return self.acc[2].at[:, zi]
        return self.acc[part].at[self.x, zi, self.y]

    def line_copy(self, part, direction, zd):
        return remote(
            self.block(part, zd),
            self.rz[part].at[direction, zd],
            self.s_z.at[part, direction, zd],
            self.r_z.at[part, direction, zd],
            self.down if direction else self.up,
        )

    def line(self, parts, step):
        for direction in range(2):
            at = DEPTH - 1 - step if direction else step
            for zd in (0, 1, 2) if direction else (3, 2, 1):
                if not ((at > zd) if direction else (at < zd)):
                    continue
                for part in parts:

                    def act(part=part, direction=direction, zd=zd):
                        if step > 0:
                            self.line_copy(part, direction, zd).wait_recv()
                            self.add(self.block(part, zd), self.rz[part].at[direction, zd])
                        self.line_copy(part, direction, zd).start()

                    pl.when(self.z == at)(act)

    def line_end(self, parts):
        for part in parts:
            for direction in range(2):

                def act(part=part, direction=direction):
                    self.line_copy(part, direction, self.z).wait_recv()
                    self.add(self.block(part, self.z), self.rz[part].at[direction, self.z])

                pl.when((self.z < DEPTH - 1) if direction else (self.z > 0))(act)

    def y_copy(self):
        return remote(self.acc[2].at[:, self.z, 1 - self.y], self.cy, self.s_c.at[0], self.r_c.at[0], self.to_y)

    def x_copy(self):
        return remote(self.acc[2].at[1 - self.x, self.z, self.y], self.cx, self.s_c.at[1], self.r_c.at[1], self.to_x)

    def turn(self):
        self.y_copy().wait_recv()
        self.add(self.acc[2].at[:, self.z, self.y], self.cy)
        self.x_copy().start()

    def turn_end(self):
        self.x_copy().wait_recv()
        self.add(self.acc[2].at[self.x, self.z, self.y], self.cx)

    def stores(self, outs):
        return [
            pltpu.make_async_copy(
                self.final[part].at[:, pl.ds(at, width)], outs[weight].at[:, pl.ds(src, width)], self.s_out.at[part, i]
            )
            for part in range(3)
            for i, (_, weight, at, src, width) in enumerate(self.by_part[part])
        ]

    def finish(self, outs):
        for part in range(3):
            self.final[part][...] = self.acc[part][self.x, self.z, self.y].astype(f32)
        for store in self.stores(outs):
            store.start()

    def drain(self, outs):
        for part in range(3):
            remote(
                self.acc[part], self.rcore[part], self.s_core.at[part], self.r_core.at[part, 0, 0], self.to_core
            ).wait_send()
            for direction in range(2):
                for zd in range(DEPTH):
                    pl.when((self.z > zd) if direction else (self.z < zd))(
                        lambda part=part, direction=direction, zd=zd: self.line_copy(part, direction, zd).wait_send()
                    )
            if part < 2:
                for (buf, device), send, recv in (
                    (self.first[part], self.s_one, self.r_one),
                    (self.second[part], self.s_two, self.r_two),
                ):
                    remote(buf, buf, send.at[part], recv.at[part, 0], device).wait_send()
        self.y_copy().wait_send()
        self.x_copy().wait_send()
        for store in self.stores(outs):
            store.wait()


PAIR_ORDER = (2, 5, 0, 3, 1, 4)


def back_kernel(shape, *refs):
    (
        g_out, g_fc, g_proj, packed, attended, p_all, inv_all, gatt, normed_t, w_qkv, x_all, middle, gain_ref, small_in,
        o_qkv, o_out, o_fc, o_proj, o_sum, o_input,
    ) = refs[:20]
    scr = refs[20:]
    first = Reducer.SCRATCH
    place = my_place()
    z, y, core, x = place
    early = Reducer(place, [g_out, g_fc, g_proj], shape["early"], shape["early_cuts"], scr[:first])
    qkv, o_buf, p_buf, inv_buf, g_buf, nt_buf, w_buf, x_buf, m_buf, gqkv, gi, col_sum, srecv, sacc = scr[2 * first : 2 * first + 14]
    s_all, s_pair, s_mid, s_gi, r_gi, l_gi, s_s, r_s = scr[2 * first + 14 :]
    late = Reducer(place, [gqkv], shape["late"], shape["late_cuts"], scr[first : 2 * first])
    whole = [
        pltpu.make_async_copy(packed, qkv, s_all.at[0]),
        pltpu.make_async_copy(normed_t, nt_buf, s_all.at[1]),
        pltpu.make_async_copy(w_qkv, w_buf, s_all.at[2]),
        pltpu.make_async_copy(x_all, x_buf, s_all.at[3]),
    ]

    def pair_loads(step):
        j = PAIR_ORDER[step]
        slot = step % 2
        cols = pl.ds(j * PAIR, PAIR)
        return [
            pltpu.make_async_copy(p_all.at[j], p_buf.at[slot], s_pair.at[slot, 0]),
            pltpu.make_async_copy(attended.at[:, cols], o_buf.at[slot], s_pair.at[slot, 1]),
            pltpu.make_async_copy(inv_all.at[:, cols], inv_buf.at[slot], s_pair.at[slot, 2]),
            pltpu.make_async_copy(gatt.at[:, cols], g_buf.at[slot], s_pair.at[slot, 3]),
        ]

    def begin(copies):
        for copy in copies:
            copy.start()

    def end(copies):
        for copy in copies:
            copy.wait()

    begin(whole[:1])
    begin(pair_loads(0))
    begin(whole[1:])
    to_z1 = (row_of(z + 1 - 2 * (z % 2), y, core), x)
    to_z2 = (row_of((z + 2) % 4, y, core), x)
    greet([early.to_core, early.to_x, early.to_y, to_z2], z, early.up, early.down)
    early.start((0, 1, 2))
    end(whole[:1])

    def pair(step):
        j = PAIR_ORDER[step]
        slot = step % 2
        if step < 5:
            begin(pair_loads(step + 1))
        end(pair_loads(step))
        attend_back_pair(qkv, o_buf.at[slot], p_buf.at[slot], inv_buf.at[slot], g_buf.at[slot], col_sum.at[j], 3 * PAIR * j)
        if step == 0:
            end(whole[1:2])
        cols = slice(3 * PAIR * j, 3 * PAIR * (j + 1))
        grad = nn(nt_buf[...], qkv[:, cols]).astype(bf16)
        gqkv[:, :, :, :, cols] = grad.reshape(gqkv.shape[:4] + (3 * PAIR,))

    rows = m_buf.shape[1]
    blocks = x_buf.shape[0] // rows

    def mid_load(i):
        return pltpu.make_async_copy(middle.at[pl.ds(i * rows, rows)], m_buf.at[i % 2], s_mid.at[i % 2])

    def input_copies(i):
        span = pl.ds(i * rows, rows)
        return (
            pltpu.make_async_copy(gi.at[0, span], o_input.at[x, span], l_gi.at[i]),
            remote(gi.at[1, span], o_input.at[x, span], s_gi.at[i], r_gi.at[i], early.to_x),
        )

    sums = [None, None]

    def input_block(i):
        span = slice(i * rows, (i + 1) * rows)
        grad = nt(qkv[span, :], w_buf[...])
        if i + 1 < blocks:
            mid_load(i + 1).start()
        mid_load(i).wait()
        value = x_buf[span, :].astype(f32)
        width = value.shape[1]
        average = jnp.sum(value, axis=1, keepdims=True) / width
        square = jnp.sum(value * value, axis=1, keepdims=True) / width
        inverse = lax.rsqrt(square - average * average + epsilon)
        centred = (value - average) * inverse
        scaled = grad * gain_ref[...]
        one = jnp.sum(scaled, axis=1, keepdims=True) / width
        two = jnp.sum(scaled * centred, axis=1, keepdims=True) / width
        out = m_buf[i % 2] + inverse * (scaled - one - centred * two)
        for k, term in enumerate((grad * centred, grad)):
            term = jnp.sum(term, axis=0, keepdims=True)
            sums[k] = term if sums[k] is None else sums[k] + term
        half = width // 2
        is_low = x == 0
        gi[0, span, :] = jnp.where(is_low, out[:, :half], out[:, half:]).astype(bf16)
        gi[1, span, :] = jnp.where(is_low, out[:, half:], out[:, :half]).astype(bf16)
        for copy in input_copies(i):
            copy.start()

    partners = [early.to_core, early.to_x, early.to_y, to_z1, to_z2]

    def small_copy(step):
        return remote(sacc.at[step], srecv.at[step], s_s.at[step], r_s.at[step], partners[step])

    def small_start():
        sacc[0] = small_in[...]
        at = 0
        for k in range(2):
            for i in range(6):
                sacc[0, at : at + 1, :] = sums[k][:, i * PAIR : (i + 1) * PAIR]
                at += 1
        for k in range(2):
            for i in range(6):
                sacc[0, at : at + 1, :] = col_sum[i, k]
                at += 1
        small_copy(0).start()

    def small_next(step):
        small_copy(step).wait()
        sacc[step + 1] = sacc[step] + srecv[step]
        if step < 4:
            small_copy(step + 1).start()

    both = (0, 1)
    pair(0)
    early.far((0, 1, 2))
    early.line((2,), 0)
    pair(1)
    late.start((2,))
    pair(2)
    early.line((2,), 1)
    pair(3)
    late.start((0,))
    late.far((2,))
    early.line((2,), 2)
    late.line((2,), 0)
    mid_load(0).start()
    pair(4)
    early.near(both)
    late.far((0,))
    pair(5)
    late.start((1,))
    early.line_end((2,))
    early.y_copy().start()
    late.line((2,), 1)
    end(whole[2:])
    input_block(0)
    early.last(both)
    early.line(both, 0)
    late.far((1,))
    late.line((2,), 2)
    input_block(1)
    early.turn()
    early.line(both, 1)
    late.near((0,))
    late.line_end((2,))
    late.y_copy().start()
    input_block(2)
    early.turn_end()
    early.line(both, 2)
    late.near((1,))
    late.turn()
    input_block(3)
    small_start()
    late.last((0,))
    late.line((0,), 0)
    early.line_end(both)
    early.finish([o_out, o_fc, o_proj])
    small_next(0)
    late.last((1,))
    late.line((1,), 0)
    late.turn_end()
    late.line(both, 1)
    small_next(1)
    late.line(both, 2)
    small_next(2)
    late.line_end(both)
    late.finish([o_qkv])
    small_next(3)
    small_next(4)
    o_sum[...] = sacc[5]
    for i in range(blocks):
        local, other = input_copies(i)
        local.wait()
        other.wait()
    early.drain([o_out, o_fc, o_proj])
    late.drain([o_qkv])


def back_near(grads, packed, attended, p, inv, gatt, normed_t, w_qkv, x, middle, gain, small, rows):
    length, width = x.shape
    wide = packed.shape[1]
    early = [grad.shape[1] // 2 for grad in grads]
    shape = {"early": early, "early_cuts": part_cuts(early, *REDUCE_CUT), "late": [wide // 2]}
    shape["late_cuts"] = [0, wide // 6, wide // 3, wide // 2]
    dma = pltpu.SemaphoreType.DMA
    half = length // 2
    blocks = 4
    scratch = Reducer.scratch_shapes(early, shape["early_cuts"], rows)
    scratch += Reducer.scratch_shapes(shape["late"], shape["late_cuts"], rows)
    scratch += [
        pltpu.VMEM((length, wide), bf16),
        pltpu.VMEM((2, length, PAIR), bf16),
        pltpu.VMEM((2, 2, 3, half, half), bf16),
        pltpu.VMEM((2, length, PAIR), f32),
        pltpu.VMEM((2, length, PAIR), bf16),
        pltpu.VMEM((width, length), bf16),
        pltpu.VMEM((width, wide), bf16),
        pltpu.VMEM((length, width), bf16),
        pltpu.VMEM((2, length // blocks, width), f32),
        pltpu.VMEM((4, 2, 2, rows, wide), bf16),
        pltpu.VMEM((2, length, width // 2), bf16),
        pltpu.VMEM((width // PAIR, 2, 1, PAIR), f32),
        pltpu.VMEM((5,) + small.shape, f32),
        pltpu.VMEM((6,) + small.shape, f32),
    ]
    scratch += [dma((4,)), dma((2, 4)), dma((2,)), dma((4,)), dma((4,)), dma((4,)), dma((5,)), dma((5,))]
    shaped = [grad.reshape(4, 2, 2, rows, grad.shape[1]) for grad in grads]
    any_space = pl.BlockSpec(memory_space=pl.ANY)
    vmem = pl.BlockSpec(memory_space=pltpu.VMEM)
    outs = pl.pallas_call(
        lambda *refs: back_kernel(shape, *refs),
        in_specs=[any_space] * 12 + [vmem, vmem],
        out_specs=[any_space] * 4 + [vmem, any_space],
        out_shape=[jax.ShapeDtypeStruct((rows, w), f32) for w in [wide // 2] + early]
        + [jax.ShapeDtypeStruct(small.shape, f32), jax.ShapeDtypeStruct((2, length, width // 2), bf16)],
        scratch_shapes=scratch,
        compiler_params=pltpu.CompilerParams(
            collective_id=1, has_side_effects=True, vmem_limit_bytes=67043328
        ),
        cost_estimate=pl.CostEstimate(flops=30 << 30, bytes_accessed=200 << 20, transcendentals=0),
        name="reduce_grads",
    )(*shaped, packed, attended, p, inv, gatt, normed_t, w_qkv, x, middle, gain.reshape(1, -1), small)
    return outs


def gather_far(shards):
    fulls = []
    for shard in shards:
        rows = lax.all_gather(shard, ("col", "row"), axis=0, tiled=True)
        fulls.append(jnp.concatenate(jnp.split(rows, 2, axis=0), axis=1))
    return fulls


def reduce_far(grads, small):
    outs = []
    for grad in grads:
        halves = jnp.concatenate(jnp.split(grad, 2, axis=1), axis=0)
        outs.append(lax.psum_scatter(halves, ("col", "row"), scatter_dimension=0, tiled=True).astype(f32))
    return outs, lax.psum(small, ("row", "col"))


def part_cuts(widths, first, second):
    total = sum(widths) // 128
    one = round(total * first)
    two = round(total * (first + second))
    return [0, one * 128, two * 128, total * 128]


def layer_norm(value):
    width = value.shape[-1]
    average = jnp.sum(value, axis=-1, keepdims=True) / width
    square = jnp.sum(value * value, axis=-1, keepdims=True) / width
    inverse = lax.rsqrt(square - average * average + epsilon)
    return (value - average) * inverse, inverse


def norm_backward(grad, centred, inverse, gain):
    scaled = grad * gain
    first = jnp.mean(scaled, axis=-1, keepdims=True)
    second = jnp.mean(scaled * centred, axis=-1, keepdims=True)
    back = inverse * (scaled - first - centred * second)
    return back, jnp.sum(grad * centred, axis=0), jnp.sum(grad, axis=0)


def by_pairs(block):
    rows, three, half = block.shape
    return block.reshape(rows, three, half // PAIR, PAIR).transpose(0, 2, 1, 3).reshape(rows, three * half)


def body(
    near, x_in, span_start, span_kind, ln1_gain, ln1_bias, w_qkv, b_query, b_value, w_out, b_out,
    ln2_gain, ln2_bias, w_fc, b_fc, w_proj, b_proj, cotangent,
):
    half_width = x_in.shape[2]
    shard = w_qkv.shape[0]
    col = lax.axis_index("col")

    vectors = [ln1_gain, ln1_bias, b_query, b_value, b_out, ln2_gain, ln2_bias, b_fc, b_proj]
    shards = [by_pairs(w_qkv), w_out.T, w_fc, w_proj.T]
    width = 2 * half_width
    if near:
        weights, (x_own, grad_out), vectors, saved = front_near(shards, x_in, cotangent, vectors, span_start, span_kind)
        qkv_all, out_all, fc_all, proj_all = weights
        ln1_gain, _, _, _, _, ln2_gain, _, _, b_proj = vectors
        packed, p, inv, attended, normed_first, middle, normed_second, active, slope = saved
        centred_second, inverse_second = layer_norm(middle)
    else:
        x_own = own_micro(x_in)
        residual = x_own.astype(f32)
        grad_out = own_micro(cotangent)
        qkv_all, out_all, fc_all, proj_all = gather_far(shards)
        flat = jnp.concatenate(vectors)
        flat_other = swap(flat)
        full = []
        at = 0
        for vector in vectors:
            full.append(ordered(vector, flat_other[at : at + vector.shape[0]], 0))
            at += vector.shape[0]
        ln1_gain, ln1_bias, b_query, b_value, b_out, ln2_gain, ln2_bias, b_fc, b_proj = full
        starts = lax.dynamic_index_in_dim(span_start, col, 0, keepdims=False)[0]
        kinds = lax.dynamic_index_in_dim(span_kind, col, 0, keepdims=False)[0]
        spans = jnp.stack([starts, kinds])
        centred_first, inverse_first = layer_norm(residual)
        normed_first = (centred_first * ln1_gain + ln1_bias).astype(bf16)
        bias = jnp.stack([b_query, jnp.zeros_like(b_query), b_value]).reshape(3, -1, PAIR)
        packed = (nn(normed_first, qkv_all) + bias.transpose(1, 0, 2).reshape(-1)).astype(bf16)
        attended, p, inv = attend_forward(packed, spans)
        middle = residual + nt(attended, out_all) + b_out
        centred_second, inverse_second = layer_norm(middle)
        normed_second = (centred_second * ln2_gain + ln2_bias).astype(bf16)
        hidden = nn(normed_second, fc_all) + b_fc
        squared = hidden * hidden
        tanh = jnp.tanh(GELU_A * hidden * (1.0 + GELU_B * squared))
        active = (0.5 * hidden * (1.0 + tanh)).astype(bf16)
        slope = (
            0.5 * (1.0 + tanh)
            + 0.5 * hidden * (1.0 - tanh * tanh) * GELU_A * (1.0 + 3.0 * GELU_B * squared)
        ).astype(bf16)
    layer_out = back_micro((middle + nt(active, proj_all) + b_proj).astype(bf16))

    grad_out_wide = grad_out.astype(f32)
    g_proj = tn(grad_out, active).astype(bf16)
    grad_hidden = (nn(grad_out, proj_all) * slope.astype(f32)).astype(bf16)
    g_fc = tn(normed_second, grad_hidden).astype(bf16)
    g_bfc = jnp.sum(grad_hidden.astype(f32), axis=0)
    grad_normed = nt(grad_hidden, fc_all)
    back, g_ln2_gain, g_ln2_bias = norm_backward(grad_normed, centred_second, inverse_second, ln2_gain)
    grad_middle = grad_out_wide + back
    g_bproj = jnp.sum(grad_out_wide, axis=0)
    g_bout = jnp.sum(grad_middle, axis=0)
    grad_low = grad_middle.astype(bf16)
    g_out = tn(grad_low, attended).astype(bf16)
    grad_attended = nn(grad_low, out_all).astype(bf16)
    zeros = jnp.zeros((width,), f32)
    small = [zeros, zeros, zeros, zeros, g_bout, g_ln2_gain, g_ln2_bias, g_bfc, g_bproj]
    if near:
        flat = jnp.concatenate(small).reshape(-1, 128)
        *outs, summed, grad_input = back_near(
            [g_out, g_fc, g_proj], packed, attended, p, inv, grad_attended, normed_first.T, qkv_all,
            x_own, grad_middle, ln1_gain, flat, shard,
        )
    else:
        grad_packed, sums = attend_backward(packed, attended, p, inv, grad_attended)
        g_qkv = tn(normed_first, grad_packed).astype(bf16)
        grad_normed = nt(grad_packed, qkv_all)
        back, g_ln1_gain, g_ln1_bias = norm_backward(grad_normed, centred_first, inverse_first, ln1_gain)
        grad_input = back_micro((grad_middle + back).astype(bf16))
        small[:4] = [g_ln1_gain, g_ln1_bias, sums[:, 0, 0].reshape(-1), sums[:, 1, 0].reshape(-1)]
        outs, summed = reduce_far([g_qkv, g_out, g_fc, g_proj], jnp.concatenate(small))
    out_qkv, out_out, out_fc, out_proj = outs
    summed = summed.reshape(-1)
    kept = []
    at = 0
    for vector in small:
        size = vector.shape[0] // 2
        kept.append(lax.dynamic_slice_in_dim(summed, at + col * size, size, 0))
        at += vector.shape[0]
    return (
        layer_out,
        grad_input,
        kept[0],
        kept[1],
        out_qkv.reshape(shard, -1, 3, PAIR).transpose(0, 2, 1, 3).reshape(shard, 3, half_width),
        kept[2],
        kept[3],
        out_out.T,
        kept[4],
        kept[5],
        kept[6],
        out_fc,
        kept[7],
        out_proj.T,
        kept[8],
    )


def solution(mesh):
    placed = (
        P(None, "row", "col"), P(None, "row", None), P(None, "row", None), P("col"), P("col"),
        P("row", None, "col"), P("col"), P("col"), P("col", "row"), P("col"), P("col"), P("col"),
        P("row", "col"), P("col"), P("col", "row"), P("col"), P(None, "row", "col"),
    )
    near = mesh.shape["row"] == 16
    return jax.shard_map(
        partial(body, near),
        mesh=mesh,
        in_specs=placed,
        out_specs=(
            P(None, "row", "col"), P(None, "row", "col"), P("col"), P("col"), P("row", None, "col"),
            P("col"), P("col"), P("col", "row"), P("col"), P("col"), P("col"), P("row", "col"),
            P("col"), P("col", "row"), P("col"),
        ),
        check_vma=False,
    )
```

```python
from functools import partial

import jax
import jax.numpy as jnp
from jax import lax
from jax.experimental import pallas as pl
from jax.experimental.pallas import tpu as pltpu
from jax.sharding import PartitionSpec as P

HEAD = 64
IMG = 256
epsilon = 1e-05
bf16 = jnp.bfloat16
f32 = jnp.float32
GELU_A = 0.7978845608028654
GELU_B = 0.044715
PAIR = 2 * HEAD


def nn(a, b):
    return lax.dot_general(a, b, (((1,), (0,)), ((), ())), preferred_element_type=f32)


def nt(a, b):
    return lax.dot_general(a, b, (((1,), (1,)), ((), ())), preferred_element_type=f32)


def tn(a, b):
    return lax.dot_general(a, b, (((0,), (0,)), ((), ())), preferred_element_type=f32)


def half_bias(start, kind, part, half):
    base = part * half
    rows = lax.broadcasted_iota(jnp.int32, (half, half), 0) + base
    cols = lax.broadcasted_iota(jnp.int32, (half, half), 1) + base
    first = jnp.where(kind == 1, start, 4 * half)
    joined = (rows >= first) & (rows < first + IMG) & (cols >= first) & (cols < first + IMG)
    return jnp.where((cols <= rows) | joined, 0.0, -1e30).astype(f32)


def lane_masks(rows):
    lane = lax.broadcasted_iota(jnp.int32, (rows, PAIR), 1)
    return lane < HEAD


def attend_pair(qkv_ref, o_ref, p_ref, inv_ref, bias_ref):
    half = qkv_ref.shape[0] // 2
    q_ref, k_ref, v_ref = (qkv_ref.at[:, i * PAIR : (i + 1) * PAIR] for i in range(3))
    low = lane_masks(half)
    for part in range(2):
        rows = slice(part * half, (part + 1) * half)
        q = q_ref[rows, :] * jnp.asarray(0.125, bf16)
        zero = jnp.zeros_like(q)
        outs = []
        invs = []
        for head in range(2):
            mine = low if head == 0 else jnp.logical_not(low)
            qh = jnp.where(mine, q, zero)
            own = nt(qh, k_ref[rows, :]) + bias_ref[part]
            largest = jnp.max(own, axis=1, keepdims=True)
            if part == 1:
                before = nt(qh, k_ref[:half, :])
                largest = jnp.maximum(largest, jnp.max(before, axis=1, keepdims=True))
            own = jnp.exp(own - largest)
            total = jnp.sum(own, axis=1, keepdims=True)
            own = own.astype(bf16)
            p_ref[:, (3 * head + 2 * part) * half : (3 * head + 2 * part + 1) * half] = own
            out = nn(own, v_ref[rows, :])
            if part == 1:
                before = jnp.exp(before - largest)
                total = total + jnp.sum(before, axis=1, keepdims=True)
                before = before.astype(bf16)
                p_ref[:, (3 * head + 1) * half : (3 * head + 2) * half] = before
                out = out + nn(before, v_ref[:half, :])
            inv = 1.0 / total
            outs.append(out * inv)
            invs.append(inv)
        o_ref[rows, :] = jnp.where(low, outs[0], outs[1]).astype(bf16)
        inv_ref[rows, :] = jnp.where(low, invs[0], invs[1])


def attend_forward_kernel(span_ref, qkv_ref, o_ref, p_ref, inv_ref, bias_ref):
    half = qkv_ref.shape[0] // 2

    @pl.when(pl.program_id(0) == 0)
    def _():
        for part in range(2):
            bias_ref[part] = half_bias(span_ref[0, part], span_ref[1, part], part, half)

    attend_pair(qkv_ref, o_ref, p_ref.at[0], inv_ref, bias_ref)


def attend_forward(packed, spans):
    length = packed.shape[0]
    width = packed.shape[1] // 3
    pairs = width // PAIR
    half = length // 2
    return pl.pallas_call(
        attend_forward_kernel,
        grid=(pairs,),
        in_specs=[
            pl.BlockSpec(memory_space=pltpu.SMEM),
            pl.BlockSpec((length, 3 * PAIR), lambda j: (0, j)),
        ],
        out_specs=[
            pl.BlockSpec((length, PAIR), lambda j: (0, j)),
            pl.BlockSpec((1, half, 6 * half), lambda j: (j, 0, 0)),
            pl.BlockSpec((length, PAIR), lambda j: (0, j)),
        ],
        out_shape=[
            jax.ShapeDtypeStruct((length, width), bf16),
            jax.ShapeDtypeStruct((pairs, half, 6 * half), bf16),
            jax.ShapeDtypeStruct((length, width), f32),
        ],
        scratch_shapes=[pltpu.VMEM((2, half, half), f32)],
        compiler_params=pltpu.CompilerParams(vmem_limit_bytes=60 << 20),
        cost_estimate=pl.CostEstimate(
            flops=4 * 3 * half * half * width * 4, bytes_accessed=24 << 20, transcendentals=3 * half * half * 12
        ),
        name="attend_forward",
    )(spans, packed)


def attend_back_pair(qkv_ref, o_ref, p_ref, inv_ref, g_ref, sum_ref):
    length = qkv_ref.shape[0]
    half = length // 2
    low = lane_masks(half)
    q_ref, k_ref, v_ref = (qkv_ref.at[:, i * PAIR : (i + 1) * PAIR] for i in range(3))
    dks = [None, None]
    dvs = [None, None]
    dqs = []

    def add(total, part, value):
        total[part] = value if total[part] is None else total[part] + value

    for part in range(2):
        rows = slice(part * half, (part + 1) * half)
        inv = inv_ref[rows, :]
        g = g_ref[rows, :].astype(f32) * inv
        scaled = g * o_ref[rows, :].astype(f32)
        q = q_ref[rows, :]
        gb = g.astype(bf16)
        zero = jnp.zeros_like(gb)
        dq = None
        for head in range(2):
            mine = low if head == 0 else jnp.logical_not(low)
            gh = jnp.where(mine, gb, zero)
            qh = jnp.where(mine, q, zero)
            rowdot = jnp.sum(jnp.where(mine, scaled, 0.0), axis=1, keepdims=True)
            for kpart in range(part + 1):
                krows = slice(kpart * half, (kpart + 1) * half)
                at = (3 * head + part + kpart) * half
                p = p_ref[:, at : at + half]
                kh = jnp.where(mine, k_ref[krows, :], zero)
                dp = nt(gh, v_ref[krows, :])
                ds = (p.astype(f32) * (dp - rowdot)).astype(bf16)
                term = nn(ds, kh)
                dq = term if dq is None else dq + term
                add(dks, kpart, tn(ds, qh))
                add(dvs, kpart, tn(p, gh))
        dqs.append(dq)
    for which, (ref, values, scale) in enumerate(((q_ref, dqs, 0.125), (k_ref, dks, 0.125), (v_ref, dvs, 1.0))):
        total = None
        for part in range(2):
            value = (values[part] * scale).astype(bf16)
            ref[part * half : (part + 1) * half, :] = value
            term = jnp.sum(value.astype(f32), axis=0, keepdims=True)
            total = term if total is None else total + term
        if which != 1:
            sum_ref[which // 2] = total


def attend_backward_kernel(qkv_ref, o_ref, p_ref, inv_ref, g_ref, d_ref, sum_ref):
    d_ref[...] = qkv_ref[...]
    attend_back_pair(d_ref, o_ref, p_ref.at[0], inv_ref, g_ref, sum_ref.at[0])


def attend_backward(packed, attended, p, inv, grad_attended):
    length = packed.shape[0]
    width = packed.shape[1] // 3
    pairs = width // PAIR
    half = length // 2
    one = pl.BlockSpec((length, PAIR), lambda j: (0, j))
    three = pl.BlockSpec((length, 3 * PAIR), lambda j: (0, j))
    return pl.pallas_call(
        attend_backward_kernel,
        grid=(pairs,),
        in_specs=[three, one, pl.BlockSpec((1, half, 6 * half), lambda j: (j, 0, 0)), one, one],
        out_specs=[three, pl.BlockSpec((1, 2, 1, PAIR), lambda j: (j, 0, 0, 0))],
        out_shape=[
            jax.ShapeDtypeStruct(packed.shape, bf16),
            jax.ShapeDtypeStruct((pairs, 2, 1, PAIR), f32),
        ],
        compiler_params=pltpu.CompilerParams(vmem_limit_bytes=56 << 20),
        name="attend_backward",
    )(packed, attended, p, inv, grad_attended)


SWAP = [(0, 1), (1, 0)]


def swap(value):
    return lax.ppermute(value, "col", SWAP)


def ordered(mine, other, axis):
    first = lax.axis_index("col") == 0
    low = jnp.where(first, mine, other)
    high = jnp.where(first, other, mine)
    return jnp.concatenate([low, high], axis=axis)


def own_micro(halves):
    col = lax.axis_index("col")
    mine = lax.dynamic_index_in_dim(halves, col, 0, keepdims=False)
    other = swap(lax.dynamic_index_in_dim(halves, 1 - col, 0, keepdims=False))
    return ordered(mine, other, 1)


def back_micro(full):
    col = lax.axis_index("col")
    half = full.shape[1] // 2
    mine = lax.dynamic_slice_in_dim(full, col * half, half, 1)
    other = swap(lax.dynamic_slice_in_dim(full, (1 - col) * half, half, 1))
    first = col == 0
    return jnp.stack([jnp.where(first, mine, other), jnp.where(first, other, mine)])


G0_ORDERS = ("xzy", "xzy", "xyz")
REST_ORDERS = ("zxy", "zxy", "xyz")
MIDDLE_CUT = (5 / 15, 6 / 15)
GATHER_CUT = (4 / 12, 4 / 12)
REDUCE_CUT = (10 / 27, 11 / 27)


MESH = pl.DeviceIdType.MESH
DEPTH = 4
WAYS = ("up", "down", "y", "x", "core")
SIZES = {"z": DEPTH, "y": 2, "x": 2}


def row_of(z, y, core):
    return z * 4 + y * 2 + core


def my_place():
    row = lax.axis_index("row")
    return row // 4, (row // 2) % 2, row % 2, lax.axis_index("col")


def maybe(cond, act):
    if cond is None:
        act()
    else:
        pl.when(cond)(act)


def remote(src, dst, send, recv, device):
    return pltpu.make_async_remote_copy(
        src_ref=src, dst_ref=dst, send_sem=send, recv_sem=recv, device_id=device, device_id_type=MESH
    )


def greet(always, z, up, down):
    barrier = pltpu.get_barrier_semaphore()

    def hello(device):
        pl.semaphore_signal(barrier, inc=1, device_id=device, device_id_type=MESH)

    for device in always:
        hello(device)
    pl.when(z < DEPTH - 1)(lambda: hello(up))
    pl.when(z > 0)(lambda: hello(down))
    pl.semaphore_wait(
        barrier, len(always) + (z < DEPTH - 1).astype(jnp.int32) + (z > 0).astype(jnp.int32)
    )


def tree_rounds(order):
    rounds = {}
    for dz in (0, -1, 1, -2, 2, -3, 3):
        for dy in (0, 1):
            for dx in (0, 1):
                step = {"z": dz, "y": dy, "x": dx}
                via = None
                for axis in order:
                    if step[axis]:
                        via = axis
                onward = []
                open_now = via is None
                for axis in order:
                    if axis == via:
                        open_now = True
                    if not open_now:
                        continue
                    if axis == "z":
                        onward += ["up"] if dz <= 0 else []
                        onward += ["down"] if dz >= 0 else []
                    elif axis != via:
                        onward.append(axis)
                onward.append("core")
                rounds.setdefault(abs(dz) + dy + dx, []).append((dz, dy, dx, onward))
    return rounds


def pieces_of(widths, cuts):
    found = []
    for part in range(3):
        base = 0
        for weight, width in enumerate(widths):
            lo = max(base, cuts[part])
            hi = min(base + width, cuts[part + 1])
            if hi > lo:
                found.append((part, weight, lo - cuts[part], lo - base, hi - lo))
            base += width
    return found


class Gatherer:
    def __init__(self, place, shards, widths, cuts, orders, scratch):
        self.z, self.y, self.core, self.x = place
        z, y, core, x = place
        self.shards, self.widths = shards, widths
        self.by_pairs = len(scratch) == 4
        self.whole = scratch[0]
        self.bufs = [scratch[0].at[part] for part in range(3)] if self.by_pairs else scratch[:3]
        self.send, self.recv, self.local = scratch[-3:]
        self.near = {
            "up": (row_of(z + 1, y, core), x),
            "down": (row_of(z - 1, y, core), x),
            "y": (row_of(z, 1 - y, core), x),
            "x": (row_of(z, y, core), 1 - x),
            "core": (row_of(z, y, 1 - core), x),
        }
        self.has = {"up": z < DEPTH - 1, "down": z > 0}
        self.orders = orders
        self.pieces = pieces_of(widths, cuts)
        self.trees = [tree_rounds(order) for order in orders]

    @staticmethod
    def scratch_shapes(cuts, rows, by_pairs):
        dma = pltpu.SemaphoreType.DMA
        if by_pairs:
            bufs = [pltpu.VMEM((3, 2, 16, rows, 3 * PAIR), bf16)]
        else:
            bufs = [pltpu.VMEM((2, 16, rows, cuts[i + 1] - cuts[i]), bf16) for i in range(3)]
        return bufs + [
            dma((3, 5)),
            dma((3, 17)),
            dma((3, 6)),
        ]

    def loads(self):
        row = row_of(self.z, self.y, self.core)
        if self.by_pairs:
            return [
                pltpu.make_async_copy(
                    self.shards[0].at[which, :, pl.ds(part * PAIR, PAIR)],
                    self.bufs[part].at[self.x, row, :, pl.ds(which * PAIR, PAIR)],
                    self.local.at[which, part],
                )
                for part in range(3)
                for which in range(3)
            ]
        return [
            pltpu.make_async_copy(
                self.shards[weight].at[:, pl.ds(src, width)],
                self.bufs[part].at[self.x, row, :, pl.ds(at, width)],
                self.local.at[0, i],
            )
            for i, (part, weight, at, src, width) in enumerate(self.pieces)
        ]

    def copy(self, part, bz, by, bx, way):
        block = self.bufs[part].at[bx, row_of(bz, by, self.core)]
        slot = 16 if way == "core" else bx * 8 + bz * 2 + by
        return remote(
            block, block, self.send.at[part, WAYS.index(way)], self.recv.at[part, slot], self.near[way]
        )

    def all_of(self, part, count, way):
        blocks = self.bufs[part].at[0, pl.ds(0, count)]
        return remote(
            blocks, blocks, self.send.at[part, WAYS.index(way)], self.recv.at[part, 16], self.near[way]
        )

    def each(self, step, act, parts=(0, 1, 2)):
        for part in parts:
            for dz, dy, dx, onward in self.trees[part].get(step, []):
                bz, by, bx = self.z + dz, (self.y + dy) % 2, (self.x + dx) % 2
                cond = None if dz == 0 else ((bz >= 0) & (bz <= DEPTH - 1))
                maybe(cond, lambda: act(part, bz, by, bx, onward))

    def forward(self, step, parts=(0, 1, 2)):
        def act(part, bz, by, bx, onward):
            if step:
                self.copy(part, bz, by, bx, "y").wait_recv()
            for way in onward:
                maybe(self.has.get(way), lambda way=way: self.copy(part, bz, by, bx, way).start())

        self.each(step, act, parts)

    def arrive(self, parts=(0, 1, 2)):
        for part in parts:
            self.all_of(part, 16, "core").wait_recv()

    def drain(self):
        for part in range(3):
            count = 1
            for axis in self.orders[part]:
                if axis == "z":
                    for at in range(DEPTH):

                        def act(part=part, at=at, count=count):
                            if at < DEPTH - 1:
                                self.all_of(part, count * (at + 1), "up").wait_send()
                            if at > 0:
                                self.all_of(part, count * (DEPTH - at), "down").wait_send()

                        pl.when(self.z == at)(act)
                else:
                    self.all_of(part, count, axis).wait_send()
                count *= SIZES[axis]
            self.all_of(part, count, "core").wait_send()

    def stores(self, outs):
        return [
            pltpu.make_async_copy(
                self.bufs[part].at[side, :, :, pl.ds(at, width)],
                outs[weight].at[:, :, pl.ds(side * self.widths[weight] + src, width)],
                self.local.at[1 + side, i],
            )
            for i, (part, weight, at, src, width) in enumerate(self.pieces)
            for side in range(2)
        ]

    def weight(self, part, side, at, width):
        block = self.bufs[part][side, :, :, at : at + width]
        return block.reshape(-1, width)


def begin(copies):
    for copy in copies:
        copy.start()


def end(copies):
    for copy in copies:
        copy.wait()


FORWARD_ORDER = (0, 3, 1, 4, 2, 5)
ROWS = 256


def front_kernel(shape, *refs):
    w_qkv, w_out, w_fc, w_proj, x_in, cot, starts, kinds = refs[:8]
    vectors = refs[8:17]
    (
        o_qkv, o_out, o_fc, o_proj, o_x, o_cot, o_vec, o_packed, o_p, o_inv, o_att, o_normed, o_middle, o_second,
        o_active, o_slope,
    ) = refs[17:33]
    scr = refs[33:]
    place = my_place()
    z, y, core, x = place
    one, two, three = (
        Gatherer(place, shards, *shape["groups"][i], scr[6 * i - 2 * (i > 0) : 6 * i + 4])
        for i, shards in enumerate(([w_qkv], [w_out, w_fc], [w_proj]))
    )
    (
        xm, xo, cm, xf, n1, pk, big, ib, att, bias, mid, n2, shifts, s_x, r_x, s_c, r_c, s_v, r_v, s_in, s_pair, s_end,
    ) = scr[16:-9]
    vec_o = scr[-9:]
    length, half_width = xm.shape
    width = 2 * half_width
    half = length // 2
    blocks = length // ROWS
    to_x = one.near["x"]

    def x_copy(i):
        span = pl.ds(i * ROWS, ROWS)
        return remote(x_in.at[1 - x, span], xo.at[span], s_x.at[i], r_x.at[i], to_x)

    own_cols = pl.ds(pl.multiple_of(x * half_width, PAIR), half_width)

    def cot_copy(i):
        span = pl.ds(i * ROWS, ROWS)
        return remote(cot.at[1 - x, span], o_cot.at[span, own_cols], s_c.at[i], r_c.at[i], to_x)

    vec_at = [sum(shape["vectors"][:k]) for k in range(9)]
    vec_copies = [
        remote(vector, vec_o[k], s_v.at[k], r_v.at[k], to_x) for k, vector in enumerate(vectors)
    ]
    own_x = pltpu.make_async_copy(x_in.at[x], xm, s_in.at[0])
    own_cot = pltpu.make_async_copy(cot.at[x], cm, s_in.at[1])
    put_cot = pltpu.make_async_copy(cm, o_cot.at[:, own_cols], s_in.at[2])
    begin(one.loads())
    own_x.start()
    begin(two.loads())
    begin(three.loads())
    own_cot.start()
    greet([to_x, one.near["y"], one.near["core"]], z, one.near["up"], one.near["down"])
    begin(vec_copies)
    end(one.loads())
    one.forward(0)
    begin([x_copy(i) for i in range(blocks)])
    for part in range(2):
        bias[part] = half_bias(starts[x, 0, part], kinds[x, 0, part], part, half)
    one.forward(1)
    end(two.loads())
    end(three.loads())
    one.forward(2)
    two.forward(0)
    end(vec_copies)
    is_low = x == 0
    full = []
    for vector, brought, at, size in zip(vectors, vec_o, vec_at, shape["vectors"]):
        mine, other = vector[...].reshape(1, size), brought[...].reshape(1, size)
        low, high = jnp.where(is_low, mine, other), jnp.where(is_low, other, mine)
        o_vec[:, 2 * at : 2 * at + size] = low
        o_vec[:, 2 * at + size : 2 * at + 2 * size] = high
        full.append(slice(2 * at, 2 * at + 2 * size))
    own_x.wait()

    def norm(value, gain, shift):
        average = jnp.sum(value, axis=1, keepdims=True) / width
        square = jnp.sum(value * value, axis=1, keepdims=True) / width
        inverse = lax.rsqrt(square - average * average + epsilon)
        return ((value - average) * inverse * o_vec[:, full[gain]] + o_vec[:, full[shift]]).astype(bf16)

    def first_norm(i):
        span = slice(i * ROWS, (i + 1) * ROWS)
        x_copy(i).wait_recv()
        mine, other = xm[span, :], xo[span, :]
        xf[span, :half_width] = jnp.where(is_low, mine, other)
        xf[span, half_width:] = jnp.where(is_low, other, mine)
        n1[span, :] = norm(xf[span, :].astype(f32), 0, 1)

    one.forward(3)
    first_norm(0)
    first_norm(1)
    one.forward(4)
    first_norm(2)
    one.forward(5)
    first_norm(3)
    two.forward(1)
    to_x_out = pltpu.make_async_copy(xf, o_x, s_end.at[0])
    to_normed = pltpu.make_async_copy(n1, o_normed, s_end.at[1])
    begin([to_x_out, to_normed])

    def pair_puts(j, step):
        wide = pl.ds(pl.multiple_of(3 * PAIR * j, PAIR), 3 * PAIR)
        cols = pl.ds(pl.multiple_of(PAIR * j, PAIR), PAIR)
        return [
            pltpu.make_async_copy(pk.at[j], o_packed.at[:, wide], s_pair.at[0]),
            pltpu.make_async_copy(big.at[step], o_p.at[j], s_pair.at[1]),
            pltpu.make_async_copy(ib.at[j], o_inv.at[:, cols], s_pair.at[2]),
            pltpu.make_async_copy(att.at[j], o_att.at[:, cols], s_pair.at[3]),
        ]

    def serve_0():
        two.forward(2)
        one.arrive((1,))

    def serve_1():
        two.forward(3)
        three.forward(0)

    def serve_2():
        two.forward(4)
        cot_copy(0).start()
        one.arrive((2,))
        begin(one.stores([o_qkv]))

    def serve_3():
        two.forward(5)
        three.forward(1)
        cot_copy(1).start()
        own_cot.wait()
        put_cot.start()

    def serve_4():
        three.forward(2)
        cot_copy(2).start()

    def serve_5():
        three.forward(3)
        cot_copy(3).start()

    serves = (serve_0, serve_1, serve_2, serve_3, serve_4, serve_5)
    for j in range(6):
        for k, vector in ((0, 2), (2, 3)):
            cols = slice(full[vector].start + PAIR * j, full[vector].start + PAIR * (j + 1))
            shifts[j, :, k * PAIR : (k + 1) * PAIR] = o_vec[:, cols]
        shifts[j, :, PAIR : 2 * PAIR] = jnp.zeros((1, PAIR), f32)

    def pair(step, carry):
        part, side = step // 2, step % 2
        j = 3 * side + part
        weight = one.whole[part, side].reshape(width, 3 * PAIR)
        pk[j] = (nn(n1[...], weight) + shifts[j]).astype(bf16)
        attend_pair(pk.at[j], att.at[j], big.at[step], ib.at[j], bias)
        begin(pair_puts(j, step))
        for k, serve in enumerate(serves):
            pl.when(step == k)(serve)
        return carry

    one.arrive((0,))
    lax.fori_loop(0, 6, pair, 0)
    qkv_stores = one.stores([o_qkv])
    two.arrive()
    two_stores = two.stores([o_out, o_fc])
    begin(two_stores)
    out_pieces = [p for p in two.pieces if p[1] == 0]
    fc_pieces = [p for p in two.pieces if p[1] == 1]

    def second(i, carry):
        span = pl.ds(pl.multiple_of(i * ROWS, ROWS), ROWS)
        total = xf[span, :].astype(f32) + o_vec[:, full[4]]
        rows = jnp.concatenate([att[j, span, :] for j in range(6)], axis=1)
        for part, _, at, src, w in out_pieces:
            for side in range(2):
                cols = slice(side * half_width + src, side * half_width + src + w)
                total = total + nt(rows[:, cols], two.weight(part, side, at, w))
        mid[span, :] = total
        n2[span, :] = norm(total, 5, 6)
        return carry

    lax.fori_loop(0, blocks, second, 0)
    for step in range(6):
        end(pair_puts(3 * (step % 2) + step // 2, step))
    to_mid = pltpu.make_async_copy(mid, o_middle, s_end.at[3])
    to_second = pltpu.make_async_copy(n2, o_second, s_end.at[4])
    begin([to_mid, to_second])
    three.forward(4)
    ff_half = two.widths[1]
    puts = []
    for k, ((part, _, at, src, w), side) in enumerate([(p, side) for p in fc_pieces for side in range(2)]):
        cols = slice(side * ff_half + src, side * ff_half + src + w)
        b_cols = slice(full[7].start + cols.start, full[7].start + cols.stop)

        def block(i, carry):
            span = pl.ds(pl.multiple_of(i * ROWS, ROWS), ROWS)
            hidden = nn(n2[span, :], two.weight(part, side, at, w)) + o_vec[:, b_cols]
            squared = hidden * hidden
            tanh = jnp.tanh(hidden * (GELU_A + (GELU_A * GELU_B) * squared))
            gate = 0.5 + 0.5 * tanh
            here = pl.ds(pl.multiple_of((i % 2) * ROWS, ROWS), ROWS)
            big[i // 2, here, cols] = (hidden * gate).astype(bf16)
            inner = hidden * (GELU_A + (3.0 * GELU_A * GELU_B) * squared)
            big[2 + i // 2, here, cols] = (gate + inner * (0.5 - 0.5 * tanh * tanh)).astype(bf16)
            return carry

        lax.fori_loop(0, blocks, block, 0)
        now = [
            pltpu.make_async_copy(big.at[0:2, :, cols], o_active.at[:, :, cols], s_end.at[5 + 2 * k]),
            pltpu.make_async_copy(big.at[2:4, :, cols], o_slope.at[:, :, cols], s_end.at[6 + 2 * k]),
        ]
        begin(now)
        puts += now
        if k == 1:
            three.forward(5)
    three.arrive()
    three_stores = three.stores([o_proj])
    begin(three_stores)
    one.drain()
    two.drain()
    three.drain()
    for i in range(blocks):
        x_copy(i).wait_send()
    for i in range(blocks):
        cot_copy(i).wait()
    end([put_cot, to_x_out, to_normed, to_mid, to_second] + puts)
    end(qkv_stores)
    end(two_stores)
    end(three_stores)


def front_near(shards, x_in, cot, vectors, starts, kinds):
    rows = shards[1].shape[0]
    widths = [3 * shards[0].shape[2]] + [shard.shape[1] for shard in shards[1:]]
    _, length, half_width = x_in.shape
    width = 2 * half_width
    half = length // 2
    pairs = width // PAIR
    groups = [
        (widths[:1], [0, 3 * PAIR, 6 * PAIR, 9 * PAIR], G0_ORDERS),
        (widths[1:3], part_cuts(widths[1:3], *MIDDLE_CUT), REST_ORDERS),
        (widths[3:], part_cuts(widths[3:], *GATHER_CUT), REST_ORDERS),
    ]
    ff = 2 * widths[2]
    sizes = [v.shape[0] for v in vectors]
    shape = {"groups": groups, "vectors": sizes}
    dma = pltpu.SemaphoreType.DMA
    scratch = []
    for i, (_, cuts, _) in enumerate(groups):
        scratch += Gatherer.scratch_shapes(cuts, rows, i == 0)
    scratch += [
        pltpu.VMEM((length, half_width), bf16),
        pltpu.VMEM((length, half_width), bf16),
        pltpu.VMEM((length, half_width), bf16),
        pltpu.VMEM((length, width), bf16),
        pltpu.VMEM((length, width), bf16),
        pltpu.VMEM((pairs, length, 3 * PAIR), bf16),
        pltpu.VMEM((pairs, half, 6 * half), bf16),
        pltpu.VMEM((pairs, length, PAIR), f32),
        pltpu.VMEM((pairs, length, PAIR), bf16),
        pltpu.VMEM((2, half, half), f32),
        pltpu.VMEM((length, width), f32),
        pltpu.VMEM((length, width), bf16),
        pltpu.VMEM((pairs, 1, 3 * PAIR), f32),
    ]
    scratch += [dma((4,)), dma((4,)), dma((4,)), dma((4,)), dma((9,)), dma((9,)), dma((3,)), dma((4,)), dma((17,))]
    scratch += [pltpu.VMEM((size,), f32) for size in sizes]
    any_space = pl.BlockSpec(memory_space=pl.ANY)
    vmem = pl.BlockSpec(memory_space=pltpu.VMEM)
    smem = pl.BlockSpec(memory_space=pltpu.SMEM)

    def out(dims, kind=bf16):
        return jax.ShapeDtypeStruct(dims, kind)

    outs = pl.pallas_call(
        lambda *refs: front_kernel(shape, *refs),
        in_specs=[any_space] * 6 + [smem, smem] + [vmem] * 9,
        out_specs=[any_space] * 6 + [vmem] + [any_space] * 9,
        out_shape=[out((16, rows, 2 * w)) for w in widths]
        + [
            out((length, width)),
            out((length, width)),
            out((1, 2 * sum(sizes)), f32),
            out((length, 3 * width)),
            out((pairs, half, 6 * half)),
            out((length, width), f32),
            out((length, width)),
            out((length, width)),
            out((length, width), f32),
            out((length, width)),
            out((2, half, ff)),
            out((2, half, ff)),
        ],
        scratch_shapes=scratch,
        compiler_params=pltpu.CompilerParams(
            collective_id=0, has_side_effects=True, vmem_limit_bytes=67043328
        ),
        cost_estimate=pl.CostEstimate(flops=20 << 30, bytes_accessed=200 << 20, transcendentals=0),
        name="gather_weights",
    )(*shards, x_in, cot, starts, kinds, *vectors)
    full = [w.reshape(16 * rows, -1) for w in outs[:4]]
    vec = outs[6].reshape(-1)
    at = 0
    fulls = []
    for size in sizes:
        fulls.append(vec[at : at + 2 * size])
        at += 2 * size
    saved = list(outs[7:14]) + [out.reshape(length, ff) for out in outs[14:]]
    return full, list(outs[4:6]), fulls, saved


class Reducer:
    def __init__(self, place, grads, widths, cuts, scratch):
        self.z, self.y, self.core, self.x = place
        z, y, core, x = place
        self.grads = grads
        self.widths = widths
        self.acc, self.rcore = scratch[0:3], scratch[3:6]
        rx, ry, self.rz, self.cy, self.cx = scratch[6:8], scratch[8:10], scratch[10:13], scratch[13], scratch[14]
        self.final = scratch[15:18]
        (
            self.s_core, self.r_core, self.s_one, self.r_one, self.s_two, self.r_two, self.s_z, self.r_z, self.s_c,
            self.r_c, self.s_load, self.s_out,
        ) = scratch[18:]
        self.up, self.down = (row_of(z + 1, y, core), x), (row_of(z - 1, y, core), x)
        self.to_y, self.to_x = (row_of(z, 1 - y, core), x), (row_of(z, y, core), 1 - x)
        self.to_core = (row_of(z, y, 1 - core), x)
        self.by_part = [[p for p in pieces_of(widths, cuts) if p[0] == part] for part in range(3)]
        self.first = [(rx[0], self.to_x), (ry[0], self.to_y)]
        self.second = [(ry[1], self.to_y), (rx[1], self.to_x)]

    SCRATCH = 30

    @staticmethod
    def scratch_shapes(widths, cuts, rows):
        w = [cuts[i + 1] - cuts[i] for i in range(3)]
        dma = pltpu.SemaphoreType.DMA

        def low(*shape):
            return pltpu.VMEM(shape, bf16)

        scratch = [low(2, 4, 2, rows, k) for k in w] * 2
        scratch += [low(4, 2, rows, w[0]), low(4, rows, w[1])]
        scratch += [low(4, 2, rows, w[1]), low(4, rows, w[0])]
        scratch += [low(2, 4, rows, w[0]), low(2, 4, rows, w[1]), low(2, 4, 2, 2, rows, w[2])]
        scratch += [low(2, rows, w[2]), low(rows, w[2])]
        scratch += [pltpu.VMEM((rows, k), f32) for k in w]
        scratch += [dma((3,)), dma((3, 2, 4)), dma((2,)), dma((2, 4)), dma((2,)), dma((2, 4))]
        scratch += [dma((3, 2, 4)), dma((3, 2, 4)), dma((2,)), dma((2,)), dma((3,)), dma((3, 3))]
        return scratch

    def cols(self, weight, side, src, width):
        return pl.ds(pl.multiple_of(side * self.widths[weight] + src, 128), width)

    def loop(self, act):
        def step(zi, carry):
            act(zi)
            return carry

        lax.fori_loop(0, DEPTH, step, 0)

    def add(self, total, term):
        total[...] = total[...] + term[...]

    def loads(self, part):
        return [
            pltpu.make_async_copy(
                self.grads[weight].at[:, :, self.core, :, self.cols(weight, side, src, width)],
                self.acc[part].at[side, :, :, :, pl.ds(at, width)],
                self.s_load.at[part],
            )
            for i, (_, weight, at, src, width) in enumerate(self.by_part[part])
            for side in range(2)
        ]

    def view(self, part, ref, far, zi):
        if part == 0:
            return ref.at[(1 - self.x) if far else self.x, zi]
        return ref.at[:, zi, (1 - self.y) if far else self.y]

    def core_copies(self, part, far, zi):
        other = 1 - self.core
        copies = []
        for i, (_, weight, at, src, width) in enumerate(self.by_part[part]):
            cols = pl.ds(at, width)
            if part == 0:
                sides = [(1 - self.x) if far else self.x]
            else:
                sides = [0, 1]
            for k, side in enumerate(sides):
                gcols = self.cols(weight, side, src, width)
                if part == 1:
                    by = (1 - self.y) if far else self.y
                    src_ref = self.grads[weight].at[zi, by, other, :, gcols]
                    dst_ref = self.rcore[1].at[side, zi, by, :, cols]
                else:
                    src_ref = self.grads[weight].at[zi, :, other, :, gcols]
                    dst_ref = self.rcore[part].at[side, zi, :, :, cols]
                copies.append(
                    remote(
                        src_ref, dst_ref, self.s_core.at[part], self.r_core.at[part, int(far), zi], self.to_core
                    )
                )
        return copies

    def core_wait(self, part, far, zi):
        if part == 2:
            blocks = self.rcore[2].at[:, zi]
        else:
            blocks = self.view(part, self.rcore[part], far, zi)
        remote(
            blocks, blocks, self.s_core.at[part], self.r_core.at[part, int(far), zi], self.to_core
        ).wait_recv()

    def start(self, parts):
        for part in parts:
            for load in self.loads(part):
                load.start()

        def begin(far):
            def act(zi):
                for part in parts:
                    if far or part < 2:
                        for copy in self.core_copies(part, far, zi):
                            copy.start()

            self.loop(act)

        begin(True)
        begin(False)

    def first_copy(self, part, zi):
        buf, device = self.first[part]
        return remote(
            self.view(part, self.acc[part], True, zi), buf.at[zi], self.s_one.at[part], self.r_one.at[part, zi], device
        )

    def half_of(self, part, zi, far):
        if part == 0:
            return self.acc[0].at[self.x, zi, (1 - self.y) if far else self.y]
        return self.acc[1].at[(1 - self.x) if far else self.x, zi, self.y]

    def second_copy(self, part, zi):
        buf, device = self.second[part]
        return remote(self.half_of(part, zi, True), buf.at[zi], self.s_two.at[part], self.r_two.at[part, zi], device)

    def far(self, parts):
        for part in parts:
            pltpu.make_async_copy(self.rcore[part], self.acc[part], self.s_load.at[part]).wait()

        def act(zi):
            for part in parts:
                self.core_wait(part, True, zi)
                if part == 2:
                    self.add(self.acc[2].at[:, zi], self.rcore[2].at[:, zi])
                else:
                    self.add(self.view(part, self.acc[part], True, zi), self.view(part, self.rcore[part], True, zi))
                    self.first_copy(part, zi).start()

        self.loop(act)

    def near(self, parts):
        def act(zi):
            for part in parts:
                self.core_wait(part, False, zi)
                mine = self.view(part, self.acc[part], False, zi)
                self.add(mine, self.view(part, self.rcore[part], False, zi))
                self.first_copy(part, zi).wait_recv()
                self.add(mine, self.first[part][0].at[zi])
                self.second_copy(part, zi).start()

        self.loop(act)

    def last(self, parts):
        def act(zi):
            for part in parts:
                self.second_copy(part, zi).wait_recv()
                self.add(self.half_of(part, zi, False), self.second[part][0].at[zi])

        self.loop(act)

    def block(self, part, zi):
        if part == 2:
            return self.acc[2].at[:, zi]
        return self.acc[part].at[self.x, zi, self.y]

    def line_copy(self, part, direction, zd):
        return remote(
            self.block(part, zd),
            self.rz[part].at[direction, zd],
            self.s_z.at[part, direction, zd],
            self.r_z.at[part, direction, zd],
            self.down if direction else self.up,
        )

    def line(self, parts, step):
        for direction in range(2):
            at = DEPTH - 1 - step if direction else step
            for zd in (0, 1, 2) if direction else (3, 2, 1):
                if not ((at > zd) if direction else (at < zd)):
                    continue
                for part in parts:

                    def act(part=part, direction=direction, zd=zd):
                        if step > 0:
                            self.line_copy(part, direction, zd).wait_recv()
                            self.add(self.block(part, zd), self.rz[part].at[direction, zd])
                        self.line_copy(part, direction, zd).start()

                    pl.when(self.z == at)(act)

    def line_end(self, parts):
        for part in parts:
            for direction in range(2):

                def act(part=part, direction=direction):
                    self.line_copy(part, direction, self.z).wait_recv()
                    self.add(self.block(part, self.z), self.rz[part].at[direction, self.z])

                pl.when((self.z < DEPTH - 1) if direction else (self.z > 0))(act)

    def y_copy(self):
        return remote(self.acc[2].at[:, self.z, 1 - self.y], self.cy, self.s_c.at[0], self.r_c.at[0], self.to_y)

    def x_copy(self):
        return remote(self.acc[2].at[1 - self.x, self.z, self.y], self.cx, self.s_c.at[1], self.r_c.at[1], self.to_x)

    def turn(self):
        self.y_copy().wait_recv()
        self.add(self.acc[2].at[:, self.z, self.y], self.cy)
        self.x_copy().start()

    def turn_end(self):
        self.x_copy().wait_recv()
        self.add(self.acc[2].at[self.x, self.z, self.y], self.cx)

    def stores(self, outs):
        if len(outs[0].shape) == 3:
            return [
                pltpu.make_async_copy(
                    self.final[part].at[:, pl.ds(which * PAIR, PAIR)],
                    outs[0].at[which, :, pl.ds(part * PAIR, PAIR)],
                    self.s_out.at[part, which],
                )
                for part in range(3)
                for which in range(3)
            ]
        return [
            pltpu.make_async_copy(
                self.final[part].at[:, pl.ds(at, width)], outs[weight].at[:, pl.ds(src, width)], self.s_out.at[part, i]
            )
            for part in range(3)
            for i, (_, weight, at, src, width) in enumerate(self.by_part[part])
        ]

    def finish(self, outs):
        for part in range(3):
            self.final[part][...] = self.acc[part][self.x, self.z, self.y].astype(f32)
        for store in self.stores(outs):
            store.start()

    def drain(self, outs):
        for part in range(3):
            remote(
                self.acc[part], self.rcore[part], self.s_core.at[part], self.r_core.at[part, 0, 0], self.to_core
            ).wait_send()
            for direction in range(2):
                for zd in range(DEPTH):
                    pl.when((self.z > zd) if direction else (self.z < zd))(
                        lambda part=part, direction=direction, zd=zd: self.line_copy(part, direction, zd).wait_send()
                    )
            if part < 2:
                for (buf, device), send, recv in (
                    (self.first[part], self.s_one, self.r_one),
                    (self.second[part], self.s_two, self.r_two),
                ):
                    remote(buf, buf, send.at[part], recv.at[part, 0], device).wait_send()
        self.y_copy().wait_send()
        self.x_copy().wait_send()
        for store in self.stores(outs):
            store.wait()


def back_kernel(shape, *refs):
    (
        g_out, g_fc, g_proj, packed, attended, p_all, inv_all, gatt, normed_t, w_qkv, x_all, middle, gain_ref, small_in,
        o_qkv, o_out, o_fc, o_proj, o_sum, o_input,
    ) = refs[:20]
    scr = refs[20:]
    first = Reducer.SCRATCH
    place = my_place()
    z, y, core, x = place
    early = Reducer(place, [g_out, g_fc, g_proj], shape["early"], shape["early_cuts"], scr[:first])
    qkv, o_buf, p_buf, inv_buf, g_buf, nt_buf, w_buf, x_buf, m_buf, gqkv, gi, col_sum, srecv, sacc, sums = scr[2 * first : 2 * first + 15]
    s_all, s_pair, s_mid, s_gi, r_gi, l_gi, s_s, r_s = scr[2 * first + 15 :]
    late = Reducer(place, [gqkv], shape["late"], shape["late_cuts"], scr[first : 2 * first])
    whole = [
        pltpu.make_async_copy(packed, qkv, s_all.at[0]),
        pltpu.make_async_copy(normed_t, nt_buf, s_all.at[1]),
        pltpu.make_async_copy(w_qkv, w_buf, s_all.at[2]),
        pltpu.make_async_copy(x_all, x_buf, s_all.at[3]),
    ]

    def pair_loads(step):
        j = (step // 2 + 2) % 3 + 3 * (step % 2)
        slot = step % 2
        cols = pl.ds(pl.multiple_of(j * PAIR, PAIR), PAIR)
        return [
            pltpu.make_async_copy(p_all.at[j], p_buf.at[slot], s_pair.at[slot, 0]),
            pltpu.make_async_copy(attended.at[:, cols], o_buf.at[slot], s_pair.at[slot, 1]),
            pltpu.make_async_copy(inv_all.at[:, cols], inv_buf.at[slot], s_pair.at[slot, 2]),
            pltpu.make_async_copy(gatt.at[:, cols], g_buf.at[slot], s_pair.at[slot, 3]),
        ]

    begin(whole[:1])
    begin(pair_loads(0))
    begin(whole[1:])
    to_z1 = (row_of(z + 1 - 2 * (z % 2), y, core), x)
    to_z2 = (row_of((z + 2) % 4, y, core), x)
    greet([early.to_core, early.to_x, early.to_y, to_z2], z, early.up, early.down)
    early.start((0, 1, 2))
    end(whole[:1])

    def pair(step, carry):
        j = (step // 2 + 2) % 3 + 3 * (step % 2)
        slot = step % 2
        pl.when(step < 5)(lambda: begin(pair_loads(step + 1)))
        end(pair_loads(step))
        cols = pl.ds(pl.multiple_of(3 * PAIR * j, PAIR), 3 * PAIR)
        attend_back_pair(qkv.at[:, cols], o_buf.at[slot], p_buf.at[slot], inv_buf.at[slot], g_buf.at[slot], col_sum.at[j])
        pl.when(step == 0)(lambda: end(whole[1:2]))
        grad = nn(nt_buf[...], qkv[:, cols]).astype(bf16)
        gqkv[:, :, :, :, cols] = grad.reshape(gqkv.shape[:4] + (3 * PAIR,))
        for k, serve in enumerate(serves):
            pl.when(step == k)(serve)
        return carry

    rows = m_buf.shape[1]
    blocks = x_buf.shape[0] // rows

    def mid_load(i):
        return pltpu.make_async_copy(middle.at[pl.ds(pl.multiple_of(i * rows, rows), rows)], m_buf.at[i % 2], s_mid.at[i % 2])

    def input_copies(i):
        span = pl.ds(pl.multiple_of(i * rows, rows), rows)
        return (
            pltpu.make_async_copy(gi.at[0, span], o_input.at[x, span], l_gi.at[i]),
            remote(gi.at[1, span], o_input.at[x, span], s_gi.at[i], r_gi.at[i], early.to_x),
        )

    def input_block(i):
        span = pl.ds(pl.multiple_of(i * rows, rows), rows)
        grad = nt(qkv[span, :], w_buf[...])
        pl.when(i + 1 < blocks)(lambda: mid_load(i + 1).start())
        mid_load(i).wait()
        value = x_buf[span, :].astype(f32)
        width = value.shape[1]
        average = jnp.sum(value, axis=1, keepdims=True) / width
        square = jnp.sum(value * value, axis=1, keepdims=True) / width
        inverse = lax.rsqrt(square - average * average + epsilon)
        centred = (value - average) * inverse
        scaled = grad * gain_ref[...]
        one = jnp.sum(scaled, axis=1, keepdims=True) / width
        two = jnp.sum(scaled * centred, axis=1, keepdims=True) / width
        out = m_buf[i % 2] + inverse * (scaled - one - centred * two)
        for k, term in enumerate((grad * centred, grad)):
            sums[k] = sums[k] + jnp.sum(term, axis=0, keepdims=True)
        half = width // 2
        is_low = x == 0
        gi[0, span, :] = jnp.where(is_low, out[:, :half], out[:, half:]).astype(bf16)
        gi[1, span, :] = jnp.where(is_low, out[:, half:], out[:, :half]).astype(bf16)
        for copy in input_copies(i):
            copy.start()

    partners = [early.to_core, early.to_x, early.to_y, to_z1, to_z2]

    def small_copy(step):
        return remote(sacc.at[step], srecv.at[step], s_s.at[step], r_s.at[step], partners[step])

    def small_start():
        sacc[0] = small_in[...]
        at = 0
        for k in range(2):
            for i in range(6):
                sacc[0, at : at + 1, :] = sums[k][:, i * PAIR : (i + 1) * PAIR]
                at += 1
        for k in range(2):
            for i in range(6):
                sacc[0, at : at + 1, :] = col_sum[i, k]
                at += 1
        small_copy(0).start()

    def small_next(step):
        small_copy(step).wait()
        sacc[step + 1] = sacc[step] + srecv[step]
        if step < 4:
            small_copy(step + 1).start()

    both = (0, 1)

    def serve_0():
        early.far((0, 1, 2))
        early.line((2,), 0)

    def serve_1():
        late.start((2,))

    def serve_2():
        early.line((2,), 1)

    def serve_3():
        late.start((0,))
        late.far((2,))
        early.line((2,), 2)
        late.line((2,), 0)
        mid_load(0).start()

    def serve_4():
        early.near(both)
        late.far((0,))

    def serve_5():
        late.start((1,))
        early.line_end((2,))
        early.y_copy().start()
        late.line((2,), 1)
        end(whole[2:])

    serves = (serve_0, serve_1, serve_2, serve_3, serve_4, serve_5)
    lax.fori_loop(0, 6, pair, 0)

    def block_0():
        early.last(both)
        early.line(both, 0)
        late.far((1,))
        late.line((2,), 2)

    def block_1():
        early.turn()
        early.line(both, 1)
        late.near((0,))
        late.line_end((2,))
        late.y_copy().start()

    def block_2():
        early.turn_end()
        early.line(both, 2)
        late.near((1,))
        late.turn()

    after = (block_0, block_1, block_2)
    sums[...] = jnp.zeros(sums.shape, f32)

    def input_step(i, carry):
        input_block(i)
        for k, serve in enumerate(after):
            pl.when(i == k)(serve)
        return carry

    lax.fori_loop(0, blocks, input_step, 0)
    small_start()
    late.last((0,))
    late.line((0,), 0)
    early.line_end(both)
    early.finish([o_out, o_fc, o_proj])
    small_next(0)
    late.last((1,))
    late.line((1,), 0)
    late.turn_end()
    late.line(both, 1)
    small_next(1)
    late.line(both, 2)
    small_next(2)
    late.line_end(both)
    late.finish([o_qkv])
    small_next(3)
    small_next(4)
    o_sum[...] = sacc[5]
    for i in range(blocks):
        local, other = input_copies(i)
        local.wait()
        other.wait()
    early.drain([o_out, o_fc, o_proj])
    late.drain([o_qkv])


def back_near(grads, packed, attended, p, inv, gatt, normed_t, w_qkv, x, middle, gain, small, rows):
    length, width = x.shape
    wide = packed.shape[1]
    early = [grad.shape[1] // 2 for grad in grads]
    shape = {"early": early, "early_cuts": part_cuts(early, *REDUCE_CUT), "late": [wide // 2]}
    shape["late_cuts"] = [0, wide // 6, wide // 3, wide // 2]
    dma = pltpu.SemaphoreType.DMA
    half = length // 2
    blocks = 4
    scratch = Reducer.scratch_shapes(early, shape["early_cuts"], rows)
    scratch += Reducer.scratch_shapes(shape["late"], shape["late_cuts"], rows)
    scratch += [
        pltpu.VMEM((length, wide), bf16),
        pltpu.VMEM((2, length, PAIR), bf16),
        pltpu.VMEM((2, half, 6 * half), bf16),
        pltpu.VMEM((2, length, PAIR), f32),
        pltpu.VMEM((2, length, PAIR), bf16),
        pltpu.VMEM((width, length), bf16),
        pltpu.VMEM((width, wide), bf16),
        pltpu.VMEM((length, width), bf16),
        pltpu.VMEM((2, length // blocks, width), f32),
        pltpu.VMEM((4, 2, 2, rows, wide), bf16),
        pltpu.VMEM((2, length, width // 2), bf16),
        pltpu.VMEM((width // PAIR, 2, 1, PAIR), f32),
        pltpu.VMEM((5,) + small.shape, f32),
        pltpu.VMEM((6,) + small.shape, f32),
        pltpu.VMEM((2, 1, width), f32),
    ]
    scratch += [dma((4,)), dma((2, 4)), dma((2,)), dma((4,)), dma((4,)), dma((4,)), dma((5,)), dma((5,))]
    shaped = [grad.reshape(4, 2, 2, rows, grad.shape[1]) for grad in grads]
    any_space = pl.BlockSpec(memory_space=pl.ANY)
    vmem = pl.BlockSpec(memory_space=pltpu.VMEM)
    outs = pl.pallas_call(
        lambda *refs: back_kernel(shape, *refs),
        in_specs=[any_space] * 12 + [vmem, vmem],
        out_specs=[any_space] * 4 + [vmem, any_space],
        out_shape=[jax.ShapeDtypeStruct((3, rows, wide // 6), f32)]
        + [jax.ShapeDtypeStruct((rows, w), f32) for w in early]
        + [jax.ShapeDtypeStruct(small.shape, f32), jax.ShapeDtypeStruct((2, length, width // 2), bf16)],
        scratch_shapes=scratch,
        compiler_params=pltpu.CompilerParams(
            collective_id=1, has_side_effects=True, vmem_limit_bytes=67043328
        ),
        cost_estimate=pl.CostEstimate(flops=30 << 30, bytes_accessed=200 << 20, transcendentals=0),
        name="reduce_grads",
    )(*shaped, packed, attended, p, inv, gatt, normed_t, w_qkv, x, middle, gain.reshape(1, -1), small)
    return outs


def gather_far(shards):
    fulls = []
    for shard in shards:
        rows = lax.all_gather(shard, ("col", "row"), axis=0, tiled=True)
        fulls.append(jnp.concatenate(jnp.split(rows, 2, axis=0), axis=1))
    return fulls


def reduce_far(grads, small):
    outs = []
    for grad in grads:
        halves = jnp.concatenate(jnp.split(grad, 2, axis=1), axis=0)
        outs.append(lax.psum_scatter(halves, ("col", "row"), scatter_dimension=0, tiled=True).astype(f32))
    return outs, lax.psum(small, ("row", "col"))


def part_cuts(widths, first, second):
    total = sum(widths) // 128
    one = round(total * first)
    two = round(total * (first + second))
    return [0, one * 128, two * 128, total * 128]


def layer_norm(value):
    width = value.shape[-1]
    average = jnp.sum(value, axis=-1, keepdims=True) / width
    square = jnp.sum(value * value, axis=-1, keepdims=True) / width
    inverse = lax.rsqrt(square - average * average + epsilon)
    return (value - average) * inverse, inverse


def norm_backward(grad, centred, inverse, gain):
    scaled = grad * gain
    first = jnp.mean(scaled, axis=-1, keepdims=True)
    second = jnp.mean(scaled * centred, axis=-1, keepdims=True)
    back = inverse * (scaled - first - centred * second)
    return back, jnp.sum(grad * centred, axis=0), jnp.sum(grad, axis=0)


def by_pairs(block):
    rows, three, half = block.shape
    return block.reshape(rows, three, half // PAIR, PAIR).transpose(0, 2, 1, 3).reshape(rows, three * half)


def body(
    near, x_in, span_start, span_kind, ln1_gain, ln1_bias, w_qkv, b_query, b_value, w_out, b_out,
    ln2_gain, ln2_bias, w_fc, b_fc, w_proj, b_proj, cotangent,
):
    half_width = x_in.shape[2]
    shard = w_qkv.shape[0]
    col = lax.axis_index("col")

    vectors = [ln1_gain, ln1_bias, b_query, b_value, b_out, ln2_gain, ln2_bias, b_fc, b_proj]
    shards = [w_out.T, w_fc, w_proj.T]
    width = 2 * half_width
    if near:
        weights, (x_own, grad_out), vectors, saved = front_near(
            [w_qkv.transpose(1, 0, 2)] + shards, x_in, cotangent, vectors, span_start, span_kind
        )
        qkv_all, out_all, fc_all, proj_all = weights
        ln1_gain, _, _, _, _, ln2_gain, _, _, b_proj = vectors
        packed, p, inv, attended, normed_first, middle, normed_second, active, slope = saved
        centred_second, inverse_second = layer_norm(middle)
    else:
        x_own = own_micro(x_in)
        residual = x_own.astype(f32)
        grad_out = own_micro(cotangent)
        qkv_all, out_all, fc_all, proj_all = gather_far([by_pairs(w_qkv)] + shards)
        flat = jnp.concatenate(vectors)
        flat_other = swap(flat)
        full = []
        at = 0
        for vector in vectors:
            full.append(ordered(vector, flat_other[at : at + vector.shape[0]], 0))
            at += vector.shape[0]
        ln1_gain, ln1_bias, b_query, b_value, b_out, ln2_gain, ln2_bias, b_fc, b_proj = full
        starts = lax.dynamic_index_in_dim(span_start, col, 0, keepdims=False)[0]
        kinds = lax.dynamic_index_in_dim(span_kind, col, 0, keepdims=False)[0]
        spans = jnp.stack([starts, kinds])
        centred_first, inverse_first = layer_norm(residual)
        normed_first = (centred_first * ln1_gain + ln1_bias).astype(bf16)
        bias = jnp.stack([b_query, jnp.zeros_like(b_query), b_value]).reshape(3, -1, PAIR)
        packed = (nn(normed_first, qkv_all) + bias.transpose(1, 0, 2).reshape(-1)).astype(bf16)
        attended, p, inv = attend_forward(packed, spans)
        middle = residual + nt(attended, out_all) + b_out
        centred_second, inverse_second = layer_norm(middle)
        normed_second = (centred_second * ln2_gain + ln2_bias).astype(bf16)
        hidden = nn(normed_second, fc_all) + b_fc
        squared = hidden * hidden
        tanh = jnp.tanh(GELU_A * hidden * (1.0 + GELU_B * squared))
        active = (0.5 * hidden * (1.0 + tanh)).astype(bf16)
        slope = (
            0.5 * (1.0 + tanh)
            + 0.5 * hidden * (1.0 - tanh * tanh) * GELU_A * (1.0 + 3.0 * GELU_B * squared)
        ).astype(bf16)
    layer_out = back_micro((middle + nt(active, proj_all) + b_proj).astype(bf16))

    grad_out_wide = grad_out.astype(f32)
    g_proj = tn(grad_out, active).astype(bf16)
    grad_hidden = (nn(grad_out, proj_all) * slope.astype(f32)).astype(bf16)
    g_fc = tn(normed_second, grad_hidden).astype(bf16)
    g_bfc = jnp.sum(grad_hidden.astype(f32), axis=0)
    grad_normed = nt(grad_hidden, fc_all)
    back, g_ln2_gain, g_ln2_bias = norm_backward(grad_normed, centred_second, inverse_second, ln2_gain)
    grad_middle = grad_out_wide + back
    g_bproj = jnp.sum(grad_out_wide, axis=0)
    g_bout = jnp.sum(grad_middle, axis=0)
    grad_low = grad_middle.astype(bf16)
    g_out = tn(grad_low, attended).astype(bf16)
    grad_attended = nn(grad_low, out_all).astype(bf16)
    zeros = jnp.zeros((width,), f32)
    small = [zeros, zeros, zeros, zeros, g_bout, g_ln2_gain, g_ln2_bias, g_bfc, g_bproj]
    if near:
        flat = jnp.concatenate(small).reshape(-1, 128)
        *outs, summed, grad_input = back_near(
            [g_out, g_fc, g_proj], packed, attended, p, inv, grad_attended, normed_first.T, qkv_all,
            x_own, grad_middle, ln1_gain, flat, shard,
        )
        outs[0] = outs[0].transpose(1, 0, 2)
    else:
        grad_packed, sums = attend_backward(packed, attended, p, inv, grad_attended)
        g_qkv = tn(normed_first, grad_packed).astype(bf16)
        grad_normed = nt(grad_packed, qkv_all)
        back, g_ln1_gain, g_ln1_bias = norm_backward(grad_normed, centred_first, inverse_first, ln1_gain)
        grad_input = back_micro((grad_middle + back).astype(bf16))
        small[:4] = [g_ln1_gain, g_ln1_bias, sums[:, 0, 0].reshape(-1), sums[:, 1, 0].reshape(-1)]
        outs, summed = reduce_far([g_qkv, g_out, g_fc, g_proj], jnp.concatenate(small))
        outs[0] = outs[0].reshape(shard, -1, 3, PAIR).transpose(0, 2, 1, 3).reshape(shard, 3, half_width)
    out_qkv, out_out, out_fc, out_proj = outs
    summed = summed.reshape(-1)
    kept = []
    at = 0
    for vector in small:
        size = vector.shape[0] // 2
        kept.append(lax.dynamic_slice_in_dim(summed, at + col * size, size, 0))
        at += vector.shape[0]
    return (
        layer_out,
        grad_input,
        kept[0],
        kept[1],
        out_qkv,
        kept[2],
        kept[3],
        out_out.T,
        kept[4],
        kept[5],
        kept[6],
        out_fc,
        kept[7],
        out_proj.T,
        kept[8],
    )


def solution(mesh):
    placed = (
        P(None, "row", "col"), P(None, "row", None), P(None, "row", None), P("col"), P("col"),
        P("row", None, "col"), P("col"), P("col"), P("col", "row"), P("col"), P("col"), P("col"),
        P("row", "col"), P("col"), P("col", "row"), P("col"), P(None, "row", "col"),
    )
    near = mesh.shape["row"] == 16
    return jax.shard_map(
        partial(body, near),
        mesh=mesh,
        in_specs=placed,
        out_specs=(
            P(None, "row", "col"), P(None, "row", "col"), P("col"), P("col"), P("row", None, "col"),
            P("col"), P("col"), P("col", "row"), P("col"), P("col"), P("col"), P("row", "col"),
            P("col"), P("col", "row"), P("col"),
        ),
        check_vma=False,
    )
```

```python
from functools import partial

import jax
import jax.numpy as jnp
from jax import lax
from jax.experimental import pallas as pl
from jax.experimental.pallas import tpu as pltpu
from jax.sharding import PartitionSpec as P

HEAD = 64
IMG = 256
epsilon = 1e-05
bf16 = jnp.bfloat16
f32 = jnp.float32
GELU_A = 0.7978845608028654
GELU_B = 0.044715
PAIR = 2 * HEAD


def nn(a, b):
    return lax.dot_general(a, b, (((1,), (0,)), ((), ())), preferred_element_type=f32)


def nt(a, b):
    return lax.dot_general(a, b, (((1,), (1,)), ((), ())), preferred_element_type=f32)


def tn(a, b):
    return lax.dot_general(a, b, (((0,), (0,)), ((), ())), preferred_element_type=f32)


def half_bias(start, kind, part, half):
    base = part * half
    rows = lax.broadcasted_iota(jnp.int32, (half, half), 0) + base
    cols = lax.broadcasted_iota(jnp.int32, (half, half), 1) + base
    first = jnp.where(kind == 1, start, 4 * half)
    joined = (rows >= first) & (rows < first + IMG) & (cols >= first) & (cols < first + IMG)
    return jnp.where((cols <= rows) | joined, 0.0, -1e30).astype(f32)


def lane_masks(rows):
    lane = lax.broadcasted_iota(jnp.int32, (rows, PAIR), 1)
    return lane < HEAD


def attend_pair(qkv_ref, o_ref, p_ref, inv_ref, bias_ref):
    half = qkv_ref.shape[0] // 2
    q_ref, k_ref, v_ref = (qkv_ref.at[:, i * PAIR : (i + 1) * PAIR] for i in range(3))
    low = lane_masks(half)
    for part in range(2):
        rows = slice(part * half, (part + 1) * half)
        q = q_ref[rows, :] * jnp.asarray(0.125, bf16)
        zero = jnp.zeros_like(q)
        outs = []
        invs = []
        for head in range(2):
            mine = low if head == 0 else jnp.logical_not(low)
            qh = jnp.where(mine, q, zero)
            own = nt(qh, k_ref[rows, :]) + bias_ref[part]
            largest = jnp.max(own, axis=1, keepdims=True)
            if part == 1:
                before = nt(qh, k_ref[:half, :])
                largest = jnp.maximum(largest, jnp.max(before, axis=1, keepdims=True))
            own = jnp.exp(own - largest)
            total = jnp.sum(own, axis=1, keepdims=True)
            own = own.astype(bf16)
            p_ref[:, (3 * head + 2 * part) * half : (3 * head + 2 * part + 1) * half] = own
            out = nn(own, v_ref[rows, :])
            if part == 1:
                before = jnp.exp(before - largest)
                total = total + jnp.sum(before, axis=1, keepdims=True)
                before = before.astype(bf16)
                p_ref[:, (3 * head + 1) * half : (3 * head + 2) * half] = before
                out = out + nn(before, v_ref[:half, :])
            inv = 1.0 / total
            outs.append(out * inv)
            invs.append(inv)
        o_ref[rows, :] = jnp.where(low, outs[0], outs[1]).astype(bf16)
        inv_ref[rows, :] = jnp.where(low, invs[0], invs[1])


def attend_forward_kernel(span_ref, qkv_ref, o_ref, p_ref, inv_ref, bias_ref):
    half = qkv_ref.shape[0] // 2

    @pl.when(pl.program_id(0) == 0)
    def _():
        for part in range(2):
            bias_ref[part] = half_bias(span_ref[0, part], span_ref[1, part], part, half)

    attend_pair(qkv_ref, o_ref, p_ref.at[0], inv_ref, bias_ref)


def attend_forward(packed, spans):
    length = packed.shape[0]
    width = packed.shape[1] // 3
    pairs = width // PAIR
    half = length // 2
    return pl.pallas_call(
        attend_forward_kernel,
        grid=(pairs,),
        in_specs=[
            pl.BlockSpec(memory_space=pltpu.SMEM),
            pl.BlockSpec((length, 3 * PAIR), lambda j: (0, j)),
        ],
        out_specs=[
            pl.BlockSpec((length, PAIR), lambda j: (0, j)),
            pl.BlockSpec((1, half, 6 * half), lambda j: (j, 0, 0)),
            pl.BlockSpec((length, PAIR), lambda j: (0, j)),
        ],
        out_shape=[
            jax.ShapeDtypeStruct((length, width), bf16),
            jax.ShapeDtypeStruct((pairs, half, 6 * half), bf16),
            jax.ShapeDtypeStruct((length, width), f32),
        ],
        scratch_shapes=[pltpu.VMEM((2, half, half), f32)],
        compiler_params=pltpu.CompilerParams(vmem_limit_bytes=60 << 20),
        cost_estimate=pl.CostEstimate(
            flops=4 * 3 * half * half * width * 4, bytes_accessed=24 << 20, transcendentals=3 * half * half * 12
        ),
        name="attend_forward",
    )(spans, packed)


def attend_back_pair(qkv_ref, o_ref, p_ref, inv_ref, g_ref, sum_ref):
    length = qkv_ref.shape[0]
    half = length // 2
    low = lane_masks(half)
    q_ref, k_ref, v_ref = (qkv_ref.at[:, i * PAIR : (i + 1) * PAIR] for i in range(3))
    dks = [None, None]
    dvs = [None, None]
    dqs = []

    def add(total, part, value):
        total[part] = value if total[part] is None else total[part] + value

    for part in range(2):
        rows = slice(part * half, (part + 1) * half)
        inv = inv_ref[rows, :]
        g = g_ref[rows, :].astype(f32) * inv
        scaled = g * o_ref[rows, :].astype(f32)
        q = q_ref[rows, :]
        gb = g.astype(bf16)
        zero = jnp.zeros_like(gb)
        dq = None
        for head in range(2):
            mine = low if head == 0 else jnp.logical_not(low)
            gh = jnp.where(mine, gb, zero)
            qh = jnp.where(mine, q, zero)
            rowdot = jnp.sum(jnp.where(mine, scaled, 0.0), axis=1, keepdims=True)
            for kpart in range(part + 1):
                krows = slice(kpart * half, (kpart + 1) * half)
                at = (3 * head + part + kpart) * half
                p = p_ref[:, at : at + half]
                kh = jnp.where(mine, k_ref[krows, :], zero)
                dp = nt(gh, v_ref[krows, :])
                ds = (p.astype(f32) * (dp - rowdot)).astype(bf16)
                term = nn(ds, kh)
                dq = term if dq is None else dq + term
                add(dks, kpart, tn(ds, qh))
                add(dvs, kpart, tn(p, gh))
        dqs.append(dq)
    for which, (ref, values, scale) in enumerate(((q_ref, dqs, 0.125), (k_ref, dks, 0.125), (v_ref, dvs, 1.0))):
        total = None
        for part in range(2):
            value = (values[part] * scale).astype(bf16)
            ref[part * half : (part + 1) * half, :] = value
            term = jnp.sum(value.astype(f32), axis=0, keepdims=True)
            total = term if total is None else total + term
        if which != 1:
            sum_ref[which // 2] = total


def attend_backward_kernel(qkv_ref, o_ref, p_ref, inv_ref, g_ref, d_ref, sum_ref):
    d_ref[...] = qkv_ref[...]
    attend_back_pair(d_ref, o_ref, p_ref.at[0], inv_ref, g_ref, sum_ref.at[0])


def attend_backward(packed, attended, p, inv, grad_attended):
    length = packed.shape[0]
    width = packed.shape[1] // 3
    pairs = width // PAIR
    half = length // 2
    one = pl.BlockSpec((length, PAIR), lambda j: (0, j))
    three = pl.BlockSpec((length, 3 * PAIR), lambda j: (0, j))
    return pl.pallas_call(
        attend_backward_kernel,
        grid=(pairs,),
        in_specs=[three, one, pl.BlockSpec((1, half, 6 * half), lambda j: (j, 0, 0)), one, one],
        out_specs=[three, pl.BlockSpec((1, 2, 1, PAIR), lambda j: (j, 0, 0, 0))],
        out_shape=[
            jax.ShapeDtypeStruct(packed.shape, bf16),
            jax.ShapeDtypeStruct((pairs, 2, 1, PAIR), f32),
        ],
        compiler_params=pltpu.CompilerParams(vmem_limit_bytes=56 << 20),
        name="attend_backward",
    )(packed, attended, p, inv, grad_attended)


SWAP = [(0, 1), (1, 0)]


def swap(value):
    return lax.ppermute(value, "col", SWAP)


def ordered(mine, other, axis):
    first = lax.axis_index("col") == 0
    low = jnp.where(first, mine, other)
    high = jnp.where(first, other, mine)
    return jnp.concatenate([low, high], axis=axis)


def own_micro(halves):
    col = lax.axis_index("col")
    mine = lax.dynamic_index_in_dim(halves, col, 0, keepdims=False)
    other = swap(lax.dynamic_index_in_dim(halves, 1 - col, 0, keepdims=False))
    return ordered(mine, other, 1)


def back_micro(full):
    col = lax.axis_index("col")
    half = full.shape[1] // 2
    mine = lax.dynamic_slice_in_dim(full, col * half, half, 1)
    other = swap(lax.dynamic_slice_in_dim(full, (1 - col) * half, half, 1))
    first = col == 0
    return jnp.stack([jnp.where(first, mine, other), jnp.where(first, other, mine)])


G0_ORDERS = ("xzy", "xzy", "xyz")
MIDDLE_ORDERS = ("zxy", "xyz")
REST_ORDERS = ("zxy", "xyz")
MIDDLE_CUT = (11 / 15,)
GATHER_CUT = (9 / 12,)
REDUCE_CUT = (10 / 27, 11 / 27)


MESH = pl.DeviceIdType.MESH
DEPTH = 4
WAYS = ("up", "down", "y", "x", "core")
SIZES = {"z": DEPTH, "y": 2, "x": 2}


def row_of(z, y, core):
    return z * 4 + y * 2 + core


def my_place():
    row = lax.axis_index("row")
    return row // 4, (row // 2) % 2, row % 2, lax.axis_index("col")


def maybe(cond, act):
    if cond is None:
        act()
    else:
        pl.when(cond)(act)


def remote(src, dst, send, recv, device):
    return pltpu.make_async_remote_copy(
        src_ref=src, dst_ref=dst, send_sem=send, recv_sem=recv, device_id=device, device_id_type=MESH
    )


def greet(always, z, up, down):
    barrier = pltpu.get_barrier_semaphore()

    def hello(device):
        pl.semaphore_signal(barrier, inc=1, device_id=device, device_id_type=MESH)

    for device in always:
        hello(device)
    pl.when(z < DEPTH - 1)(lambda: hello(up))
    pl.when(z > 0)(lambda: hello(down))
    pl.semaphore_wait(
        barrier, len(always) + (z < DEPTH - 1).astype(jnp.int32) + (z > 0).astype(jnp.int32)
    )


def tree_rounds(order):
    rounds = {}
    for dz in (0, -1, 1, -2, 2, -3, 3):
        for dy in (0, 1):
            for dx in (0, 1):
                step = {"z": dz, "y": dy, "x": dx}
                via = None
                for axis in order:
                    if step[axis]:
                        via = axis
                onward = []
                open_now = via is None
                for axis in order:
                    if axis == via:
                        open_now = True
                    if not open_now:
                        continue
                    if axis == "z":
                        onward += ["up"] if dz <= 0 else []
                        onward += ["down"] if dz >= 0 else []
                    elif axis != via:
                        onward.append(axis)
                onward.append("core")
                rounds.setdefault(abs(dz) + dy + dx, []).append((dz, dy, dx, onward))
    return rounds


def pieces_of(widths, cuts):
    found = []
    for part in range(len(cuts) - 1):
        base = 0
        for weight, width in enumerate(widths):
            lo = max(base, cuts[part])
            hi = min(base + width, cuts[part + 1])
            if hi > lo:
                found.append((part, weight, lo - cuts[part], lo - base, hi - lo))
            base += width
    return found


class Gatherer:
    def __init__(self, place, shards, widths, cuts, orders, scratch):
        self.z, self.y, self.core, self.x = place
        z, y, core, x = place
        self.shards, self.widths = shards, widths
        self.by_pairs = len(scratch) == 4
        self.whole = scratch[0]
        self.bufs = [scratch[0].at[part] for part in range(3)] if self.by_pairs else scratch[:-3]
        self.parts = range(len(orders))
        self.send, self.recv, self.local = scratch[-3:]
        self.near = {
            "up": (row_of(z + 1, y, core), x),
            "down": (row_of(z - 1, y, core), x),
            "y": (row_of(z, 1 - y, core), x),
            "x": (row_of(z, y, core), 1 - x),
            "core": (row_of(z, y, 1 - core), x),
        }
        self.has = {"up": z < DEPTH - 1, "down": z > 0}
        self.orders = orders
        self.pieces = pieces_of(widths, cuts)
        self.trees = [tree_rounds(order) for order in orders]

    @staticmethod
    def scratch_shapes(cuts, rows, by_pairs):
        dma = pltpu.SemaphoreType.DMA
        if by_pairs:
            bufs = [pltpu.VMEM((3, 2, 16, rows, 3 * PAIR), bf16)]
        else:
            bufs = [pltpu.VMEM((2, 16, rows, cuts[i + 1] - cuts[i]), bf16) for i in range(len(cuts) - 1)]
        return bufs + [
            dma((3, 5)),
            dma((3, 17)),
            dma((3, 6)),
        ]

    def loads(self):
        row = row_of(self.z, self.y, self.core)
        if self.by_pairs:
            return [
                pltpu.make_async_copy(
                    self.shards[0].at[which, :, pl.ds(part * PAIR, PAIR)],
                    self.bufs[part].at[self.x, row, :, pl.ds(which * PAIR, PAIR)],
                    self.local.at[which, part],
                )
                for part in range(3)
                for which in range(3)
            ]
        return [
            pltpu.make_async_copy(
                self.shards[weight].at[:, pl.ds(src, width)],
                self.bufs[part].at[self.x, row, :, pl.ds(at, width)],
                self.local.at[0, i],
            )
            for i, (part, weight, at, src, width) in enumerate(self.pieces)
        ]

    def copy(self, part, bz, by, bx, way):
        block = self.bufs[part].at[bx, row_of(bz, by, self.core)]
        slot = 16 if way == "core" else bx * 8 + bz * 2 + by
        return remote(
            block, block, self.send.at[part, WAYS.index(way)], self.recv.at[part, slot], self.near[way]
        )

    def all_of(self, part, count, way):
        blocks = self.bufs[part].at[0, pl.ds(0, count)]
        return remote(
            blocks, blocks, self.send.at[part, WAYS.index(way)], self.recv.at[part, 16], self.near[way]
        )

    def each(self, step, act, parts=None):
        for part in self.parts if parts is None else parts:
            for dz, dy, dx, onward in self.trees[part].get(step, []):
                bz, by, bx = self.z + dz, (self.y + dy) % 2, (self.x + dx) % 2
                cond = None if dz == 0 else ((bz >= 0) & (bz <= DEPTH - 1))
                maybe(cond, lambda: act(part, bz, by, bx, onward))

    def forward(self, step, parts=None):
        def act(part, bz, by, bx, onward):
            if step:
                self.copy(part, bz, by, bx, "y").wait_recv()
            for way in onward:
                maybe(self.has.get(way), lambda way=way: self.copy(part, bz, by, bx, way).start())

        self.each(step, act, parts)

    def arrive(self, parts=None):
        for part in self.parts if parts is None else parts:
            self.all_of(part, 16, "core").wait_recv()

    def drain(self):
        for part in self.parts:
            count = 1
            for axis in self.orders[part]:
                if axis == "z":
                    for at in range(DEPTH):

                        def act(part=part, at=at, count=count):
                            if at < DEPTH - 1:
                                self.all_of(part, count * (at + 1), "up").wait_send()
                            if at > 0:
                                self.all_of(part, count * (DEPTH - at), "down").wait_send()

                        pl.when(self.z == at)(act)
                else:
                    self.all_of(part, count, axis).wait_send()
                count *= SIZES[axis]
            self.all_of(part, count, "core").wait_send()

    def stores(self, outs):
        return [
            pltpu.make_async_copy(
                self.bufs[part].at[side, :, :, pl.ds(at, width)],
                outs[weight].at[:, :, pl.ds(side * self.widths[weight] + src, width)],
                self.local.at[1 + side, i],
            )
            for i, (part, weight, at, src, width) in enumerate(self.pieces)
            for side in range(2)
        ]

    def weight(self, part, side, at, width):
        block = self.bufs[part][side, :, :, at : at + width]
        return block.reshape(-1, width)


def begin(copies):
    for copy in copies:
        copy.start()


def end(copies):
    for copy in copies:
        copy.wait()


FORWARD_ORDER = (0, 3, 1, 4, 2, 5)
ROWS = 256


def front_kernel(shape, *refs):
    w_qkv, w_out, w_fc, w_proj, x_in, cot, starts, kinds = refs[:8]
    vectors = refs[8:17]
    (
        o_qkv, o_out, o_fc, o_proj, o_x, o_cot, o_vec, o_packed, o_p, o_inv, o_att, o_normed, o_middle, o_second,
        o_active, o_slope,
    ) = refs[17:33]
    scr = refs[33:]
    place = my_place()
    z, y, core, x = place
    one, two, three = (
        Gatherer(place, shards, *shape["groups"][i], scr[shape["at"][i] : shape["at"][i + 1]])
        for i, shards in enumerate(([w_qkv], [w_out, w_fc], [w_proj]))
    )
    (
        xm, xo, cm, xf, n1, pk, big, ib, att, bias, mid, n2, shifts, n1t, s_x, r_x, s_c, r_c, s_v, r_v, s_in, s_pair, s_end,
    ) = scr[shape["at"][3] : -9]
    vec_o = scr[-9:]
    length, half_width = xm.shape
    width = 2 * half_width
    half = length // 2
    blocks = length // ROWS
    to_x = one.near["x"]

    def x_copy(i):
        span = pl.ds(pl.multiple_of(i * ROWS, ROWS), ROWS)
        return remote(x_in.at[1 - x, span], xo.at[span], s_x.at[i], r_x.at[i], to_x)

    own_cols = pl.ds(pl.multiple_of(x * half_width, PAIR), half_width)

    def cot_copy(i):
        span = pl.ds(i * ROWS, ROWS)
        return remote(cot.at[1 - x, span], o_cot.at[span, own_cols], s_c.at[i], r_c.at[i], to_x)

    vec_at = [sum(shape["vectors"][:k]) for k in range(9)]
    vec_copies = [
        remote(vector, vec_o[k], s_v.at[k], r_v.at[k], to_x) for k, vector in enumerate(vectors)
    ]
    own_x = pltpu.make_async_copy(x_in.at[x], xm, s_in.at[0])
    own_cot = pltpu.make_async_copy(cot.at[x], cm, s_in.at[1])
    put_cot = pltpu.make_async_copy(cm, o_cot.at[:, own_cols], s_in.at[2])
    begin(one.loads())
    own_x.start()
    begin(two.loads())
    begin(three.loads())
    own_cot.start()
    greet([to_x, one.near["y"], one.near["core"]], z, one.near["up"], one.near["down"])
    begin(vec_copies)
    end(one.loads())
    one.forward(0)
    begin([x_copy(i) for i in range(blocks)])
    for part in range(2):
        bias[part] = half_bias(starts[x, 0, part], kinds[x, 0, part], part, half)
    one.forward(1, (0,))
    one.forward(1, (1,))
    end(two.loads())
    end(three.loads())
    one.forward(2, (0,))
    one.forward(1, (2,))
    one.forward(2, (1,))
    one.forward(3, (0,))
    end(vec_copies)
    is_low = x == 0
    full = []
    for vector, brought, at, size in zip(vectors, vec_o, vec_at, shape["vectors"]):
        mine, other = vector[...].reshape(1, size), brought[...].reshape(1, size)
        low, high = jnp.where(is_low, mine, other), jnp.where(is_low, other, mine)
        o_vec[:, 2 * at : 2 * at + size] = low
        o_vec[:, 2 * at + size : 2 * at + 2 * size] = high
        full.append(slice(2 * at, 2 * at + 2 * size))
    own_x.wait()

    def norm(value, gain, shift):
        average = jnp.sum(value, axis=1, keepdims=True) / width
        square = jnp.sum(value * value, axis=1, keepdims=True) / width
        inverse = lax.rsqrt(square - average * average + epsilon)
        return ((value - average) * inverse * o_vec[:, full[gain]] + o_vec[:, full[shift]]).astype(bf16)

    def first_norm(i):
        span = pl.ds(pl.multiple_of(i * ROWS, ROWS), ROWS)
        x_copy(i).wait_recv()
        mine, other = xm[span, :], xo[span, :]
        xf[span, :half_width] = jnp.where(is_low, mine, other)
        xf[span, half_width:] = jnp.where(is_low, other, mine)
        n1[span, :] = norm(xf[span, :].astype(f32), 0, 1)

    one.forward(2, (2,))
    one.forward(3, (1,))
    two.forward(0)
    one.forward(4, (0,))
    first_norm(0)
    one.forward(3, (2,))
    one.forward(4, (1,))
    one.forward(5, (0,))
    two.forward(1)
    lax.fori_loop(1, blocks, lambda i, carry: (first_norm(i), carry)[1], 0)
    to_x_out = pltpu.make_async_copy(xf, o_x, s_end.at[0])
    to_normed = pltpu.make_async_copy(n1t, o_normed, s_end.at[1])
    to_x_out.start()

    def pair_puts(j, step):
        wide = pl.ds(pl.multiple_of(3 * PAIR * j, PAIR), 3 * PAIR)
        cols = pl.ds(pl.multiple_of(PAIR * j, PAIR), PAIR)
        return [
            pltpu.make_async_copy(pk.at[j], o_packed.at[:, wide], s_pair.at[0]),
            pltpu.make_async_copy(big.at[step], o_p.at[j], s_pair.at[1]),
            pltpu.make_async_copy(ib.at[j], o_inv.at[:, cols], s_pair.at[2]),
            pltpu.make_async_copy(att.at[j], o_att.at[:, cols], s_pair.at[3]),
        ]

    def serve_0():
        one.forward(5, (1,))
        one.forward(4, (2,))
        two.forward(2)

    def serve_1():
        one.forward(5, (2,))
        two.forward(3)
        one.arrive((1,))
        n1t[...] = n1[...].T
        to_normed.start()

    def serve_2():
        two.forward(4)
        three.forward(0)

    def serve_3():
        two.forward(5)
        three.forward(1)
        one.arrive((2,))
        begin(one.stores([o_qkv]))
        cot_copy(0).start()

    def serve_4():
        three.forward(2)
        cot_copy(1).start()
        own_cot.wait()
        put_cot.start()

    def serve_5():
        three.forward(3)
        cot_copy(2).start()
        cot_copy(3).start()

    serves = (serve_0, serve_1, serve_2, serve_3, serve_4, serve_5)
    for j in range(6):
        for k, vector in ((0, 2), (2, 3)):
            cols = slice(full[vector].start + PAIR * j, full[vector].start + PAIR * (j + 1))
            shifts[j, :, k * PAIR : (k + 1) * PAIR] = o_vec[:, cols]
        shifts[j, :, PAIR : 2 * PAIR] = jnp.zeros((1, PAIR), f32)

    def pair(step, carry):
        part, side = step // 2, step % 2
        j = 3 * side + part
        weight = one.whole[part, side].reshape(width, 3 * PAIR)
        pk[j] = (nn(n1[...], weight) + shifts[j]).astype(bf16)
        attend_pair(pk.at[j], att.at[j], big.at[step], ib.at[j], bias)
        begin(pair_puts(j, step))
        for k, serve in enumerate(serves):
            pl.when(step == k)(serve)
        return carry

    one.arrive((0,))
    lax.fori_loop(0, 6, pair, 0)
    qkv_stores = one.stores([o_qkv])
    two.arrive()
    two_stores = two.stores([o_out, o_fc])
    begin(two_stores)
    out_pieces = [p for p in two.pieces if p[1] == 0]
    fc_pieces = [p for p in two.pieces if p[1] == 1]

    def second(i, carry):
        span = pl.ds(pl.multiple_of(i * ROWS, ROWS), ROWS)
        total = xf[span, :].astype(f32) + o_vec[:, full[4]]
        rows = jnp.concatenate([att[j, span, :] for j in range(6)], axis=1)
        for part, _, at, src, w in out_pieces:
            for side in range(2):
                cols = slice(side * half_width + src, side * half_width + src + w)
                total = total + nt(rows[:, cols], two.weight(part, side, at, w))
        mid[span, :] = total
        n2[span, :] = norm(total, 5, 6)
        return carry

    lax.fori_loop(0, blocks, second, 0)
    for step in range(6):
        end(pair_puts(3 * (step % 2) + step // 2, step))
    to_mid = pltpu.make_async_copy(mid, o_middle, s_end.at[3])
    to_second = pltpu.make_async_copy(n2, o_second, s_end.at[4])
    begin([to_mid, to_second])
    three.forward(4)
    ff_half = two.widths[1]
    puts = []
    for k, (part, _, at, src, w) in enumerate(fc_pieces):

        def block(step, carry):
            side, i = step // blocks, step % blocks
            cols = pl.ds(pl.multiple_of(side * ff_half + src, PAIR), w)
            span = pl.ds(pl.multiple_of(i * ROWS, ROWS), ROWS)
            b_cols = pl.ds(pl.multiple_of(full[7].start + side * ff_half + src, PAIR), w)
            hidden = nn(n2[span, :], two.weight(part, side, at, w)) + o_vec[:, b_cols]
            squared = hidden * hidden
            tanh = jnp.tanh(hidden * (GELU_A + (GELU_A * GELU_B) * squared))
            gate = 0.5 + 0.5 * tanh
            here = pl.ds(pl.multiple_of((i % 2) * ROWS, ROWS), ROWS)
            big[i // 2, here, cols] = (hidden * gate).astype(bf16)
            inner = hidden * (GELU_A + (3.0 * GELU_A * GELU_B) * squared)
            big[2 + i // 2, here, cols] = (gate + inner * (0.5 - 0.5 * tanh * tanh)).astype(bf16)
            return carry

        lax.fori_loop(0, 2 * blocks, block, 0)
        for side in range(2):
            cols = slice(side * ff_half + src, side * ff_half + src + w)
            slot = 5 + 4 * k + 2 * side
            now = [
                pltpu.make_async_copy(big.at[0:2, :, cols], o_active.at[:, :, cols], s_end.at[slot]),
                pltpu.make_async_copy(big.at[2:4, :, cols], o_slope.at[:, :, cols], s_end.at[slot + 1]),
            ]
            begin(now)
            puts += now
        if k == 0:
            three.forward(5)
    three.arrive()
    three_stores = three.stores([o_proj])
    begin(three_stores)
    one.drain()
    two.drain()
    three.drain()
    for i in range(blocks):
        x_copy(i).wait_send()
    for i in range(blocks):
        cot_copy(i).wait()
    end([put_cot, to_x_out, to_normed, to_mid, to_second] + puts)
    end(qkv_stores)
    end(two_stores)
    end(three_stores)


def front_near(shards, x_in, cot, vectors, starts, kinds):
    rows = shards[1].shape[0]
    widths = [3 * shards[0].shape[2]] + [shard.shape[1] for shard in shards[1:]]
    _, length, half_width = x_in.shape
    width = 2 * half_width
    half = length // 2
    pairs = width // PAIR
    groups = [
        (widths[:1], [0, 3 * PAIR, 6 * PAIR, 9 * PAIR], G0_ORDERS),
        (widths[1:3], part_cuts(widths[1:3], *MIDDLE_CUT), MIDDLE_ORDERS),
        (widths[3:], part_cuts(widths[3:], *GATHER_CUT), REST_ORDERS),
    ]
    ff = 2 * widths[2]
    sizes = [v.shape[0] for v in vectors]
    shape = {"groups": groups, "vectors": sizes, "at": [0]}
    dma = pltpu.SemaphoreType.DMA
    scratch = []
    for i, (_, cuts, _) in enumerate(groups):
        scratch += Gatherer.scratch_shapes(cuts, rows, i == 0)
        shape["at"].append(len(scratch))
    scratch += [
        pltpu.VMEM((length, half_width), bf16),
        pltpu.VMEM((length, half_width), bf16),
        pltpu.VMEM((length, half_width), bf16),
        pltpu.VMEM((length, width), bf16),
        pltpu.VMEM((length, width), bf16),
        pltpu.VMEM((pairs, length, 3 * PAIR), bf16),
        pltpu.VMEM((pairs, half, 6 * half), bf16),
        pltpu.VMEM((pairs, length, PAIR), f32),
        pltpu.VMEM((pairs, length, PAIR), bf16),
        pltpu.VMEM((2, half, half), f32),
        pltpu.VMEM((length, width), f32),
        pltpu.VMEM((length, width), bf16),
        pltpu.VMEM((pairs, 1, 3 * PAIR), f32),
        pltpu.VMEM((width, length), bf16),
    ]
    scratch += [dma((4,)), dma((4,)), dma((4,)), dma((4,)), dma((9,)), dma((9,)), dma((3,)), dma((4,)), dma((17,))]
    scratch += [pltpu.VMEM((size,), f32) for size in sizes]
    any_space = pl.BlockSpec(memory_space=pl.ANY)
    vmem = pl.BlockSpec(memory_space=pltpu.VMEM)
    smem = pl.BlockSpec(memory_space=pltpu.SMEM)

    def out(dims, kind=bf16):
        return jax.ShapeDtypeStruct(dims, kind)

    outs = pl.pallas_call(
        lambda *refs: front_kernel(shape, *refs),
        in_specs=[any_space] * 6 + [smem, smem] + [vmem] * 9,
        out_specs=[any_space] * 6 + [vmem] + [any_space] * 9,
        out_shape=[out((16, rows, 2 * w)) for w in widths]
        + [
            out((length, width)),
            out((length, width)),
            out((1, 2 * sum(sizes)), f32),
            out((length, 3 * width)),
            out((pairs, half, 6 * half)),
            out((length, width), f32),
            out((length, width)),
            out((width, length)),
            out((length, width), f32),
            out((length, width)),
            out((2, half, ff)),
            out((2, half, ff)),
        ],
        scratch_shapes=scratch,
        compiler_params=pltpu.CompilerParams(
            collective_id=0, has_side_effects=True, vmem_limit_bytes=67043328
        ),
        cost_estimate=pl.CostEstimate(flops=20 << 30, bytes_accessed=200 << 20, transcendentals=0),
        name="gather_weights",
    )(*shards, x_in, cot, starts, kinds, *vectors)
    full = [w.reshape(16 * rows, -1) for w in outs[:4]]
    vec = outs[6].reshape(-1)
    at = 0
    fulls = []
    for size in sizes:
        fulls.append(vec[at : at + 2 * size])
        at += 2 * size
    saved = list(outs[7:14]) + [out.reshape(length, ff) for out in outs[14:]]
    return full, list(outs[4:6]), fulls, saved


class Reducer:
    def __init__(self, place, grads, widths, cuts, scratch):
        self.z, self.y, self.core, self.x = place
        z, y, core, x = place
        self.grads = grads
        self.widths = widths
        self.acc, self.rcore = scratch[0:3], scratch[3:6]
        rx, ry, self.rz, self.cy, self.cx = scratch[6:8], scratch[8:10], scratch[10:13], scratch[13], scratch[14]
        self.final = scratch[15:18]
        (
            self.s_core, self.r_core, self.s_one, self.r_one, self.s_two, self.r_two, self.s_z, self.r_z, self.s_c,
            self.r_c, self.s_load, self.s_out,
        ) = scratch[18:]
        self.up, self.down = (row_of(z + 1, y, core), x), (row_of(z - 1, y, core), x)
        self.to_y, self.to_x = (row_of(z, 1 - y, core), x), (row_of(z, y, core), 1 - x)
        self.to_core = (row_of(z, y, 1 - core), x)
        self.by_part = [[p for p in pieces_of(widths, cuts) if p[0] == part] for part in range(3)]
        self.first = [(rx[0], self.to_x), (ry[0], self.to_y)]
        self.second = [(ry[1], self.to_y), (rx[1], self.to_x)]

    SCRATCH = 30

    @staticmethod
    def scratch_shapes(widths, cuts, rows):
        w = [cuts[i + 1] - cuts[i] for i in range(3)]
        dma = pltpu.SemaphoreType.DMA

        def low(*shape):
            return pltpu.VMEM(shape, bf16)

        scratch = [low(2, 4, 2, rows, k) for k in w] * 2
        scratch += [low(4, 2, rows, w[0]), low(4, rows, w[1])]
        scratch += [low(4, 2, rows, w[1]), low(4, rows, w[0])]
        scratch += [low(2, 4, rows, w[0]), low(2, 4, rows, w[1]), low(2, 4, 2, 2, rows, w[2])]
        scratch += [low(2, rows, w[2]), low(rows, w[2])]
        scratch += [pltpu.VMEM((rows, k), f32) for k in w]
        scratch += [dma((3,)), dma((3, 2, 4)), dma((2,)), dma((2, 4)), dma((2,)), dma((2, 4))]
        scratch += [dma((3, 2, 4)), dma((3, 2, 4)), dma((2,)), dma((2,)), dma((3,)), dma((3, 3))]
        return scratch

    def cols(self, weight, side, src, width):
        return pl.ds(pl.multiple_of(side * self.widths[weight] + src, 128), width)

    def loop(self, act):
        def step(zi, carry):
            act(zi)
            return carry

        lax.fori_loop(0, DEPTH, step, 0)

    def add(self, total, term):
        total[...] = total[...] + term[...]

    def loads(self, part):
        return [
            pltpu.make_async_copy(
                self.grads[weight].at[:, :, self.core, :, self.cols(weight, side, src, width)],
                self.acc[part].at[side, :, :, :, pl.ds(at, width)],
                self.s_load.at[part],
            )
            for i, (_, weight, at, src, width) in enumerate(self.by_part[part])
            for side in range(2)
        ]

    def view(self, part, ref, far, zi):
        if part == 0:
            return ref.at[(1 - self.x) if far else self.x, zi]
        return ref.at[:, zi, (1 - self.y) if far else self.y]

    def core_copies(self, part, far, zi):
        other = 1 - self.core
        copies = []
        for i, (_, weight, at, src, width) in enumerate(self.by_part[part]):
            cols = pl.ds(at, width)
            if part == 0:
                sides = [(1 - self.x) if far else self.x]
            else:
                sides = [0, 1]
            for k, side in enumerate(sides):
                gcols = self.cols(weight, side, src, width)
                if part == 1:
                    by = (1 - self.y) if far else self.y
                    src_ref = self.grads[weight].at[zi, by, other, :, gcols]
                    dst_ref = self.rcore[1].at[side, zi, by, :, cols]
                else:
                    src_ref = self.grads[weight].at[zi, :, other, :, gcols]
                    dst_ref = self.rcore[part].at[side, zi, :, :, cols]
                copies.append(
                    remote(
                        src_ref, dst_ref, self.s_core.at[part], self.r_core.at[part, int(far), zi], self.to_core
                    )
                )
        return copies

    def core_wait(self, part, far, zi):
        if part == 2:
            blocks = self.rcore[2].at[:, zi]
        else:
            blocks = self.view(part, self.rcore[part], far, zi)
        remote(
            blocks, blocks, self.s_core.at[part], self.r_core.at[part, int(far), zi], self.to_core
        ).wait_recv()

    def start(self, parts):
        for part in parts:
            for load in self.loads(part):
                load.start()

        def begin(far):
            def act(zi):
                for part in parts:
                    if far or part < 2:
                        for copy in self.core_copies(part, far, zi):
                            copy.start()

            self.loop(act)

        begin(True)
        begin(False)

    def first_copy(self, part, zi):
        buf, device = self.first[part]
        return remote(
            self.view(part, self.acc[part], True, zi), buf.at[zi], self.s_one.at[part], self.r_one.at[part, zi], device
        )

    def half_of(self, part, zi, far):
        if part == 0:
            return self.acc[0].at[self.x, zi, (1 - self.y) if far else self.y]
        return self.acc[1].at[(1 - self.x) if far else self.x, zi, self.y]

    def second_copy(self, part, zi):
        buf, device = self.second[part]
        return remote(self.half_of(part, zi, True), buf.at[zi], self.s_two.at[part], self.r_two.at[part, zi], device)

    def far(self, parts):
        for part in parts:
            pltpu.make_async_copy(self.rcore[part], self.acc[part], self.s_load.at[part]).wait()

        def act(zi):
            for part in parts:
                self.core_wait(part, True, zi)
                if part == 2:
                    self.add(self.acc[2].at[:, zi], self.rcore[2].at[:, zi])
                else:
                    self.add(self.view(part, self.acc[part], True, zi), self.view(part, self.rcore[part], True, zi))
                    self.first_copy(part, zi).start()

        self.loop(act)

    def near(self, parts):
        def act(zi):
            for part in parts:
                self.core_wait(part, False, zi)
                mine = self.view(part, self.acc[part], False, zi)
                self.add(mine, self.view(part, self.rcore[part], False, zi))
                self.first_copy(part, zi).wait_recv()
                self.add(mine, self.first[part][0].at[zi])
                self.second_copy(part, zi).start()

        self.loop(act)

    def last(self, parts):
        def act(zi):
            for part in parts:
                self.second_copy(part, zi).wait_recv()
                self.add(self.half_of(part, zi, False), self.second[part][0].at[zi])

        self.loop(act)

    def block(self, part, zi):
        if part == 2:
            return self.acc[2].at[:, zi]
        return self.acc[part].at[self.x, zi, self.y]

    def line_copy(self, part, direction, zd):
        return remote(
            self.block(part, zd),
            self.rz[part].at[direction, zd],
            self.s_z.at[part, direction, zd],
            self.r_z.at[part, direction, zd],
            self.down if direction else self.up,
        )

    def line(self, parts, step):
        for direction in range(2):
            at = DEPTH - 1 - step if direction else step
            for zd in (0, 1, 2) if direction else (3, 2, 1):
                if not ((at > zd) if direction else (at < zd)):
                    continue
                for part in parts:

                    def act(part=part, direction=direction, zd=zd):
                        if step > 0:
                            self.line_copy(part, direction, zd).wait_recv()
                            self.add(self.block(part, zd), self.rz[part].at[direction, zd])
                        self.line_copy(part, direction, zd).start()

                    pl.when(self.z == at)(act)

    def line_end(self, parts):
        for part in parts:
            for direction in range(2):

                def act(part=part, direction=direction):
                    self.line_copy(part, direction, self.z).wait_recv()
                    self.add(self.block(part, self.z), self.rz[part].at[direction, self.z])

                pl.when((self.z < DEPTH - 1) if direction else (self.z > 0))(act)

    def y_copy(self):
        return remote(self.acc[2].at[:, self.z, 1 - self.y], self.cy, self.s_c.at[0], self.r_c.at[0], self.to_y)

    def x_copy(self):
        return remote(self.acc[2].at[1 - self.x, self.z, self.y], self.cx, self.s_c.at[1], self.r_c.at[1], self.to_x)

    def turn(self):
        self.y_copy().wait_recv()
        self.add(self.acc[2].at[:, self.z, self.y], self.cy)
        self.x_copy().start()

    def turn_end(self):
        self.x_copy().wait_recv()
        self.add(self.acc[2].at[self.x, self.z, self.y], self.cx)

    def stores(self, outs):
        if len(outs[0].shape) == 3:
            return [
                pltpu.make_async_copy(
                    self.final[part].at[:, pl.ds(which * PAIR, PAIR)],
                    outs[0].at[which, :, pl.ds(part * PAIR, PAIR)],
                    self.s_out.at[part, which],
                )
                for part in range(3)
                for which in range(3)
            ]
        return [
            pltpu.make_async_copy(
                self.final[part].at[:, pl.ds(at, width)], outs[weight].at[:, pl.ds(src, width)], self.s_out.at[part, i]
            )
            for part in range(3)
            for i, (_, weight, at, src, width) in enumerate(self.by_part[part])
        ]

    def finish(self, outs):
        for part in range(3):
            self.final[part][...] = self.acc[part][self.x, self.z, self.y].astype(f32)
        for store in self.stores(outs):
            store.start()

    def drain(self, outs):
        for part in range(3):
            remote(
                self.acc[part], self.rcore[part], self.s_core.at[part], self.r_core.at[part, 0, 0], self.to_core
            ).wait_send()
            for direction in range(2):
                for zd in range(DEPTH):
                    pl.when((self.z > zd) if direction else (self.z < zd))(
                        lambda part=part, direction=direction, zd=zd: self.line_copy(part, direction, zd).wait_send()
                    )
            if part < 2:
                for (buf, device), send, recv in (
                    (self.first[part], self.s_one, self.r_one),
                    (self.second[part], self.s_two, self.r_two),
                ):
                    remote(buf, buf, send.at[part], recv.at[part, 0], device).wait_send()
        self.y_copy().wait_send()
        self.x_copy().wait_send()
        for store in self.stores(outs):
            store.wait()


def back_kernel(shape, *refs):
    (
        g_out, g_fc, g_proj, packed, attended, p_all, inv_all, gatt, normed_t, w_qkv, x_all, middle, gain_ref, small_in,
        o_qkv, o_out, o_fc, o_proj, o_sum, o_input,
    ) = refs[:20]
    scr = refs[20:]
    first = Reducer.SCRATCH
    place = my_place()
    z, y, core, x = place
    early = Reducer(place, [g_out, g_fc, g_proj], shape["early"], shape["early_cuts"], scr[:first])
    qkv, o_buf, p_buf, inv_buf, g_buf, nt_buf, w_buf, x_buf, m_buf, gqkv, gi, col_sum, srecv, sacc, sums = scr[2 * first : 2 * first + 15]
    s_all, s_pair, s_mid, s_gi, r_gi, l_gi, s_s, r_s = scr[2 * first + 15 :]
    late = Reducer(place, [gqkv], shape["late"], shape["late_cuts"], scr[first : 2 * first])
    whole = [
        pltpu.make_async_copy(packed, qkv, s_all.at[0]),
        pltpu.make_async_copy(normed_t, nt_buf, s_all.at[1]),
        pltpu.make_async_copy(w_qkv, w_buf, s_all.at[2]),
        pltpu.make_async_copy(x_all, x_buf, s_all.at[3]),
    ]

    def pair_loads(step):
        j = (step // 2 + 2) % 3 + 3 * (step % 2)
        slot = step % 2
        cols = pl.ds(pl.multiple_of(j * PAIR, PAIR), PAIR)
        return [
            pltpu.make_async_copy(p_all.at[j], p_buf.at[slot], s_pair.at[slot, 0]),
            pltpu.make_async_copy(attended.at[:, cols], o_buf.at[slot], s_pair.at[slot, 1]),
            pltpu.make_async_copy(inv_all.at[:, cols], inv_buf.at[slot], s_pair.at[slot, 2]),
            pltpu.make_async_copy(gatt.at[:, cols], g_buf.at[slot], s_pair.at[slot, 3]),
        ]

    begin(whole[:1])
    begin(pair_loads(0))
    begin(whole[1:])
    to_z1 = (row_of(z + 1 - 2 * (z % 2), y, core), x)
    to_z2 = (row_of((z + 2) % 4, y, core), x)
    greet([early.to_core, early.to_x, early.to_y, to_z2], z, early.up, early.down)
    early.start((0, 1, 2))
    end(whole[:1])

    def pair(step, carry):
        j = (step // 2 + 2) % 3 + 3 * (step % 2)
        slot = step % 2
        pl.when(step < 5)(lambda: begin(pair_loads(step + 1)))
        end(pair_loads(step))
        cols = pl.ds(pl.multiple_of(3 * PAIR * j, PAIR), 3 * PAIR)
        attend_back_pair(qkv.at[:, cols], o_buf.at[slot], p_buf.at[slot], inv_buf.at[slot], g_buf.at[slot], col_sum.at[j])
        pl.when(step == 0)(lambda: end(whole[1:2]))
        grad = nn(nt_buf[...], qkv[:, cols]).astype(bf16)
        gqkv[:, :, :, :, cols] = grad.reshape(gqkv.shape[:4] + (3 * PAIR,))
        for k, serve in enumerate(serves):
            pl.when(step == k)(serve)
        return carry

    rows = m_buf.shape[1]
    blocks = x_buf.shape[0] // rows

    def mid_load(i):
        return pltpu.make_async_copy(middle.at[pl.ds(pl.multiple_of(i * rows, rows), rows)], m_buf.at[i % 2], s_mid.at[i % 2])

    def input_copies(i):
        span = pl.ds(pl.multiple_of(i * rows, rows), rows)
        return (
            pltpu.make_async_copy(gi.at[0, span], o_input.at[x, span], l_gi.at[i]),
            remote(gi.at[1, span], o_input.at[x, span], s_gi.at[i], r_gi.at[i], early.to_x),
        )

    def input_block(i):
        span = pl.ds(pl.multiple_of(i * rows, rows), rows)
        grad = nt(qkv[span, :], w_buf[...])
        pl.when(i + 1 < blocks)(lambda: mid_load(i + 1).start())
        mid_load(i).wait()
        value = x_buf[span, :].astype(f32)
        width = value.shape[1]
        average = jnp.sum(value, axis=1, keepdims=True) / width
        square = jnp.sum(value * value, axis=1, keepdims=True) / width
        inverse = lax.rsqrt(square - average * average + epsilon)
        centred = (value - average) * inverse
        scaled = grad * gain_ref[...]
        one = jnp.sum(scaled, axis=1, keepdims=True) / width
        two = jnp.sum(scaled * centred, axis=1, keepdims=True) / width
        out = m_buf[i % 2] + inverse * (scaled - one - centred * two)
        for k, term in enumerate((grad * centred, grad)):
            sums[k] = sums[k] + jnp.sum(term, axis=0, keepdims=True)
        half = width // 2
        is_low = x == 0
        gi[0, span, :] = jnp.where(is_low, out[:, :half], out[:, half:]).astype(bf16)
        gi[1, span, :] = jnp.where(is_low, out[:, half:], out[:, :half]).astype(bf16)
        for copy in input_copies(i):
            copy.start()

    partners = [early.to_core, early.to_x, early.to_y, to_z1, to_z2]

    def small_copy(step):
        return remote(sacc.at[step], srecv.at[step], s_s.at[step], r_s.at[step], partners[step])

    def small_start():
        sacc[0] = small_in[...]
        at = 0
        for k in range(2):
            for i in range(6):
                sacc[0, at : at + 1, :] = sums[k][:, i * PAIR : (i + 1) * PAIR]
                at += 1
        for k in range(2):
            for i in range(6):
                sacc[0, at : at + 1, :] = col_sum[i, k]
                at += 1
        small_copy(0).start()

    def small_next(step):
        small_copy(step).wait()
        sacc[step + 1] = sacc[step] + srecv[step]
        if step < 4:
            small_copy(step + 1).start()

    both = (0, 1)

    def serve_0():
        early.far((0, 1, 2))
        early.line((2,), 0)

    def serve_1():
        late.start((2,))

    def serve_2():
        early.line((2,), 1)

    def serve_3():
        late.start((0,))
        late.far((2,))
        early.line((2,), 2)
        late.line((2,), 0)
        mid_load(0).start()

    def serve_4():
        early.near(both)
        late.far((0,))

    def serve_5():
        late.start((1,))
        early.line_end((2,))
        early.y_copy().start()
        late.line((2,), 1)
        end(whole[2:])

    serves = (serve_0, serve_1, serve_2, serve_3, serve_4, serve_5)
    lax.fori_loop(0, 6, pair, 0)

    def block_0():
        early.last(both)
        early.line(both, 0)
        late.far((1,))
        late.line((2,), 2)

    def block_1():
        early.turn()
        early.line(both, 1)
        late.near((0,))
        late.line_end((2,))
        late.y_copy().start()

    def block_2():
        early.turn_end()
        early.line(both, 2)
        late.near((1,))
        late.turn()

    after = (block_0, block_1, block_2)
    sums[...] = jnp.zeros(sums.shape, f32)

    def input_step(i, carry):
        input_block(i)
        for k, serve in enumerate(after):
            pl.when(i == k)(serve)
        return carry

    lax.fori_loop(0, blocks, input_step, 0)
    small_start()
    late.last((0,))
    late.line((0,), 0)
    early.line_end(both)
    early.finish([o_out, o_fc, o_proj])
    small_next(0)
    late.last((1,))
    late.line((1,), 0)
    late.turn_end()
    late.line(both, 1)
    small_next(1)
    late.line(both, 2)
    small_next(2)
    late.line_end(both)
    late.finish([o_qkv])
    small_next(3)
    small_next(4)
    o_sum[...] = sacc[5]
    for i in range(blocks):
        local, other = input_copies(i)
        local.wait()
        other.wait()
    early.drain([o_out, o_fc, o_proj])
    late.drain([o_qkv])


def back_near(grads, packed, attended, p, inv, gatt, normed_t, w_qkv, x, middle, gain, small, rows):
    length, width = x.shape
    wide = packed.shape[1]
    early = [grad.shape[1] // 2 for grad in grads]
    shape = {"early": early, "early_cuts": part_cuts(early, *REDUCE_CUT), "late": [wide // 2]}
    shape["late_cuts"] = [0, wide // 6, wide // 3, wide // 2]
    dma = pltpu.SemaphoreType.DMA
    half = length // 2
    blocks = 4
    scratch = Reducer.scratch_shapes(early, shape["early_cuts"], rows)
    scratch += Reducer.scratch_shapes(shape["late"], shape["late_cuts"], rows)
    scratch += [
        pltpu.VMEM((length, wide), bf16),
        pltpu.VMEM((2, length, PAIR), bf16),
        pltpu.VMEM((2, half, 6 * half), bf16),
        pltpu.VMEM((2, length, PAIR), f32),
        pltpu.VMEM((2, length, PAIR), bf16),
        pltpu.VMEM((width, length), bf16),
        pltpu.VMEM((width, wide), bf16),
        pltpu.VMEM((length, width), bf16),
        pltpu.VMEM((2, length // blocks, width), f32),
        pltpu.VMEM((4, 2, 2, rows, wide), bf16),
        pltpu.VMEM((2, length, width // 2), bf16),
        pltpu.VMEM((width // PAIR, 2, 1, PAIR), f32),
        pltpu.VMEM((5,) + small.shape, f32),
        pltpu.VMEM((6,) + small.shape, f32),
        pltpu.VMEM((2, 1, width), f32),
    ]
    scratch += [dma((4,)), dma((2, 4)), dma((2,)), dma((4,)), dma((4,)), dma((4,)), dma((5,)), dma((5,))]
    shaped = [grad.reshape(4, 2, 2, rows, grad.shape[1]) for grad in grads]
    any_space = pl.BlockSpec(memory_space=pl.ANY)
    vmem = pl.BlockSpec(memory_space=pltpu.VMEM)
    outs = pl.pallas_call(
        lambda *refs: back_kernel(shape, *refs),
        in_specs=[any_space] * 12 + [vmem, vmem],
        out_specs=[any_space] * 4 + [vmem, any_space],
        out_shape=[jax.ShapeDtypeStruct((3, rows, wide // 6), f32)]
        + [jax.ShapeDtypeStruct((rows, w), f32) for w in early]
        + [jax.ShapeDtypeStruct(small.shape, f32), jax.ShapeDtypeStruct((2, length, width // 2), bf16)],
        scratch_shapes=scratch,
        compiler_params=pltpu.CompilerParams(
            collective_id=1, has_side_effects=True, vmem_limit_bytes=67043328
        ),
        cost_estimate=pl.CostEstimate(flops=30 << 30, bytes_accessed=200 << 20, transcendentals=0),
        name="reduce_grads",
    )(*shaped, packed, attended, p, inv, gatt, normed_t, w_qkv, x, middle, gain.reshape(1, -1), small)
    return outs


def gather_far(shards):
    fulls = []
    for shard in shards:
        rows = lax.all_gather(shard, ("col", "row"), axis=0, tiled=True)
        fulls.append(jnp.concatenate(jnp.split(rows, 2, axis=0), axis=1))
    return fulls


def reduce_far(grads, small):
    outs = []
    for grad in grads:
        halves = jnp.concatenate(jnp.split(grad, 2, axis=1), axis=0)
        outs.append(lax.psum_scatter(halves, ("col", "row"), scatter_dimension=0, tiled=True).astype(f32))
    return outs, lax.psum(small, ("row", "col"))


def part_cuts(widths, *shares):
    total = sum(widths) // 128
    ends = [round(total * sum(shares[: k + 1])) for k in range(len(shares))]
    return [0] + [128 * end for end in ends] + [128 * total]


def layer_norm(value):
    width = value.shape[-1]
    average = jnp.sum(value, axis=-1, keepdims=True) / width
    square = jnp.sum(value * value, axis=-1, keepdims=True) / width
    inverse = lax.rsqrt(square - average * average + epsilon)
    return (value - average) * inverse, inverse


def norm_backward(grad, centred, inverse, gain):
    scaled = grad * gain
    first = jnp.mean(scaled, axis=-1, keepdims=True)
    second = jnp.mean(scaled * centred, axis=-1, keepdims=True)
    back = inverse * (scaled - first - centred * second)
    return back, jnp.sum(grad * centred, axis=0), jnp.sum(grad, axis=0)


def by_pairs(block):
    rows, three, half = block.shape
    return block.reshape(rows, three, half // PAIR, PAIR).transpose(0, 2, 1, 3).reshape(rows, three * half)


def body(
    near, x_in, span_start, span_kind, ln1_gain, ln1_bias, w_qkv, b_query, b_value, w_out, b_out,
    ln2_gain, ln2_bias, w_fc, b_fc, w_proj, b_proj, cotangent,
):
    half_width = x_in.shape[2]
    shard = w_qkv.shape[0]
    col = lax.axis_index("col")

    vectors = [ln1_gain, ln1_bias, b_query, b_value, b_out, ln2_gain, ln2_bias, b_fc, b_proj]
    shards = [w_out.T, w_fc, w_proj.T]
    width = 2 * half_width
    if near:
        weights, (x_own, grad_out), vectors, saved = front_near(
            [w_qkv.transpose(1, 0, 2)] + shards, x_in, cotangent, vectors, span_start, span_kind
        )
        qkv_all, out_all, fc_all, proj_all = weights
        ln1_gain, _, _, _, _, ln2_gain, _, _, b_proj = vectors
        packed, p, inv, attended, normed_turned, middle, normed_second, active, slope = saved
        centred_second, inverse_second = layer_norm(middle)
    else:
        x_own = own_micro(x_in)
        residual = x_own.astype(f32)
        grad_out = own_micro(cotangent)
        qkv_all, out_all, fc_all, proj_all = gather_far([by_pairs(w_qkv)] + shards)
        flat = jnp.concatenate(vectors)
        flat_other = swap(flat)
        full = []
        at = 0
        for vector in vectors:
            full.append(ordered(vector, flat_other[at : at + vector.shape[0]], 0))
            at += vector.shape[0]
        ln1_gain, ln1_bias, b_query, b_value, b_out, ln2_gain, ln2_bias, b_fc, b_proj = full
        starts = lax.dynamic_index_in_dim(span_start, col, 0, keepdims=False)[0]
        kinds = lax.dynamic_index_in_dim(span_kind, col, 0, keepdims=False)[0]
        spans = jnp.stack([starts, kinds])
        centred_first, inverse_first = layer_norm(residual)
        normed_first = (centred_first * ln1_gain + ln1_bias).astype(bf16)
        bias = jnp.stack([b_query, jnp.zeros_like(b_query), b_value]).reshape(3, -1, PAIR)
        packed = (nn(normed_first, qkv_all) + bias.transpose(1, 0, 2).reshape(-1)).astype(bf16)
        attended, p, inv = attend_forward(packed, spans)
        middle = residual + nt(attended, out_all) + b_out
        centred_second, inverse_second = layer_norm(middle)
        normed_second = (centred_second * ln2_gain + ln2_bias).astype(bf16)
        hidden = nn(normed_second, fc_all) + b_fc
        squared = hidden * hidden
        tanh = jnp.tanh(GELU_A * hidden * (1.0 + GELU_B * squared))
        active = (0.5 * hidden * (1.0 + tanh)).astype(bf16)
        slope = (
            0.5 * (1.0 + tanh)
            + 0.5 * hidden * (1.0 - tanh * tanh) * GELU_A * (1.0 + 3.0 * GELU_B * squared)
        ).astype(bf16)
    layer_out = back_micro((middle + nt(active, proj_all) + b_proj).astype(bf16))

    grad_out_wide = grad_out.astype(f32)
    g_proj = tn(grad_out, active).astype(bf16)
    grad_hidden = (nn(grad_out, proj_all) * slope.astype(f32)).astype(bf16)
    g_fc = tn(normed_second, grad_hidden).astype(bf16)
    g_bfc = jnp.sum(grad_hidden.astype(f32), axis=0)
    grad_normed = nt(grad_hidden, fc_all)
    back, g_ln2_gain, g_ln2_bias = norm_backward(grad_normed, centred_second, inverse_second, ln2_gain)
    grad_middle = grad_out_wide + back
    g_bproj = jnp.sum(grad_out_wide, axis=0)
    g_bout = jnp.sum(grad_middle, axis=0)
    grad_low = grad_middle.astype(bf16)
    g_out = tn(grad_low, attended).astype(bf16)
    grad_attended = nn(grad_low, out_all).astype(bf16)
    zeros = jnp.zeros((width,), f32)
    small = [zeros, zeros, zeros, zeros, g_bout, g_ln2_gain, g_ln2_bias, g_bfc, g_bproj]
    if near:
        flat = jnp.concatenate(small).reshape(-1, 128)
        *outs, summed, grad_input = back_near(
            [g_out, g_fc, g_proj], packed, attended, p, inv, grad_attended, normed_turned, qkv_all,
            x_own, grad_middle, ln1_gain, flat, shard,
        )
        outs[0] = outs[0].transpose(1, 0, 2)
    else:
        grad_packed, sums = attend_backward(packed, attended, p, inv, grad_attended)
        g_qkv = tn(normed_first, grad_packed).astype(bf16)
        grad_normed = nt(grad_packed, qkv_all)
        back, g_ln1_gain, g_ln1_bias = norm_backward(grad_normed, centred_first, inverse_first, ln1_gain)
        grad_input = back_micro((grad_middle + back).astype(bf16))
        small[:4] = [g_ln1_gain, g_ln1_bias, sums[:, 0, 0].reshape(-1), sums[:, 1, 0].reshape(-1)]
        outs, summed = reduce_far([g_qkv, g_out, g_fc, g_proj], jnp.concatenate(small))
        outs[0] = outs[0].reshape(shard, -1, 3, PAIR).transpose(0, 2, 1, 3).reshape(shard, 3, half_width)
    out_qkv, out_out, out_fc, out_proj = outs
    summed = summed.reshape(-1)
    kept = []
    at = 0
    for vector in small:
        size = vector.shape[0] // 2
        kept.append(lax.dynamic_slice_in_dim(summed, at + col * size, size, 0))
        at += vector.shape[0]
    return (
        layer_out,
        grad_input,
        kept[0],
        kept[1],
        out_qkv,
        kept[2],
        kept[3],
        out_out.T,
        kept[4],
        kept[5],
        kept[6],
        out_fc,
        kept[7],
        out_proj.T,
        kept[8],
    )


def solution(mesh):
    placed = (
        P(None, "row", "col"), P(None, "row", None), P(None, "row", None), P("col"), P("col"),
        P("row", None, "col"), P("col"), P("col"), P("col", "row"), P("col"), P("col"), P("col"),
        P("row", "col"), P("col"), P("col", "row"), P("col"), P(None, "row", "col"),
    )
    near = mesh.shape["row"] == 16
    return jax.shard_map(
        partial(body, near),
        mesh=mesh,
        in_specs=placed,
        out_specs=(
            P(None, "row", "col"), P(None, "row", "col"), P("col"), P("col"), P("row", None, "col"),
            P("col"), P("col"), P("col", "row"), P("col"), P("col"), P("col"), P("row", "col"),
            P("col"), P("col", "row"), P("col"),
        ),
        check_vma=False,
    )
```
